32 devices in a mesh: dp: 8 (over z, x), outer: 4 (over y, core).
Axes of the slice: x: 2, y: 2, z: 4, core: 2. Of those that a mesh axis runs over, the one named last changes fastest.
Arguments:
- text_rows: bfloat16 [32, 512, 768], P(('dp', 'outer')), may hold values from -6 to 6
- text_segments: int32 [32, 512], P(('dp', 'outer')), may hold values from 0 to 3, never falling along the last dimension, each value on 1 to 256 neighbouring positions
- positives: int32 [64], replicated, may hold values from 0 to 63
- w_mix: bfloat16 [768, 4608], P('dp'), may hold values from -0.21875 to 0.21875
- w_proj: bfloat16 [768, 1536], P('dp'), may hold values from -0.875 to 0.875
- w_up: bfloat16 [768, 6144], P('dp'), may hold values from -0.21875 to 0.21875
- w_down: bfloat16 [3072, 1536], P('dp'), may hold values from -0.109375 to 0.109375
- b_up: bfloat16 [3072, 2], P('dp'), may hold values from -1 to 1
- b_rows: bfloat16 [768, 12], P('dp'), may hold values from -1 to 1
- g_rows: bfloat16 [768, 4], P('dp'), may hold values from 0.5 to 1.5
Outputs:
- encoded: bfloat16 [32, 512, 768], P(('dp', 'outer'))
- row_grads: float32 [32, 512, 768], P(('dp', 'outer'))
- grad_mix: float32 [768, 4608], P('dp')
- grad_proj: float32 [768, 1536], P('dp')
- grad_up: float32 [768, 6144], P('dp')
- grad_down: float32 [3072, 1536], P('dp')
- grad_up_bias: float32 [3072, 2], P('dp')
- grad_biases: float32 [768, 12], P('dp')
- grad_gains: float32 [768, 4], P('dp')
The draws below stay inside these ranges and needn't reach their ends.
Inputs may be any that keep to these rules, and one draw needn't show every extreme that they name: `text_segments`: within each row segment numbers never fall, every number 0 to 3 occurs, and no segment has more than 256 tokens.
All inputs are finite; a program needn't handle non-finite values.
Results may differ from the reference program's by a relative error of at most 0.023.
Values may be sent and summed in bfloat16 or wider, within the bound.
A program may use at most 256 MiB of HBM per device.

```python
import math
import jax
import jax.numpy as jnp
import numpy as np
from jax import lax

D = 768
HEADS = 12
HEAD_DIM = 64
FF = 3072
ROW_LEN = 512
SEGS = 4
ROWS = 32
TEXTS = 64


def with_ends(result, key, low, largest):
    longest = result.shape.index(max(result.shape))
    spots = []
    for shift in (0, 1):
        where = [jax.random.randint(jax.random.fold_in(key, axis), (), 0, length) for axis, length in enumerate(result.shape)]
        where[longest] = (where[longest] + shift) % result.shape[longest]
        spots.append(tuple(where))
    return result.at[spots[0]].set(low).at[spots[1]].set(largest)


def steps_of(rng, extent, shards, smallest, top_value):
    loudness = 1.0
    for axis_at, parts in shards:
        draws = jax.random.uniform(jax.random.fold_in(jax.random.fold_in(rng, 6), axis_at), (parts,), jnp.float32, smallest / len(shards), top_value / len(shards))
        loudness = loudness * jnp.repeat(jnp.exp(draws), extent[axis_at] // parts).reshape((-1,) + (1,) * (len(extent) - 1 - axis_at))
    return loudness


def profile(number_of, total, bound, skew):
    portions = [(1 << 20) // math.isqrt(standing ** skew) + 1 for standing in range(2, number_of + 1)]
    rest, holding = total - bound - (number_of - 1), [1] * (number_of - 1)
    while rest > 0:
        free = [i for i in range(number_of - 1) if holding[i] < bound]
        pool, remaining = sum([portions[i] for i in free]), rest
        for i in free:
            extra = min(bound - holding[i], max(1, remaining * portions[i] // pool), rest)
            holding[i] = holding[i] + extra
            rest = rest - extra
    return np.array([bound] + holding)


def uneven(stream_key, count, total, reach, lean):
    if count == 2:
        one = jax.random.randint(stream_key, (), max(1, total - reach), min(reach, total - 1) + 1)
        return jnp.stack([one, total - one])
    sizes = jnp.asarray(profile(count, total, reach, lean), jnp.int32)
    twos = (count - 1) // 2
    source_of, taker = sizes[1:1 + 2 * twos:2], sizes[2:2 + 2 * twos:2]
    slack = jnp.minimum(source_of - 1, reach - taker)
    shifted = jax.random.randint(jax.random.fold_in(stream_key, 1), (twos,), 0, 1 << 20) % (slack + 1)
    sizes = sizes.at[1:1 + 2 * twos:2].set(source_of - shifted).at[2:2 + 2 * twos:2].set(taker + shifted)
    return sizes[jax.random.permutation(jax.random.fold_in(stream_key, 2), count)]


def gaussian(key, shape, width, limit, pieces=(), held_as=jnp.bfloat16):
    factor_of = steps_of(key, shape, pieces, -0.22, 0.18) if pieces else 1.0
    entries = jax.random.normal(key, shape, jnp.float32) * width * factor_of
    return jnp.minimum(jnp.maximum(entries, -limit), limit).astype(held_as)


def setup_inputs(seed: int = 0) -> dict:
    key_of = jax.random.split(jax.random.key(seed), 11)
    text_rows = gaussian(key_of[0], (ROWS, ROW_LEN, D), 1.0, 6.0, ((0, 32),))
    text_segments = jax.vmap(lambda own: jnp.searchsorted(jnp.cumsum(uneven(own, SEGS, ROW_LEN, ROW_LEN // 2, 2)), jnp.arange(ROW_LEN), side="right"))(jax.random.split(key_of[1], ROWS)).reshape((ROWS, ROW_LEN)).astype(jnp.int32)
    positives = with_ends(jax.random.randint(key_of[2], (TEXTS,), 0, TEXTS), jax.random.fold_in(key_of[2], 1), 0, TEXTS - 1).astype(jnp.int32)
    w_mix = gaussian(key_of[3], (D, 6 * D), D ** -0.5, 0.21875, ((0, 8),))
    w_proj = gaussian(key_of[4], (D, 2 * D), (D // 16) ** -0.5, 0.875, ((0, 8),))
    w_up = gaussian(key_of[5], (D, 2 * FF), D ** -0.5, 0.21875, ((0, 8),))
    w_down = gaussian(key_of[6], (FF, 2 * D), FF ** -0.5, 0.109375, ((0, 8),))
    b_up = gaussian(key_of[7], (FF, 2), 0.2, 1.0, ((0, 8),))
    b_rows = gaussian(key_of[8], (D, 12), 0.2, 1.0, ((0, 8),))
    g_rows = jnp.clip(1.0 + 0.1 * jax.random.normal(key_of[9], (D, 4), jnp.float32), 0.5, 1.5).astype(jnp.bfloat16)
    return dict(text_rows=text_rows, text_segments=text_segments, positives=positives, w_mix=w_mix, w_proj=w_proj, w_up=w_up, w_down=w_down, b_up=b_up, b_rows=b_rows, g_rows=g_rows)


@jax.custom_vjp
def low(v):
    return lax.optimization_barrier(v.astype(jnp.bfloat16)).astype(jnp.float32)

@jax.custom_vjp
def low_back(v):
    return v

def low_keep(v):
    return (low(v), None)

def low_pass(kept, grad):
    return (grad,)

def back_keep(v):
    return (v, None)

def back_low(kept, grad):
    return (low(grad),)
low.defvjp(low_keep, low_pass)
low_back.defvjp(back_keep, back_low)
highest = lax.Precision.HIGHEST
masked_score = -1e+30
layer_eps = 1e-05

def both_ways(inputs):
    return low(low_back(inputs))

def norm_rows(inputs, gain_row, offset):
    center = inputs - lax.optimization_barrier(jnp.mean(inputs, axis=-1, keepdims=True))
    spread = lax.optimization_barrier(jnp.mean(center * center, axis=-1, keepdims=True))
    return center * lax.rsqrt(spread + layer_eps) * gain_row + offset

def split_tower(weights_all, tower_index):
    w_mix, w_proj, w_up, w_down, b_up, b_rows, g_rows = weights_all
    return (w_mix[:, 3 * tower_index * D:3 * (tower_index + 1) * D], w_proj[:, tower_index * D:(tower_index + 1) * D], w_up[:, tower_index * FF:(tower_index + 1) * FF], w_down[:, tower_index * D:(tower_index + 1) * D], b_up[:, tower_index], b_rows[:, 6 * tower_index:6 * tower_index + 6].T, g_rows[:, 2 * tower_index:2 * tower_index + 2].T)

def encode_row(rows_in, segments, weights_one):
    w_mix, w_proj, w_up, w_down, b_up, b_rows, g_rows = weights_one
    mixed_rows = jnp.dot(rows_in, w_mix, precision=highest)
    mixed_rows = both_ways(mixed_rows + jnp.concatenate([b_rows[0], jnp.zeros_like(b_rows[0]), b_rows[1]]))
    queries = mixed_rows[:, :D].reshape(ROW_LEN, HEADS, HEAD_DIM)
    key_rows = mixed_rows[:, D:2 * D].reshape(ROW_LEN, HEADS, HEAD_DIM)
    values = mixed_rows[:, 2 * D:].reshape(ROW_LEN, HEADS, HEAD_DIM)
    allowed = segments[:, None] == segments[None, :]
    scores = jnp.einsum('qhe,khe->hqk', queries, key_rows, precision=highest) * HEAD_DIM ** (-0.5)
    scores = low_back(jnp.where(allowed[None], scores, masked_score))
    top_score = lax.optimization_barrier(jnp.max(scores, axis=-1, keepdims=True))
    raised = jnp.exp(scores - top_score)
    chances = low(raised / lax.optimization_barrier(jnp.sum(raised, axis=-1, keepdims=True)))
    attended = both_ways(jnp.einsum('hqk,khe->qhe', chances, values, precision=highest).reshape(ROW_LEN, D))
    projected = low_back(jnp.dot(attended, w_proj, precision=highest) + b_rows[2])
    normed_one = norm_rows(rows_in + projected, g_rows[0], b_rows[3])
    up_pre = low_back(jnp.dot(low(normed_one), w_up, precision=highest) + b_up)
    gelu_low = low(jax.nn.gelu(up_pre, approximate=False))
    lowered = low_back(jnp.dot(gelu_low, w_down, precision=highest) + b_rows[4])
    return norm_rows(normed_one + lowered, g_rows[1], b_rows[5])

def encode_tower(rows_in, segments, weights_one, count):
    group_rows = 8 if count % 8 == 0 else 1
    shaped = (rows_in.reshape(count // group_rows, group_rows, ROW_LEN, D), segments.reshape(count // group_rows, group_rows, ROW_LEN))

    def group_step(group_pair):
        return jax.vmap(lambda one_row, one_seg: encode_row(one_row, one_seg, weights_one))(group_pair[0], group_pair[1])
    return lax.map(jax.checkpoint(group_step), shaped).reshape(count, ROW_LEN, D)

def cls_vectors(encoded, segments, count):
    levels = jnp.arange(SEGS, dtype=jnp.int32)
    starts = lax.optimization_barrier(jnp.sum((segments[:, None, :] < levels[None, :, None]).astype(jnp.int32), axis=2))
    picked = jax.vmap(lambda enc_row, start_row: jnp.take(enc_row, start_row, axis=0))(encoded, starts)
    return low(picked.reshape(count * SEGS, D))

def reference(text_rows, text_segments, positives, w_mix, w_proj, w_up, w_down, b_up, b_rows, g_rows):
    half_rows = ROWS // 2
    query_segments = text_segments[:half_rows]
    passage_segments = text_segments[half_rows:]

    def forward(rows_all, mix_all, proj_all, up_all, down_all, upb_all, rowb_all, gain_all):
        weights_all = (mix_all, proj_all, up_all, down_all, upb_all, rowb_all, gain_all)
        query_out = encode_tower(rows_all[:half_rows], query_segments, split_tower(weights_all, 0), half_rows)
        passage_out = encode_tower(rows_all[half_rows:], passage_segments, split_tower(weights_all, 1), half_rows)
        query_cls = cls_vectors(query_out, query_segments, half_rows)
        passage_cls = cls_vectors(passage_out, passage_segments, half_rows)
        logits = low_back(2.0 * D ** (-0.5) * jnp.dot(query_cls, passage_cls.T, precision=highest))
        top_logit = lax.optimization_barrier(jnp.max(logits, axis=1, keepdims=True))
        log_total = top_logit[:, 0] + jnp.log(lax.optimization_barrier(jnp.sum(jnp.exp(logits - top_logit), axis=1)))
        chosen = jnp.take_along_axis(logits, positives[:, None], axis=1)[:, 0]
        return (jnp.sum(log_total - chosen), jnp.concatenate([query_out, passage_out], axis=0))
    floats = (text_rows.astype(jnp.float32), w_mix.astype(jnp.float32), w_proj.astype(jnp.float32), w_up.astype(jnp.float32), w_down.astype(jnp.float32), b_up.astype(jnp.float32), b_rows.astype(jnp.float32), g_rows.astype(jnp.float32))
    loss_total, pull_back, encodings = jax.vjp(forward, *floats, has_aux=True)
    gradients = pull_back(jnp.ones((), jnp.float32))
    return (encodings.astype(jnp.bfloat16), gradients[0], gradients[1], gradients[2], gradients[3], gradients[4], gradients[5], gradients[6], gradients[7])
```

```python
import functools

import jax
import jax.numpy as jnp
from jax import lax
from jax.experimental import pallas as pl
from jax.experimental.pallas import tpu as pltpu
from jax.sharding import PartitionSpec as P

D = 768
HEADS = 12
HEAD_DIM = 64
FF = 3072
SEGS = 4
BF = jnp.bfloat16
F32 = jnp.float32
MESH = pl.DeviceIdType.MESH

masked_score = -1e30
layer_eps = 1e-05


def dot_plain(left, right):
    return jnp.dot(left, right, preferred_element_type=F32)


def dot_over_rows(left, right):
    return lax.dot_general(left, right, (((0,), (0,)), ((), ())), preferred_element_type=F32)


def dot_over_columns(left, right):
    return lax.dot_general(left, right, (((1,), (1,)), ((), ())), preferred_element_type=F32)


def gelu_exact(inputs):
    return jax.nn.gelu(inputs, approximate=False)


def norm_parts(inputs):
    center = inputs - jnp.mean(inputs, axis=-1, keepdims=True)
    inverse = lax.rsqrt(jnp.mean(center * center, axis=-1, keepdims=True) + layer_eps)
    return center * inverse, inverse


def norm_back(unit, inverse, gain, grad):
    scaled = gain * grad
    return inverse * (
        scaled
        - jnp.mean(scaled, axis=-1, keepdims=True)
        - unit * jnp.mean(scaled * unit, axis=-1, keepdims=True)
    )


def gather_kernel(widths, *refs):
    kinds = len(widths)
    sources, results = refs[:kinds], refs[kinds : 2 * kinds]
    local, far_s, far_r, near_s, near_r, pass_s, pass_r, x_s, x_r, y_s, y_r, c_s, c_r = refs[2 * kinds :]
    place = lax.axis_index("dp")
    other = lax.axis_index("outer")
    z, x = place // 2, place % 2
    y, c = other // 2, other % 2
    z_near = z + 1 - 2 * (z % 2)
    z_far = 3 - z
    z_last = 3 - z_near
    tower = z // 2

    def device(zz, xx, yy, cc):
        return (zz * 2 + xx, yy * 2 + cc)

    to_far = device(z_far, x, y, c)
    to_near = device(z_near, x, y, c)
    to_x = device(z, 1 - x, y, c)
    to_y = device(z, x, 1 - y, c)
    to_core = device(z, x, y, 1 - c)
    barrier = pltpu.get_barrier_semaphore()
    for peer in (to_far, to_near, to_x, to_y, to_core):
        pl.semaphore_signal(barrier, inc=1, device_id=peer, device_id_type=MESH)
    pl.semaphore_wait(barrier, 5)

    def rows_of(k):
        return sources[k].shape[0]

    def own(k, which, half_row, half_col):
        n, r = widths[k], rows_of(k)
        row, rows = (half_row * (r // 2), r // 2)
        col, cols = which * n, n
        if half_col is not None:
            col, cols = col + half_col * (n // 2), n // 2
        return sources[k].at[
            pl.ds(pl.multiple_of(row, 16), rows), pl.ds(pl.multiple_of(col, 128), cols)
        ]

    def full(k, zz, xx, half_row, half_col):
        n, r = widths[k], rows_of(k)
        row, rows = (zz * 2 + xx) * r + half_row * (r // 2), r // 2
        col, cols = 0, n
        if half_col is not None:
            col, cols = half_col * (n // 2), n // 2
            col = pl.multiple_of(col, 128)
        return results[k].at[pl.ds(pl.multiple_of(row, 16), rows), pl.ds(col, cols)]

    def remote(src, dst, s, r, peer):
        return pltpu.make_async_remote_copy(
            src_ref=src, dst_ref=dst, send_sem=s, recv_sem=r, device_id=peer, device_id_type=MESH
        )

    planes = (z, z_near, z_far, z_last)
    sent = []

    def go(copy):
        copy.start()
        sent.append(copy)

    def x_copy(k, j):
        src = own(k, tower, c, y) if j == 0 else full(k, planes[j], x, c, y)
        return remote(src, full(k, planes[j], x, c, y), x_s.at[k, j], x_r.at[k, j], to_x)

    def y_copy(k, j):
        ref = full(k, planes[j], 1 - x, c, y)
        return remote(ref, ref, y_s.at[k, j], y_r.at[k, j], to_y)

    def c_copy(k, j):
        ref = full(k, planes[j % 4], x if j < 4 else 1 - x, c, None)
        return remote(ref, ref, c_s.at[k, j], c_r.at[k, j], to_core)

    locals_ = []
    for k in range(kinds):
        go(remote(own(k, 1 - tower, c, None), full(k, z, x, c, None), far_s.at[k], far_r.at[k], to_far))
        go(remote(own(k, tower, c, None), full(k, z, x, c, None), near_s.at[k], near_r.at[k], to_near))
        go(x_copy(k, 0))
        n, r = widths[k], rows_of(k)
        copy = pltpu.make_async_copy(
            sources[k].at[:, pl.ds(pl.multiple_of(tower * n, 128), n)],
            results[k].at[pl.ds(pl.multiple_of((z * 2 + x) * r, 16), r), :],
            local.at[k],
        )
        copy.start()
        locals_.append(copy)

    def wait_far(k):
        ref = full(k, z_far, x, c, None)
        remote(ref, ref, far_s.at[k], far_r.at[k], to_far).wait_recv()

    def wait_near(k):
        ref = full(k, z_near, x, c, None)
        remote(ref, ref, near_s.at[k], near_r.at[k], to_near).wait_recv()

    def wait_pass(k):
        ref = full(k, z_last, x, c, None)
        remote(ref, ref, pass_s.at[k], pass_r.at[k], to_near).wait_recv()

    def wait_x(k, j):
        ref = full(k, planes[j], 1 - x, c, y)
        remote(ref, ref, x_s.at[k, j], x_r.at[k, j], to_x).wait_recv()

    def wait_y(k, j):
        ref = full(k, planes[j], 1 - x, c, 1 - y)
        remote(ref, ref, y_s.at[k, j], y_r.at[k, j], to_y).wait_recv()

    def wait_c(k, j):
        ref = full(k, planes[j % 4], x if j < 4 else 1 - x, 1 - c, None)
        remote(ref, ref, c_s.at[k, j], c_r.at[k, j], to_core).wait_recv()

    def first(k):
        wait_far(k)
        ref = full(k, z_far, x, c, None)
        go(remote(ref, ref, pass_s.at[k], pass_r.at[k], to_near))
        go(x_copy(k, 2))
        go(c_copy(k, 2))
        wait_near(k)
        go(x_copy(k, 1))
        go(c_copy(k, 1))
        wait_x(k, 0)
        go(y_copy(k, 0))

    def second(k):
        wait_pass(k)
        go(x_copy(k, 3))
        go(c_copy(k, 3))
        for j in (2, 1):
            wait_x(k, j)
            go(y_copy(k, j))

    def third(k):
        wait_x(k, 3)
        go(y_copy(k, 3))
        for j in (0, 2, 1, 3):
            wait_y(k, j)
            go(c_copy(k, 4 + j))

    for step in range(kinds + 2):
        if step < kinds:
            first(step)
        if 0 <= step - 1 < kinds:
            second(step - 1)
        if 0 <= step - 2 < kinds:
            third(step - 2)
    for k in range(kinds):
        for j in range(1, 8):
            wait_c(k, j)
    for copy in sent:
        copy.wait_send()
    for copy in locals_:
        copy.wait()


def gather_weights(weights, widths, n_dp, n_outer):
    if (n_dp, n_outer) != (8, 4):
        tower = lax.axis_index("dp") * 2 // n_dp
        whole = [lax.all_gather(w, "dp", axis=0, tiled=True) for w in weights]
        return [lax.dynamic_slice_in_dim(w, tower * n, n, 1) for w, n in zip(whole, widths)]
    kinds = len(weights)
    sem = pltpu.SemaphoreType.DMA
    return pl.pallas_call(
        functools.partial(gather_kernel, widths),
        out_shape=[jax.ShapeDtypeStruct((w.shape[0] * n_dp, n), w.dtype) for w, n in zip(weights, widths)],
        in_specs=[pl.BlockSpec(memory_space=pl.ANY)] * kinds,
        out_specs=[pl.BlockSpec(memory_space=pl.ANY)] * kinds,
        scratch_shapes=[sem((kinds,))] * 7
        + [sem((kinds, 4))] * 4
        + [sem((kinds, 8))] * 2,
        compiler_params=pltpu.CompilerParams(collective_id=1, has_side_effects=True),
        name="gather_weights",
    )(*weights)


def spread_kernel(n_outer, total, whole_ref, parts_ref, all_ref, sliced_ref, local, s_one, r_one, s_two, r_two):
    dp, outer = lax.axis_index("dp"), lax.axis_index("outer")
    me = dp * n_outer + outer
    barrier = pltpu.get_barrier_semaphore()

    def greet(i, carry):
        peer = lax.rem(me + i, total)
        pl.semaphore_signal(barrier, inc=1, device_id=(peer // n_outer, lax.rem(peer, n_outer)), device_id_type=MESH)
        return carry

    lax.fori_loop(1, total, greet, 0)
    pl.semaphore_wait(barrier, total - 1)

    def copies(i):
        peer = lax.rem(me + i, total)
        there = peer // n_outer
        device = (there, lax.rem(peer, n_outer))
        one = pltpu.make_async_remote_copy(
            src_ref=whole_ref, dst_ref=all_ref.at[me], send_sem=s_one.at[i], recv_sem=r_one.at[i],
            device_id=device, device_id_type=MESH,
        )
        if parts_ref is None:
            return (one,)
        two = pltpu.make_async_remote_copy(
            src_ref=parts_ref.at[there], dst_ref=sliced_ref.at[me], send_sem=s_two.at[i], recv_sem=r_two.at[i],
            device_id=device, device_id_type=MESH,
        )
        return (one, two)

    def send(i, carry):
        for copy in copies(i):
            copy.start()
        return carry

    lax.fori_loop(1, total, send, 0)
    own = [pltpu.make_async_copy(whole_ref, all_ref.at[me], local.at[0])]
    if parts_ref is not None:
        own.append(pltpu.make_async_copy(parts_ref.at[dp], sliced_ref.at[me], local.at[1]))
    for copy in own:
        copy.start()

    def settle(i, carry):
        for copy in copies(i):
            copy.wait()
        return carry

    lax.fori_loop(1, total, settle, 0)
    for copy in own:
        copy.wait()


def spread(whole, parts, n_dp, n_outer, identity):
    total = n_dp * n_outer
    sem = pltpu.SemaphoreType.DMA
    out_shape = [jax.ShapeDtypeStruct((total,) + whole.shape, whole.dtype)]
    operands = [whole]
    if parts is not None:
        out_shape.append(jax.ShapeDtypeStruct((total,) + parts.shape[1:], parts.dtype))
        operands.append(parts)
        kernel = functools.partial(spread_kernel, n_outer, total)
        scratch = [sem((2,))] + [sem((total,))] * 4
    else:
        def kernel(w, a, local, s, r):
            spread_kernel(n_outer, total, w, None, a, None, local, s, r, None, None)
        scratch = [sem((2,))] + [sem((total,))] * 2
    return pl.pallas_call(
        kernel,
        out_shape=out_shape,
        in_specs=[pl.BlockSpec(memory_space=pltpu.VMEM)] * len(operands),
        out_specs=[pl.BlockSpec(memory_space=pltpu.VMEM)] * len(out_shape),
        scratch_shapes=scratch,
        compiler_params=pltpu.CompilerParams(
            collective_id=identity, has_side_effects=True, vmem_limit_bytes=48 << 20
        ),
        name="spread%d" % identity,
    )(*operands)


def expand_heads(rows):
    head_of = jnp.arange(D, dtype=jnp.int32) // HEAD_DIM
    keep = head_of[None, :] == jnp.arange(HEADS, dtype=jnp.int32)[:, None]
    return jnp.where(keep[:, None, :], rows[None], 0).reshape(HEADS * rows.shape[0], D)


def per_device(text_rows, text_segments, positives, w_mix, w_proj, w_up, w_down, b_up, b_rows, g_rows):
    n_dp, n_outer = lax.axis_size("dp"), lax.axis_size("outer")
    total = n_dp * n_outer
    own_index = lax.axis_index(("dp", "outer"))
    tower = own_index * 2 // total
    rows_in, segments = text_rows[0], text_segments[0]
    row_len = rows_in.shape[0]
    widths = (3 * D, D, FF, D)
    wm, wp, wu, wd = gather_weights((w_mix, w_proj, w_up, w_down), widths, n_dp, n_outer)
    part_f, part_d = b_up.shape[0], b_rows.shape[0]
    small = jnp.concatenate([b_up.reshape(part_f // part_d, part_d, 2).transpose(0, 2, 1).reshape(-1, part_d), b_rows.T, g_rows.T], axis=0)
    small = lax.all_gather(small, "dp", axis=0)
    split = 2 * (part_f // part_d)
    up_b = small[:, :split].reshape(n_dp, part_f // part_d, 2, part_d).transpose(2, 0, 1, 3).reshape(2, FF)
    row_b = small[:, split : split + 12].transpose(1, 0, 2).reshape(2, 6, D)
    gain_b = small[:, split + 12 :].transpose(1, 0, 2).reshape(2, 2, D)
    pick = lambda both_towers: jnp.where(tower == 0, both_towers[0], both_towers[1]).astype(F32)
    c_up, biases, gains = pick(up_b), pick(row_b), pick(gain_b)
    bq, bv, bo, o1, bd, o2 = (biases[i] for i in range(6))
    g1, g2 = gains[0], gains[1]

    scaled = HEAD_DIM ** (-0.5)
    mixed = (dot_plain(rows_in, wm) + jnp.concatenate([bq, jnp.zeros_like(bq), bv])).astype(BF)
    q, k, v = mixed[:, :D], mixed[:, D : 2 * D], mixed[:, 2 * D :]
    allowed = segments[:, None] == segments[None, :]
    heads = lambda m: m.reshape(row_len, HEADS, HEAD_DIM)
    scores = jnp.einsum("qhe,khe->hqk", heads(q), heads(k), preferred_element_type=F32) * scaled
    scores = jnp.where(allowed[None], scores, masked_score)
    top = jnp.max(scores, axis=-1, keepdims=True)
    raised = jnp.exp(scores - top)
    chances = (raised / jnp.sum(raised, axis=-1, keepdims=True)).astype(BF)
    attended = jnp.einsum("hqk,khe->qhe", chances, heads(v), preferred_element_type=F32).reshape(row_len, D).astype(BF)
    before_one = rows_in.astype(F32) + dot_plain(attended, wp) + bo
    unit_one, inv_one = norm_parts(before_one)
    h1 = unit_one * g1 + o1
    h1_low = h1.astype(BF)
    up_pre = dot_plain(h1_low, wu) + c_up
    gelu_low = gelu_exact(up_pre).astype(BF)
    before_two = h1 + dot_plain(gelu_low, wd) + bd
    unit_two, inv_two = norm_parts(before_two)
    encoded = unit_two * g2 + o2

    levels = jnp.arange(SEGS, dtype=jnp.int32)
    starts = jnp.sum((segments[None, :] < levels[:, None]).astype(jnp.int32), axis=1)
    at = lambda m: jnp.take(m, starts, axis=0)
    vectors = at(encoded).astype(BF)
    all_cls = spread(vectors, None, n_dp, n_outer, 2)[0].reshape(total * SEGS, D)
    texts = total * SEGS // 2
    all_q, all_p = all_cls[:texts], all_cls[texts:]
    pair_scale = 2.0 * D ** (-0.5)
    logits = dot_over_columns(all_q, all_p) * pair_scale
    raised_l = jnp.exp(logits - jnp.max(logits, axis=1, keepdims=True))
    hit = (positives[:, None] == jnp.arange(texts, dtype=jnp.int32)[None, :]).astype(F32)
    d_logits = (raised_l / jnp.sum(raised_l, axis=1, keepdims=True) - hit).astype(BF)
    position = own_index * SEGS - tower * texts
    d_q = dot_plain(lax.dynamic_slice_in_dim(d_logits, position, SEGS, 0), all_p)
    d_p = dot_over_rows(lax.dynamic_slice_in_dim(d_logits, position, SEGS, 1), all_q)
    d_cls = jnp.where(tower == 0, d_q, d_p) * pair_scale

    ut, it = at(unit_two), at(inv_two)
    dg2, do2 = jnp.sum(d_cls * ut, axis=0), jnp.sum(d_cls, axis=0)
    dz2 = norm_back(ut, it, g2, d_cls)
    df = dz2.astype(BF)
    dg = dot_over_columns(df, wd)
    u_r = at(up_pre)
    _, gelu_back = jax.vjp(gelu_exact, u_r)
    du = gelu_back(dg)[0].astype(BF)
    dh1 = dz2 + dot_over_columns(du, wu)
    uo, io = at(unit_one), at(inv_one)
    dg1, do1 = jnp.sum(dh1 * uo, axis=0), jnp.sum(dh1, axis=0)
    dz1 = norm_back(uo, io, g1, dh1)
    db = dz1.astype(BF)
    da = dot_over_columns(db, wp).astype(BF)
    q_r = at(q)
    q_wide, a_wide = expand_heads(q_r), expand_heads(da)
    own_segment = jnp.tile(levels, HEADS)
    open_keys = own_segment[:, None] == segments[None, :]
    s_r = jnp.where(open_keys, dot_over_columns(q_wide, k) * scaled, masked_score)
    e_r = jnp.exp(s_r - jnp.max(s_r, axis=-1, keepdims=True))
    p_r = e_r / jnp.sum(e_r, axis=-1, keepdims=True)
    pl_r = p_r.astype(BF)
    dp_r = dot_over_columns(a_wide, v)
    ds_r = (p_r * (dp_r - jnp.sum(p_r * dp_r, axis=-1, keepdims=True))).astype(BF)
    dq_wide = dot_plain(ds_r, k).reshape(HEADS, SEGS, HEADS, HEAD_DIM)
    dq = (jnp.einsum("hshe->she", dq_wide).reshape(SEGS, D) * scaled).astype(BF)
    y_r = (dot_plain(ds_r, rows_in) * scaled).astype(BF)
    z_r = dot_plain(pl_r, rows_in).astype(BF)
    weight_sum = jnp.sum(pl_r.astype(F32), axis=1, keepdims=True)
    dbv = jnp.sum(weight_sum * a_wide.astype(F32), axis=0)
    t_k = (dot_over_columns(q_wide, wm[:, D : 2 * D]) * scaled).astype(BF)
    t_v = dot_over_columns(a_wide, wm[:, 2 * D :]).astype(BF)
    d_rows = dot_over_rows(jnp.concatenate([ds_r, pl_r], axis=0), jnp.concatenate([t_k, t_v], axis=0))
    d_rows_at = dz1 + dot_over_columns(dq, wm[:, :D])
    spot = (starts[:, None] == jnp.arange(row_len, dtype=jnp.int32)[None, :])
    for s in range(SEGS):
        d_rows = d_rows + jnp.where(spot[s][:, None], d_rows_at[s][None, :], 0.0)

    ff_rows = SEGS * FF // D
    whole = jnp.concatenate(
        [df, db, dq, q_r, da, du.reshape(ff_rows, D), jnp.stack([dbv, do1, do2, dg1, dg2]).astype(BF), jnp.zeros((3, D), BF)],
        axis=0,
    )
    g_r, h_r, at_r, x_r = at(gelu_low), at(h1_low), at(attended), at(rows_in)
    by_part = lambda m: m.reshape(m.shape[0], n_dp, m.shape[1] // n_dp).transpose(1, 0, 2)
    parts = jnp.concatenate(
        [by_part(h_r), by_part(at_r), by_part(x_r), by_part(y_r), by_part(z_r),
         by_part(g_r).reshape(n_dp, -1, part_d)],
        axis=1,
    )
    all_w, all_s = spread(whole, parts, n_dp, n_outer, 3)
    half = total // 2
    tw = all_w.reshape(2, half, -1, D)
    ts = all_s.reshape(2, half, -1, part_d)
    rank = lambda m: m.reshape(half * SEGS, -1)
    grads = []
    outs = [[], [], [], []]
    vec_b, vec_g, vec_u = [], [], []
    mine = lax.axis_index("dp")
    for t in range(2):
        w, s = tw[t], ts[t]
        df_a, db_a, dq_a, q_a, da_a = (rank(w[:, 4 * i : 4 * i + 4]) for i in range(5))
        du_a = w[:, 20 : 20 + ff_rows].reshape(half * SEGS, FF)
        vec = jnp.sum(w[:, 20 + ff_rows : 25 + ff_rows].astype(F32), axis=0)
        h_a, at_a, x_a = (rank(s[:, 4 * i : 4 * i + 4]) for i in range(3))
        y_a = s[:, 12:60].reshape(half, HEADS, SEGS, part_d)
        z_a = s[:, 60:108].reshape(half, HEADS, SEGS, part_d)
        g_a = s[:, 108:].reshape(half * SEGS, part_f)
        by_head = lambda m: m.reshape(half, SEGS, HEADS, HEAD_DIM)
        gk = jnp.einsum("rhsa,rshe->ahe", y_a, by_head(q_a), preferred_element_type=F32).reshape(part_d, D)
        gv = jnp.einsum("rhsa,rshe->ahe", z_a, by_head(da_a), preferred_element_type=F32).reshape(part_d, D)
        outs[0] += [dot_over_rows(x_a, dq_a), gk, gv]
        outs[1].append(dot_over_rows(at_a, db_a))
        outs[2].append(dot_over_rows(h_a, du_a))
        outs[3].append(dot_over_rows(g_a, df_a))
        col = lambda m, n: lax.dynamic_slice_in_dim(m, mine * n, n, 0)
        summed = lambda m: jnp.sum(m.astype(F32), axis=0)
        vec_b += [col(m, part_d) for m in (summed(dq_a), vec[0], summed(db_a), vec[1], summed(df_a), vec[2])]
        vec_g += [col(m, part_d) for m in (vec[3], vec[4])]
        vec_u.append(col(summed(du_a), part_f))
    return (
        encoded.astype(BF)[None],
        d_rows[None],
        jnp.concatenate(outs[0], axis=1),
        jnp.concatenate(outs[1], axis=1),
        jnp.concatenate(outs[2], axis=1),
        jnp.concatenate(outs[3], axis=1),
        jnp.stack(vec_u, axis=1),
        jnp.stack(vec_b, axis=1),
        jnp.stack(vec_g, axis=1),
    )


def solution(mesh):
    rows, cols = P(("dp", "outer"), None, None), P("dp", None)
    return jax.shard_map(
        per_device,
        mesh=mesh,
        in_specs=(rows, P(("dp", "outer"), None), P(), cols, cols, cols, cols, cols, cols, cols),
        out_specs=(rows, rows, cols, cols, cols, cols, cols, cols, cols),
        check_vma=False,
    )
```

```python
import functools

import jax
import jax.numpy as jnp
from jax import lax
from jax.experimental import pallas as pl
from jax.experimental.pallas import tpu as pltpu
from jax.sharding import PartitionSpec as P

D = 768
HEADS = 12
HEAD_DIM = 64
FF = 3072
SEGS = 4
BF = jnp.bfloat16
F32 = jnp.float32
MESH = pl.DeviceIdType.MESH

masked_score = -1e30
layer_eps = 1e-05


def dot_plain(left, right):
    return jnp.dot(left, right, preferred_element_type=F32)


def dot_over_rows(left, right):
    return lax.dot_general(left, right, (((0,), (0,)), ((), ())), preferred_element_type=F32)


def dot_over_columns(left, right):
    return lax.dot_general(left, right, (((1,), (1,)), ((), ())), preferred_element_type=F32)


def gelu_exact(inputs):
    return jax.nn.gelu(inputs, approximate=False)


def norm_parts(inputs):
    center = inputs - jnp.mean(inputs, axis=-1, keepdims=True)
    inverse = lax.rsqrt(jnp.mean(center * center, axis=-1, keepdims=True) + layer_eps)
    return center * inverse, inverse


def norm_back(unit, inverse, gain, grad):
    scaled = gain * grad
    return inverse * (
        scaled
        - jnp.mean(scaled, axis=-1, keepdims=True)
        - unit * jnp.mean(scaled * unit, axis=-1, keepdims=True)
    )


def gather_weights(weights, widths, n_dp):
    tower = lax.axis_index("dp") * 2 // n_dp
    whole = [lax.all_gather(w, "dp", axis=0, tiled=True) for w in weights]
    return [lax.dynamic_slice_in_dim(w, tower * n, n, 1) for w, n in zip(whole, widths)]


def spread_kernel(n_outer, total, whole_ref, parts_ref, all_ref, sliced_ref, local, s_one, r_one, s_two, r_two):
    dp, outer = lax.axis_index("dp"), lax.axis_index("outer")
    me = dp * n_outer + outer
    barrier = pltpu.get_barrier_semaphore()

    def greet(i, carry):
        peer = lax.rem(me + i, total)
        pl.semaphore_signal(barrier, inc=1, device_id=(peer // n_outer, lax.rem(peer, n_outer)), device_id_type=MESH)
        return carry

    lax.fori_loop(1, total, greet, 0)
    pl.semaphore_wait(barrier, total - 1)

    def copies(i):
        peer = lax.rem(me + i, total)
        there = peer // n_outer
        device = (there, lax.rem(peer, n_outer))
        one = pltpu.make_async_remote_copy(
            src_ref=whole_ref, dst_ref=all_ref.at[me], send_sem=s_one.at[i], recv_sem=r_one.at[i],
            device_id=device, device_id_type=MESH,
        )
        if parts_ref is None:
            return (one,)
        two = pltpu.make_async_remote_copy(
            src_ref=parts_ref.at[there], dst_ref=sliced_ref.at[me], send_sem=s_two.at[i], recv_sem=r_two.at[i],
            device_id=device, device_id_type=MESH,
        )
        return (one, two)

    def send(i, carry):
        for copy in copies(i):
            copy.start()
        return carry

    lax.fori_loop(1, total, send, 0)
    own = [pltpu.make_async_copy(whole_ref, all_ref.at[me], local.at[0])]
    if parts_ref is not None:
        own.append(pltpu.make_async_copy(parts_ref.at[dp], sliced_ref.at[me], local.at[1]))
    for copy in own:
        copy.start()

    def settle(i, carry):
        for copy in copies(i):
            copy.wait()
        return carry

    lax.fori_loop(1, total, settle, 0)
    for copy in own:
        copy.wait()


def spread(whole, parts, n_dp, n_outer, identity):
    total = n_dp * n_outer
    sem = pltpu.SemaphoreType.DMA
    out_shape = [jax.ShapeDtypeStruct((total,) + whole.shape, whole.dtype)]
    operands = [whole]
    if parts is not None:
        out_shape.append(jax.ShapeDtypeStruct((total,) + parts.shape[1:], parts.dtype))
        operands.append(parts)
        kernel = functools.partial(spread_kernel, n_outer, total)
        scratch = [sem((2,))] + [sem((total,))] * 4
    else:
        def kernel(w, a, local, s, r):
            spread_kernel(n_outer, total, w, None, a, None, local, s, r, None, None)
        scratch = [sem((2,))] + [sem((total,))] * 2
    return pl.pallas_call(
        kernel,
        out_shape=out_shape,
        in_specs=[pl.BlockSpec(memory_space=pltpu.VMEM)] * len(operands),
        out_specs=[pl.BlockSpec(memory_space=pltpu.VMEM)] * len(out_shape),
        scratch_shapes=scratch,
        compiler_params=pltpu.CompilerParams(
            collective_id=identity, has_side_effects=True, vmem_limit_bytes=48 << 20
        ),
        name="spread%d" % identity,
    )(*operands)


def expand_heads(rows):
    head_of = jnp.arange(D, dtype=jnp.int32) // HEAD_DIM
    keep = head_of[None, :] == jnp.arange(HEADS, dtype=jnp.int32)[:, None]
    return jnp.where(keep[:, None, :], rows[None], 0).reshape(HEADS * rows.shape[0], D)


def per_device(text_rows, text_segments, positives, w_mix, w_proj, w_up, w_down, b_up, b_rows, g_rows):
    n_dp, n_outer = lax.axis_size("dp"), lax.axis_size("outer")
    total = n_dp * n_outer
    own_index = lax.axis_index(("dp", "outer"))
    tower = own_index * 2 // total
    rows_in, segments = text_rows[0], text_segments[0]
    row_len = rows_in.shape[0]
    widths = (3 * D, D, FF, D)
    wm, wp, wu, wd = gather_weights((w_mix, w_proj, w_up, w_down), widths, n_dp)
    part_f, part_d = b_up.shape[0], b_rows.shape[0]
    small = jnp.concatenate([b_up.reshape(part_f // part_d, part_d, 2).transpose(0, 2, 1).reshape(-1, part_d), b_rows.T, g_rows.T], axis=0)
    small = lax.all_gather(small, "dp", axis=0)
    split = 2 * (part_f // part_d)
    up_b = small[:, :split].reshape(n_dp, part_f // part_d, 2, part_d).transpose(2, 0, 1, 3).reshape(2, FF)
    row_b = small[:, split : split + 12].transpose(1, 0, 2).reshape(2, 6, D)
    gain_b = small[:, split + 12 :].transpose(1, 0, 2).reshape(2, 2, D)
    pick = lambda both_towers: jnp.where(tower == 0, both_towers[0], both_towers[1]).astype(F32)
    c_up, biases, gains = pick(up_b), pick(row_b), pick(gain_b)
    bq, bv, bo, o1, bd, o2 = (biases[i] for i in range(6))
    g1, g2 = gains[0], gains[1]

    scaled = HEAD_DIM ** (-0.5)
    mixed = (dot_plain(rows_in, wm) + jnp.concatenate([bq, jnp.zeros_like(bq), bv])).astype(BF)
    q, k, v = mixed[:, :D], mixed[:, D : 2 * D], mixed[:, 2 * D :]
    allowed = segments[:, None] == segments[None, :]
    heads = lambda m: m.reshape(row_len, HEADS, HEAD_DIM)
    scores = jnp.einsum("qhe,khe->hqk", heads(q), heads(k), preferred_element_type=F32) * scaled
    scores = jnp.where(allowed[None], scores, masked_score)
    top = jnp.max(scores, axis=-1, keepdims=True)
    raised = jnp.exp(scores - top)
    chances = (raised / jnp.sum(raised, axis=-1, keepdims=True)).astype(BF)
    attended = jnp.einsum("hqk,khe->qhe", chances, heads(v), preferred_element_type=F32).reshape(row_len, D).astype(BF)
    before_one = rows_in.astype(F32) + dot_plain(attended, wp) + bo
    unit_one, inv_one = norm_parts(before_one)
    h1 = unit_one * g1 + o1
    h1_low = h1.astype(BF)
    up_pre = dot_plain(h1_low, wu) + c_up
    gelu_low = gelu_exact(up_pre).astype(BF)
    before_two = h1 + dot_plain(gelu_low, wd) + bd
    unit_two, inv_two = norm_parts(before_two)
    encoded = unit_two * g2 + o2

    levels = jnp.arange(SEGS, dtype=jnp.int32)
    starts = jnp.sum((segments[None, :] < levels[:, None]).astype(jnp.int32), axis=1)
    at = lambda m: jnp.take(m, starts, axis=0)
    vectors = at(encoded).astype(BF)
    all_cls = spread(vectors, None, n_dp, n_outer, 2)[0].reshape(total * SEGS, D)
    texts = total * SEGS // 2
    all_q, all_p = all_cls[:texts], all_cls[texts:]
    pair_scale = 2.0 * D ** (-0.5)
    logits = dot_over_columns(all_q, all_p) * pair_scale
    raised_l = jnp.exp(logits - jnp.max(logits, axis=1, keepdims=True))
    hit = (positives[:, None] == jnp.arange(texts, dtype=jnp.int32)[None, :]).astype(F32)
    d_logits = (raised_l / jnp.sum(raised_l, axis=1, keepdims=True) - hit).astype(BF)
    position = own_index * SEGS - tower * texts
    d_q = dot_plain(lax.dynamic_slice_in_dim(d_logits, position, SEGS, 0), all_p)
    d_p = dot_over_rows(lax.dynamic_slice_in_dim(d_logits, position, SEGS, 1), all_q)
    d_cls = jnp.where(tower == 0, d_q, d_p) * pair_scale

    ut, it = at(unit_two), at(inv_two)
    dg2, do2 = jnp.sum(d_cls * ut, axis=0), jnp.sum(d_cls, axis=0)
    dz2 = norm_back(ut, it, g2, d_cls)
    df = dz2.astype(BF)
    dg = dot_over_columns(df, wd)
    u_r = at(up_pre)
    _, gelu_back = jax.vjp(gelu_exact, u_r)
    du = gelu_back(dg)[0].astype(BF)
    dh1 = dz2 + dot_over_columns(du, wu)
    uo, io = at(unit_one), at(inv_one)
    dg1, do1 = jnp.sum(dh1 * uo, axis=0), jnp.sum(dh1, axis=0)
    dz1 = norm_back(uo, io, g1, dh1)
    db = dz1.astype(BF)
    da = dot_over_columns(db, wp).astype(BF)
    q_r = at(q)
    q_wide, a_wide = expand_heads(q_r), expand_heads(da)
    own_segment = jnp.tile(levels, HEADS)
    open_keys = own_segment[:, None] == segments[None, :]
    s_r = jnp.where(open_keys, dot_over_columns(q_wide, k) * scaled, masked_score)
    e_r = jnp.exp(s_r - jnp.max(s_r, axis=-1, keepdims=True))
    p_r = e_r / jnp.sum(e_r, axis=-1, keepdims=True)
    pl_r = p_r.astype(BF)
    dp_r = dot_over_columns(a_wide, v)
    ds_r = (p_r * (dp_r - jnp.sum(p_r * dp_r, axis=-1, keepdims=True))).astype(BF)
    dq_wide = dot_plain(ds_r, k).reshape(HEADS, SEGS, HEADS, HEAD_DIM)
    dq = (jnp.einsum("hshe->she", dq_wide).reshape(SEGS, D) * scaled).astype(BF)
    y_r = (dot_plain(ds_r, rows_in) * scaled).astype(BF)
    z_r = dot_plain(pl_r, rows_in).astype(BF)
    weight_sum = jnp.sum(pl_r.astype(F32), axis=1, keepdims=True)
    dbv = jnp.sum(weight_sum * a_wide.astype(F32), axis=0)
    t_k = (dot_over_columns(q_wide, wm[:, D : 2 * D]) * scaled).astype(BF)
    t_v = dot_over_columns(a_wide, wm[:, 2 * D :]).astype(BF)
    d_rows = dot_over_rows(jnp.concatenate([ds_r, pl_r], axis=0), jnp.concatenate([t_k, t_v], axis=0))
    d_rows_at = dz1 + dot_over_columns(dq, wm[:, :D])
    spot = (starts[:, None] == jnp.arange(row_len, dtype=jnp.int32)[None, :])
    for s in range(SEGS):
        d_rows = d_rows + jnp.where(spot[s][:, None], d_rows_at[s][None, :], 0.0)

    ff_rows = SEGS * FF // D
    whole = jnp.concatenate(
        [df, db, dq, q_r, da, du.reshape(ff_rows, D), jnp.stack([dbv, do1, do2, dg1, dg2]).astype(BF), jnp.zeros((3, D), BF)],
        axis=0,
    )
    g_r, h_r, at_r, x_r = at(gelu_low), at(h1_low), at(attended), at(rows_in)
    by_part = lambda m: m.reshape(m.shape[0], n_dp, m.shape[1] // n_dp).transpose(1, 0, 2)
    parts = jnp.concatenate(
        [by_part(h_r), by_part(at_r), by_part(x_r), by_part(y_r), by_part(z_r),
         by_part(g_r).reshape(n_dp, -1, part_d)],
        axis=1,
    )
    all_w, all_s = spread(whole, parts, n_dp, n_outer, 3)
    half = total // 2
    tw = all_w.reshape(2, half, -1, D)
    ts = all_s.reshape(2, half, -1, part_d)
    rank = lambda m: m.reshape(half * SEGS, -1)
    grads = []
    outs = [[], [], [], []]
    vec_b, vec_g, vec_u = [], [], []
    mine = lax.axis_index("dp")
    for t in range(2):
        w, s = tw[t], ts[t]
        df_a, db_a, dq_a, q_a, da_a = (rank(w[:, 4 * i : 4 * i + 4]) for i in range(5))
        du_a = w[:, 20 : 20 + ff_rows].reshape(half * SEGS, FF)
        vec = jnp.sum(w[:, 20 + ff_rows : 25 + ff_rows].astype(F32), axis=0)
        h_a, at_a, x_a = (rank(s[:, 4 * i : 4 * i + 4]) for i in range(3))
        y_a = s[:, 12:60].reshape(half, HEADS, SEGS, part_d)
        z_a = s[:, 60:108].reshape(half, HEADS, SEGS, part_d)
        g_a = s[:, 108:].reshape(half * SEGS, part_f)
        by_head = lambda m: m.reshape(half, SEGS, HEADS, HEAD_DIM)
        gk = jnp.einsum("rhsa,rshe->ahe", y_a, by_head(q_a), preferred_element_type=F32).reshape(part_d, D)
        gv = jnp.einsum("rhsa,rshe->ahe", z_a, by_head(da_a), preferred_element_type=F32).reshape(part_d, D)
        outs[0] += [dot_over_rows(x_a, dq_a), gk, gv]
        outs[1].append(dot_over_rows(at_a, db_a))
        outs[2].append(dot_over_rows(h_a, du_a))
        outs[3].append(dot_over_rows(g_a, df_a))
        col = lambda m, n: lax.dynamic_slice_in_dim(m, mine * n, n, 0)
        summed = lambda m: jnp.sum(m.astype(F32), axis=0)
        vec_b += [col(m, part_d) for m in (summed(dq_a), vec[0], summed(db_a), vec[1], summed(df_a), vec[2])]
        vec_g += [col(m, part_d) for m in (vec[3], vec[4])]
        vec_u.append(col(summed(du_a), part_f))
    return (
        encoded.astype(BF)[None],
        d_rows[None],
        jnp.concatenate(outs[0], axis=1),
        jnp.concatenate(outs[1], axis=1),
        jnp.concatenate(outs[2], axis=1),
        jnp.concatenate(outs[3], axis=1),
        jnp.stack(vec_u, axis=1),
        jnp.stack(vec_b, axis=1),
        jnp.stack(vec_g, axis=1),
    )


PIECES = (
    [(0, D, D), (0, 2 * D, D), (0, 0, D), (1, 0, D)]
    + [(2, D * i, D) for i in range(4)]
    + [(3, 256 * i, 256) for i in range(3)]
)
WIDTHS = (3 * D, D, FF, D)
ROW = 16
BLOCK = 256


def iota(shape, dim):
    return lax.broadcasted_iota(jnp.int32, shape, dim)


def gelu_erf(u):
    return 0.5 * u * (1.0 + lax.erf(u * 0.7071067811865476))


def gelu_slope(u):
    return 0.5 * (1.0 + lax.erf(u * 0.7071067811865476)) + u * (0.3989422804014327 * jnp.exp(-0.5 * u * u))


def main_kernel(
    x_ref, seg_ref, pos_ref, sv_ref, w_mix, w_proj, w_up, w_down,
    enc_ref, drow_ref, fq_ref, fu_ref, fa_ref, se_ref, sl_ref,
    wa, wd, sv_all, q_s, k_s, v_s, a_s, mask_s, b_s, h_s, hl_s, g_s, sel_s,
    cls_own, cls_all, cls_f, src_q, src_u, src_a, src_e, src_l,
    ld, far_s, near_s, z_r, rel_s, x_s, x_r, y_s, y_r, c_s, c_r, sv_sem, sv_r, cls_sem, cls_r,
    fl, fz_s, fz_r, ff_s, ff_r, fg_s, fg_r, fc_s, fc_r, s1_s, s1_r, s2_s, s2_r, s3_s, s3_r,
):
    sources = (w_mix, w_proj, w_up, w_down)
    place, other = lax.axis_index("dp"), lax.axis_index("outer")
    z, x = place // 2, place % 2
    y, c = other // 2, other % 2
    tower, zi = z // 2, z % 2
    me = place * 4 + other
    inner = zi * (1 - tower) + (1 - zi) * tower
    zn = z + 1 - 2 * zi
    z_a, z_b = 2 - tower, 3 - 3 * tower
    scaled = HEAD_DIM ** (-0.5)
    row_len = x_ref.shape[0]

    def device(zz, xx, yy, cc):
        return (zz * 2 + xx, yy * 2 + cc)

    to_near, to_far = device(zn, x, y, c), device(z_a, x, y, c)
    to_x, to_y, to_core = device(z, 1 - x, y, c), device(z, x, 1 - y, c), device(z, x, y, 1 - c)

    barrier = pltpu.get_barrier_semaphore()

    def peer_at(i):
        p = lax.rem(me + i, 32)
        return (p // 4, lax.rem(p, 4))

    def greet(i, carry):
        pl.semaphore_signal(barrier, inc=1, device_id=peer_at(i), device_id_type=MESH)
        return carry

    lax.fori_loop(1, 32, greet, 0)
    pl.semaphore_wait(barrier, 31)

    def remote(src, dst, s, r, peer):
        return pltpu.make_async_remote_copy(
            src_ref=src, dst_ref=dst, send_sem=s, recv_sem=r, device_id=peer, device_id_type=MESH
        )

    def arrived(ref, s, r):
        remote(ref, ref, s, r, to_x).wait_recv()

    sent = []

    def go(copy):
        copy.start()
        sent.append(copy)

    def dims(k):
        tensor, first, cols = PIECES[k]
        return tensor, sources[tensor].shape[0], first, cols

    def own(k, which, half_row, half_col):
        tensor, r, first, n = dims(k)
        row, rows = (0, r) if half_row is None else (half_row * (r // 2), r // 2)
        col, cols = which * WIDTHS[tensor] + first, n
        if half_col is not None:
            col, cols = col + half_col * (n // 2), n // 2
        return sources[tensor].at[
            pl.ds(pl.multiple_of(row, 16), rows), pl.ds(pl.multiple_of(col, 128), cols)
        ]

    def held(k):
        return wa.at[k] if k < 8 else wd.at[k - 8]

    def full(k, zz, xx, half_row, half_col):
        tensor, r, first, n = dims(k)
        row, rows = (zz * 2 + xx) * r, r
        if half_row is not None:
            row, rows = row + half_row * (r // 2), r // 2
        col, cols = (0, n) if half_col is None else (pl.multiple_of(half_col * (n // 2), 128), n // 2)
        return held(k).at[pl.ds(pl.multiple_of(row, 16), rows), pl.ds(col, cols)]

    planes = (z, zn, z_a, z_b)
    kinds = len(PIECES)
    local = []

    def stage0(k):
        go(remote(own(k, 1 - tower, None, c), full(k, z, x, None, c), far_s.at[k], z_r.at[k, 2 - inner], to_far))
        go(remote(own(k, tower, y, c), full(k, z, x, y, c), near_s.at[k], z_r.at[k, 0], to_near))
        go(remote(own(k, tower, None, c), full(k, z, x, None, c), x_s.at[k, 0], x_r.at[k, 0], to_x))
        copy = pltpu.make_async_copy(own(k, tower, None, c), full(k, z, x, None, c), ld.at[k])
        copy.start()
        local.append(copy)

    def stage1(k):
        ref = full(k, zn, x, y, c)
        arrived(ref, near_s.at[k], z_r.at[k, 0])
        go(remote(ref, ref, x_s.at[k, 1], x_r.at[k, 1], to_x))
        go(remote(ref, ref, y_s.at[k, 0], y_r.at[k, 0], to_y))
        for j, zz in ((1, z_a), (2, z_b)):
            whole = full(k, zz, x, None, c)
            arrived(whole, near_s.at[k], z_r.at[k, j])

            @pl.when(inner == 1)
            def _():
                remote(whole, whole, rel_s.at[k, j - 1], z_r.at[k, j], to_near).start()

            ref = full(k, zz, x, y, c)
            go(remote(ref, ref, x_s.at[k, 1 + j], x_r.at[k, 1 + j], to_x))

    def stage2(k):
        arrived(full(k, z, 1 - x, None, c), x_s.at[k, 0], x_r.at[k, 0])
        for j in (1, 2, 3):
            ref = full(k, planes[j], 1 - x, y, c)
            arrived(ref, x_s.at[k, j], x_r.at[k, j])
            go(remote(ref, ref, y_s.at[k, j], y_r.at[k, j], to_y))

    def stage3(k):
        arrived(full(k, zn, x, 1 - y, c), y_s.at[k, 0], y_r.at[k, 0])
        for j in (1, 2, 3):
            arrived(full(k, planes[j], 1 - x, 1 - y, c), y_s.at[k, j], y_r.at[k, j])
        local[k].wait()
        n = dims(k)[3]
        ref = held(k).at[:, pl.ds(pl.multiple_of(c * (n // 2), 128), n // 2)]
        go(remote(ref, ref, c_s.at[k], c_r.at[k], to_core))

    def stage4(k):
        n = dims(k)[3]
        ref = held(k).at[:, pl.ds(pl.multiple_of((1 - c) * (n // 2), 128), n // 2)]
        arrived(ref, c_s.at[k], c_r.at[k])

    def sv_copy(i):
        there = lax.rem(place + i, 8)
        return remote(sv_ref.at[there // 4], sv_all.at[place], sv_sem.at[i], sv_r.at[i], (there, other))

    WINDOW = 2
    for k in range(WINDOW):
        stage0(k)
    for i in range(1, 8):
        sv_copy(i).start()
    sv_all[place] = sv_ref[tower]

    sel_row, sel_col = iota((D, 1024), 0), iota((D, 1024), 1)
    lane = sel_col % 128
    sel_s[...] = jnp.where((sel_row == (sel_col // 128) * 96 + lane) & (lane < 96), 1.0, 0.0).astype(BF)
    segments = seg_ref[...]
    level = iota((ROW, row_len), 0)
    begin = jnp.sum(jnp.where(segments < level, 1.0, 0.0), axis=1, keepdims=True).astype(jnp.int32)
    spot = jnp.where((iota((ROW, row_len), 1) == begin) & (level < SEGS), 1.0, 0.0).astype(BF)
    belongs = jnp.where((segments == level) & (level < SEGS), 1.0, 0.0).astype(BF)
    mask_s[...] = (dot_over_rows(belongs, belongs) - 1.0) * -masked_score
    wide_row, wide_col = iota((48, D), 0), iota((48, D), 1)
    own_head = (wide_row // SEGS) == (wide_col // HEAD_DIM)
    repeat = jnp.where(iota((48, ROW), 0) % SEGS == iota((48, ROW), 1), 1.0, 0.0).astype(BF)
    open_keys = (iota((48, row_len), 0) % SEGS) == segments
    row16 = iota((ROW, D), 0)
    x_r_rows = dot_plain(spot, x_ref[...])
    x_low = x_r_rows.astype(BF)

    def widen(rows):
        return jnp.where(own_head, dot_plain(repeat, rows), 0.0)

    def narrow(wide):
        return dot_over_rows(repeat, jnp.where(own_head, wide, 0.0).astype(BF))

    state = {}

    def small_vectors():
        for i in range(1, 8):
            sv_copy(i).wait_recv()
        rows = jnp.zeros((ROW, D), F32)
        for m in range(8):
            put = jnp.where((iota((128, D), 1) == iota((128, D), 0) + 96 * m) & (iota((128, D), 0) < 96), 1.0, 0.0)
            rows = rows + dot_plain(sv_all[m][:, :128], put.astype(BF))
        names = ("bq", "bv", "bo", "o1", "bd", "o2", "g1", "g2")
        for i, name in enumerate(names):
            state[name] = rows[1 + i : 2 + i, :]
        state["cu"] = [
            jnp.concatenate([sv_all[2 * j][0:1, :], sv_all[2 * j + 1][0:1, :]], axis=1).astype(F32) for j in range(4)
        ]

    def mix(k, out, bias, factor):
        for n in range(0, D, BLOCK):
            m = dot_plain(x_ref[...], wa[k, :, n : n + BLOCK])
            if bias is not None:
                m = m + state[bias][:, n : n + BLOCK]
            m = m.astype(BF)
            if factor is not None:
                m = m * jnp.asarray(factor, BF)
            out[:, n : n + BLOCK] = m

    def attend(low, high):
        rows = 256
        per = row_len // rows

        def body(i, carry):
            pair, part = i // per, lax.rem(i, per)
            cols = pl.ds(pl.multiple_of(pair * 128, 128), 128)
            at = pl.ds(pl.multiple_of(part * rows, rows), rows)
            qp, kp, vp = q_s[at, cols], k_s[:, cols], v_s[:, cols]
            left = iota((rows, 128), 1) < HEAD_DIM
            found = []
            for keep in (left, jnp.logical_not(left)):
                s = dot_over_columns(jnp.where(keep, qp, jnp.zeros((), BF)), kp) + mask_s[at, :]
                e = jnp.exp(s - jnp.max(s, axis=1, keepdims=True))
                p = (e * (1.0 / jnp.sum(e, axis=1, keepdims=True))).astype(BF)
                found.append(dot_plain(p, vp))
            a_s[at, cols] = jnp.where(left, found[0], found[1]).astype(BF)
            return carry

        lax.fori_loop(low * per, high * per, body, 0)

    def project():
        for n in range(0, D, BLOCK):
            b_s[:, n : n + BLOCK] = (
                x_ref[:, n : n + BLOCK].astype(F32)
                + dot_plain(a_s[...], wa[3, :, n : n + BLOCK])
                + state["bo"][:, n : n + BLOCK]
            )

        def body(i, carry):
            at = pl.ds(pl.multiple_of(i * 128, 128), 128)
            unit, _ = norm_parts(b_s[at, :])
            h = unit * state["g1"] + state["o1"]
            h_s[at, :] = h
            hl_s[at, :] = h.astype(BF)
            return carry

        lax.fori_loop(0, row_len // 128, body, 0)

    def up(j):
        for n in range(0, D, BLOCK):
            u = dot_plain(hl_s[...], wa[4 + j, :, n : n + BLOCK]) + state["cu"][j][:, n : n + BLOCK]
            g_s[j, :, n : n + BLOCK] = gelu_erf(u).astype(BF)

    def down(j):
        cols = slice(256 * j, 256 * j + 256)
        total = h_s[:, cols] + state["bd"][:, cols]
        for i in range(4):
            total = total + dot_plain(g_s[i], wd[j, D * i : D * i + D, :])
        b_s[:, cols] = total

    def finish():
        def body(i, carry):
            at = pl.ds(pl.multiple_of(i * 128, 128), 128)
            unit, _ = norm_parts(b_s[at, :])
            enc_ref[at, :] = (unit * state["g2"] + state["o2"]).astype(BF)
            return carry

        lax.fori_loop(0, row_len // 128, body, 0)

    def rows_attention():
        q_r = (dot_plain(x_low, wa[2]) + state["bq"]).astype(BF)
        state["q_r"] = q_r
        q_wide = (widen(q_r) * scaled).astype(BF)
        state["q_wide"] = q_wide
        s = jnp.where(open_keys, dot_over_columns(q_wide, k_s[...]), masked_score)
        e = jnp.exp(s - jnp.max(s, axis=1, keepdims=True))
        p = e * (1.0 / jnp.sum(e, axis=1, keepdims=True))
        state["p"] = p
        state["p_low"] = p.astype(BF)
        state["a_r"] = narrow(dot_plain(state["p_low"], v_s[...])).astype(BF)

    def rows_project():
        before = x_r_rows + dot_plain(state["a_r"], wa[3]) + state["bo"]
        unit, inverse = norm_parts(before)
        state["unit1"], state["inv1"] = unit, inverse
        state["h_r"] = unit * state["g1"] + state["o1"]
        state["hl_r"] = state["h_r"].astype(BF)
        state["u_r"], state["g_r"], state["f_r"] = [], [], []

    def rows_up(j):
        u = dot_plain(state["hl_r"], wa[4 + j]) + state["cu"][j]
        state["u_r"].append(u)
        state["g_r"].append(gelu_erf(u).astype(BF))

    def rows_down(j):
        f = jnp.zeros((ROW, 256), F32)
        for i in range(4):
            f = f + dot_plain(state["g_r"][i], wd[j, D * i : D * i + D, :])
        state["f_r"].append(f)

    def rows_finish():
        before = state["h_r"] + jnp.concatenate(state["f_r"], axis=1) + state["bd"]
        unit, inverse = norm_parts(before)
        state["unit2"], state["inv2"] = unit, inverse
        e = (unit * state["g2"] + state["o2"]).astype(BF)
        cls_own[...] = e[:SEGS, :]
        cls_all[me] = e[:SEGS, :]

    after = {
        0: [lambda: small_vectors(), lambda: mix(0, k_s, None, None)],
        1: [lambda: mix(1, v_s, "bv", None)],
        2: [lambda: mix(2, q_s, "bq", scaled), rows_attention, lambda: attend(0, 2)],
        3: [rows_project, lambda: attend(2, 4)],
        4: [lambda: rows_up(0), lambda: attend(4, 6)],
        5: [lambda: rows_up(1), project, lambda: up(0)],
        6: [lambda: rows_up(2), lambda: up(1)],
        7: [lambda: rows_up(3), lambda: up(2)],
        8: [lambda: rows_down(0), lambda: up(3)],
        9: [lambda: rows_down(1), lambda: down(0)],
        10: [lambda: rows_down(2), rows_finish],
    }
    for i in range(kinds + 3):
        if i + WINDOW < kinds:
            stage0(i + WINDOW)
        if i < kinds:
            stage1(i)
        if 0 <= i - 1 < kinds:
            stage2(i - 1)
        if 0 <= i - 2 < kinds:
            stage3(i - 2)
        if 0 <= i - 3 < kinds:
            stage4(i - 3)
            for unit in after[i - 3]:
                unit()

    def cls_copy(i):
        return remote(cls_own, cls_all.at[me], cls_sem.at[i], cls_r.at[i], peer_at(i))

    def cls_send(i, carry):
        cls_copy(i).start()
        return carry

    lax.fori_loop(1, 32, cls_send, 0)

    xf, yf = x + (1 - c) * (1 - 2 * x), y + c * (1 - 2 * y)
    xg, yg = x + c * (1 - 2 * x), y + (1 - c) * (1 - 2 * y)
    to_f, to_g = device(z, xf, yf, c), device(z, xg, yg, c)
    wholes = ((src_q, fq_ref), (src_u, fu_ref), (src_a, fa_ref))
    sliced = ((src_e, se_ref), (src_l, sl_ref))

    def slot(ref):
        return ref.at[tower, c, x, y, zi]

    def whole_z(i):
        src, dst = wholes[i]
        for r in (1, 2, 3):
            go(remote(src, slot(dst), fz_s.at[i, r], fz_r.at[i, r], device(lax.rem(z + r, 4), x, y, c)))
        copy = pltpu.make_async_copy(src, slot(dst), fl.at[i])
        copy.start()
        copy.wait()

    def whole_f(i):
        src, dst = wholes[i]
        for r in (1, 2, 3):
            arrived(slot(dst), fz_s.at[i, r], fz_r.at[i, r])
        ref = dst.at[:, c, x, y]
        go(remote(ref, ref, ff_s.at[i], ff_r.at[i], to_f))
        go(remote(ref, ref, fg_s.at[i, 0], fg_r.at[i, 0], to_g))

    def whole_g(i):
        dst = wholes[i][1]
        ref = dst.at[:, c, xf, yf]
        arrived(ref, ff_s.at[i], ff_r.at[i])
        go(remote(ref, ref, fg_s.at[i, 1], fg_r.at[i, 1], to_g))

    def whole_c(i):
        dst = wholes[i][1]
        for j in (0, 1):
            arrived(dst.at[:, c, xg, yg], fg_s.at[i, j], fg_r.at[i, j])
        ref = dst.at[:, c]
        go(remote(ref, ref, fc_s.at[i], fc_r.at[i], to_core))

    def whole_end(i):
        arrived(wholes[i][1].at[:, c], fc_s.at[i], fc_r.at[i])

    def slice_1(i):
        src, dst = sliced[i]
        for r in range(1, 8):
            there = lax.rem(place + r, 8)
            go(remote(src.at[there], slot(dst), s1_s.at[i, r], s1_r.at[i, r], (there, other)))
        copy = pltpu.make_async_copy(src.at[place], slot(dst), fl.at[3 + i])
        copy.start()
        copy.wait()

    def slice_2(i):
        dst = sliced[i][1]
        for r in range(1, 8):
            arrived(slot(dst), s1_s.at[i, r], s1_r.at[i, r])
        ref = dst.at[:, c, :, y]
        go(remote(ref, ref, s2_s.at[i], s2_r.at[i], to_y))

    def slice_3(i):
        dst = sliced[i][1]
        arrived(dst.at[:, c, :, y], s2_s.at[i], s2_r.at[i])
        ref = dst.at[:, c]
        go(remote(ref, ref, s3_s.at[i], s3_r.at[i], to_core))

    def slice_end(i):
        arrived(sliced[i][1].at[:, c], s3_s.at[i], s3_r.at[i])

    first_rows = row16 < SEGS

    def top(rows):
        return jnp.where(row16[:, : rows.shape[1]] < SEGS, rows, 0.0)

    q_f32 = top(state["q_r"].astype(F32))
    src_q[...] = q_f32.astype(BF)
    whole_z(0)
    hl_f32, a_f32, x_f32 = (top(m.astype(F32)) for m in (state["hl_r"], state["a_r"], x_low))
    four = hl_f32
    for r in (4, 8, 12):
        four = four + pltpu.roll(hl_f32, r, 0)
    pair = pltpu.roll(a_f32, 4, 0) + pltpu.roll(x_f32, 8, 0)
    z_rows = dot_plain(state["p_low"], x_ref[...])
    early = jnp.concatenate([four, pair, z_rows], axis=0).astype(BF)
    early = dot_plain(early, sel_s[...]).astype(BF)
    for d in range(8):
        src_e[d, :80, :] = early[:, 128 * d : 128 * d + 128]
        for b in range(3):
            first = 384 * d + 128 * b
            g = state["g_r"][first // D][:, first % D : first % D + 128]
            src_e[d, 80 + 16 * b : 96 + 16 * b, :] = top(g.astype(F32)).astype(BF)
    slice_1(0)

    down(1)
    down(2)
    finish()

    def cls_wait(i, carry):
        cls_copy(i).wait_recv()
        return carry

    lax.fori_loop(1, 32, cls_wait, 0)
    for i in range(32):
        cls_f[SEGS * i : SEGS * i + SEGS, :] = cls_all[i].astype(F32)
    all_q, all_p = cls_f[:64, :].astype(BF), cls_f[64:, :].astype(BF)
    pair_scale = 2.0 * D ** (-0.5)
    logits = dot_over_columns(all_p, all_q) * pair_scale
    raised = jnp.exp(logits - jnp.max(logits, axis=0, keepdims=True))
    hit = jnp.where(iota((64, 64), 0) == pos_ref[...], 1.0, 0.0)
    d_logits = (raised / jnp.sum(raised, axis=0, keepdims=True) - hit).astype(BF)
    position = me * SEGS - tower * 64
    take = jnp.where((iota((ROW, 64), 1) == iota((ROW, 64), 0) + position) & (iota((ROW, 64), 0) < SEGS), 1.0, 0.0)
    take = take.astype(BF)
    d_q = dot_plain(dot_over_columns(take, d_logits).astype(BF), all_p)
    d_p = dot_plain(dot_plain(take, d_logits).astype(BF), all_q)
    d_cls = jnp.where(tower == 0, d_q, d_p) * pair_scale

    def total(rows):
        return jnp.sum(rows, axis=0, keepdims=True)

    vec_g2, vec_o2 = total(d_cls * state["unit2"]), total(d_cls)
    dz2 = norm_back(state["unit2"], state["inv2"], state["g2"], d_cls)
    df = dz2.astype(BF)
    whole_f(0)
    dh = dz2
    du_rows = []
    for j in range(4):
        dg = jnp.zeros((ROW, D), F32)
        for i in range(3):
            dg = dg + dot_over_columns(df[:, 256 * i : 256 * i + 256], wd[i, D * j : D * j + D, :])
        du = (dg * gelu_slope(state["u_r"][j])).astype(BF)
        du_rows.append(du.astype(F32))
    packed = du_rows[0]
    for j in (1, 2, 3):
        packed = packed + pltpu.roll(du_rows[j], 4 * j, 0)
    src_u[...] = packed.astype(BF)
    whole_z(1)
    slice_2(0)
    whole_g(0)
    for j in range(4):
        dh = dh + dot_over_columns(du_rows[j].astype(BF), wa[4 + j])
    vec_g1, vec_o1 = total(dh * state["unit1"]), total(dh)
    dz1 = norm_back(state["unit1"], state["inv1"], state["g1"], dh)
    db = dz1.astype(BF)
    whole_f(1)
    slice_3(0)
    whole_c(0)
    da = dot_over_columns(db, wa[3]).astype(BF)
    a_wide = widen(da).astype(BF)
    d_p_rows = dot_over_columns(a_wide, v_s[...])
    p = state["p"]
    ds = (p * (d_p_rows - jnp.sum(p * d_p_rows, axis=1, keepdims=True))).astype(BF)
    dq = narrow(dot_plain(ds, k_s[...]) * scaled).astype(BF)
    df_f, db_f, da_f, dq_f = (m.astype(F32) for m in (df, db, da, dq))
    src_a[...] = (df_f + pltpu.roll(db_f, 4, 0) + pltpu.roll(dq_f, 8, 0) + pltpu.roll(da_f, 12, 0)).astype(BF)
    whole_z(2)
    whole_g(1)
    y_rows = dot_plain(ds, x_ref[...]) * scaled
    weight_sum = jnp.sum(state["p_low"].astype(F32), axis=1, keepdims=True)
    vec_bv = total(weight_sum * a_wide.astype(F32))
    vectors = jnp.concatenate(
        [total(dq_f), vec_bv, total(db_f), vec_o1, total(df_f), vec_o2, vec_g1, vec_g2, jnp.zeros((8, D), F32)], axis=0
    )
    late = jnp.concatenate([y_rows, vectors], axis=0).astype(BF)
    late = dot_plain(late, sel_s[...]).astype(BF)
    for d in range(8):
        src_l[d] = late[:, 128 * d : 128 * d + 128]
    slice_1(1)
    whole_f(2)
    whole_c(1)

    t_k = dot_over_columns(state["q_wide"], wa[0]).astype(BF)
    t_v = dot_over_columns(a_wide, wa[1]).astype(BF)
    at_rows = dz1 + dot_over_columns(dq, wa[2])
    high = at_rows.astype(BF)
    rest = (at_rows - high.astype(F32)).astype(BF)
    left = jnp.concatenate([ds, state["p_low"], spot, spot], axis=0)
    right = jnp.concatenate([t_k, t_v, high, rest], axis=0)
    whole_g(2)
    slice_2(1)
    for n in range(0, D, BLOCK):
        drow_ref[:, n : n + BLOCK] = dot_over_rows(left, right[:, n : n + BLOCK])
    whole_c(2)
    slice_3(1)
    for i in range(3):
        whole_end(i)
    for i in range(2):
        slice_end(i)

    for copy in sent:
        copy.wait_send()
    for k in range(kinds):

        @pl.when(inner == 1)
        def _():
            for j, zz in ((1, z_a), (2, z_b)):
                ref = full(k, zz, x, None, c)
                remote(ref, ref, rel_s.at[k, j - 1], z_r.at[k, j], to_near).wait_send()

    for i in range(1, 8):
        sv_copy(i).wait_send()

    def cls_sent(i, carry):
        cls_copy(i).wait_send()
        return carry

    lax.fori_loop(1, 32, cls_sent, 0)


def grads_kernel(fq_ref, fu_ref, fa_ref, se_ref, sl_ref, mix_ref, proj_ref, up_ref, down_ref, upb_ref, rowb_ref, gain_ref):
    place = lax.axis_index("dp")
    kind = iota((256, 128), 0) % ROW
    part = 96
    pick = iota((192, 64), 0)
    group, within = pick // 48, pick % SEGS
    head_row, head_col = iota((192, D), 0), iota((192, D), 1)
    own_head = (head_row % 48) // SEGS == head_col // HEAD_DIM
    take_q = jnp.where(iota((192, 64), 1) == group * ROW + within, 1.0, 0.0).astype(BF)
    take_a = jnp.where(iota((192, 64), 1) == group * ROW + within + 12, 1.0, 0.0).astype(BF)
    kind16, col16 = iota((256, ROW), 0) % ROW, iota((256, ROW), 1)
    biases = jnp.zeros((128, ROW), F32)
    gains = jnp.zeros((128, ROW), F32)
    up_bias = jnp.zeros((384, ROW), F32)
    for t in range(2):
        def keep(ref_rows, lo, hi):
            return jnp.where((kind >= lo) & (kind < hi), ref_rows, jnp.zeros((), BF))

        four = se_ref[t, :, 0:16, :].reshape(256, 128)
        two = se_ref[t, :, 16:32, :].reshape(256, 128)
        fa, fu = fa_ref[t], fu_ref[t]
        mix_ref[:, 3 * D * t : 3 * D * t + D] = dot_over_rows(keep(two, 8, 12), fa)[:part]
        proj_ref[:, D * t : D * t + D] = dot_over_rows(keep(two, 4, 8), fa)[:part]
        for j in range(4):
            first = FF * t + D * j
            up_ref[:, first : first + D] = dot_over_rows(keep(four, 4 * j, 4 * j + 4), fu)[:part]
        for b in range(3):
            g = se_ref[t, :, 80 + 16 * b : 96 + 16 * b, :].reshape(256, 128)
            down_ref[128 * b : 128 * b + 128, D * t : D * t + D] = dot_over_rows(g, fa)
        gk = jnp.zeros((128, D), F32)
        gv = jnp.zeros((128, D), F32)
        for s in range(4):
            q_wide = jnp.where(own_head, dot_plain(take_q, fq_ref[t, 64 * s : 64 * s + 64, :]), 0.0).astype(BF)
            a_wide = jnp.where(own_head, dot_plain(take_a, fa[64 * s : 64 * s + 64, :]), 0.0).astype(BF)
            y = sl_ref[t, 4 * s : 4 * s + 4, 0:48, :].reshape(192, 128)
            z = se_ref[t, 4 * s : 4 * s + 4, 32:80, :].reshape(192, 128)
            gk = gk + dot_over_rows(y, q_wide)
            gv = gv + dot_over_rows(z, a_wide)
        mix_ref[:, 3 * D * t + D : 3 * D * t + 2 * D] = gk[:part]
        mix_ref[:, 3 * D * t + 2 * D : 3 * D * t + 3 * D] = gv[:part]
        vec = sl_ref[t, :, 48:64, :].reshape(256, 128)
        to_bias = jnp.where((kind16 < 6) & (col16 == kind16 + 6 * t), 1.0, 0.0).astype(BF)
        to_gain = jnp.where((kind16 >= 6) & (kind16 < 8) & (col16 == kind16 - 6 + 2 * t), 1.0, 0.0).astype(BF)
        biases = biases + dot_over_rows(vec, to_bias)
        gains = gains + dot_over_rows(vec, to_gain)
        mine = fu_ref[t, :, pl.ds(pl.multiple_of(place % 2 * 384, 128), 384)]
        to_up = jnp.where((kind16 // 4 == place // 2) & (col16 == t), 1.0, 0.0).astype(BF)
        up_bias = up_bias + dot_over_rows(mine, to_up)
    rowb_ref[...] = biases[:part, :12]
    gain_ref[...] = gains[:part, :4]
    upb_ref[...] = up_bias[:, :2]


def fast_device(text_rows, text_segments, positives, w_mix, w_proj, w_up, w_down, b_up, b_rows, g_rows):
    sem = pltpu.SemaphoreType.DMA
    vm = pltpu.VMEM
    part = b_rows.shape[0]
    towers = []
    for t in range(2):
        narrow = jnp.concatenate([b_rows[:, 6 * t : 6 * t + 6], g_rows[:, 2 * t : 2 * t + 2]], axis=1).T
        narrow = jnp.pad(narrow, ((0, 7), (0, 4 * part - part)))
        towers.append(jnp.concatenate([b_up[:, t][None, :], narrow], axis=0))
    small = jnp.stack(towers)
    kinds = len(PIECES)
    fulls = jax.ShapeDtypeStruct((2, 2, 2, 2, 2, ROW, D), BF)
    row_len = text_rows.shape[1]
    here, there = pl.BlockSpec(memory_space=vm), pl.BlockSpec(memory_space=pl.ANY)
    encoded, d_rows, fq, fu, fa, se, sl = pl.pallas_call(
        main_kernel,
        out_shape=[
            jax.ShapeDtypeStruct((row_len, D), BF),
            jax.ShapeDtypeStruct((row_len, D), F32),
            fulls, fulls, fulls,
            jax.ShapeDtypeStruct((2, 2, 2, 2, 2, 128, 128), BF),
            jax.ShapeDtypeStruct((2, 2, 2, 2, 2, 64, 128), BF),
        ],
        in_specs=[here] * 4 + [there] * 4,
        out_specs=[here] * 2 + [there] * 5,
        scratch_shapes=[
            vm((8, D, D), BF), vm((3, FF, 256), BF), vm((8, ROW, 384), BF),
            vm((row_len, D), BF), vm((row_len, D), BF), vm((row_len, D), BF), vm((row_len, D), BF),
            vm((row_len, row_len), F32), vm((row_len, D), F32), vm((row_len, D), F32), vm((row_len, D), BF),
            vm((4, row_len, D), BF), vm((D, 1024), BF),
            vm((SEGS, D), BF), vm((32, SEGS, D), BF), vm((128, D), F32),
            vm((ROW, D), BF), vm((ROW, D), BF), vm((ROW, D), BF), vm((8, 128, 128), BF), vm((8, 64, 128), BF),
            sem((kinds,)), sem((kinds,)), sem((kinds,)), sem((kinds, 3)), sem((kinds, 2)),
            sem((kinds, 4)), sem((kinds, 4)), sem((kinds, 4)), sem((kinds, 4)), sem((kinds,)), sem((kinds,)),
            sem((8,)), sem((8,)), sem((32,)), sem((32,)),
            sem((5,)), sem((3, 4)), sem((3, 4)), sem((3,)), sem((3,)), sem((3, 2)), sem((3, 2)), sem((3,)), sem((3,)),
            sem((2, 8)), sem((2, 8)), sem((2,)), sem((2,)), sem((2,)), sem((2,)),
        ],
        compiler_params=pltpu.CompilerParams(collective_id=5, has_side_effects=True, vmem_limit_bytes=60 << 20),
        name="main_step",
    )(text_rows[0], text_segments, positives[None, :], small, w_mix, w_proj, w_up, w_down)
    shape = lambda r, n: jax.ShapeDtypeStruct((r, n), F32)
    grads = pl.pallas_call(
        grads_kernel,
        out_shape=[
            shape(part, 6 * D), shape(part, 2 * D), shape(part, 2 * FF), shape(4 * part, 2 * D),
            shape(4 * part, 2), shape(part, 12), shape(part, 4),
        ],
        in_specs=[here] * 5,
        out_specs=[here] * 7,
        compiler_params=pltpu.CompilerParams(vmem_limit_bytes=60 << 20),
        name="weight_grads",
    )(
        fq.reshape(2, 256, D), fu.reshape(2, 256, D), fa.reshape(2, 256, D),
        se.reshape(2, 16, 128, 128), sl.reshape(2, 16, 64, 128),
    )
    return (encoded[None], d_rows[None], *grads)


def solution(mesh):
    rows, cols = P(("dp", "outer"), None, None), P("dp", None)
    sizes = (mesh.shape["dp"], mesh.shape["outer"])
    return jax.shard_map(
        fast_device if sizes == (8, 4) else per_device,
        mesh=mesh,
        in_specs=(rows, P(("dp", "outer"), None), P(), cols, cols, cols, cols, cols, cols, cols),
        out_specs=(rows, rows, cols, cols, cols, cols, cols, cols, cols),
        check_vma=False,
    )
```

```python
import functools

import jax
import jax.numpy as jnp
from jax import lax
from jax.experimental import pallas as pl
from jax.experimental.pallas import tpu as pltpu
from jax.sharding import PartitionSpec as P

D = 768
HEADS = 12
HEAD_DIM = 64
FF = 3072
SEGS = 4
BF = jnp.bfloat16
F32 = jnp.float32
MESH = pl.DeviceIdType.MESH

masked_score = -1e30
layer_eps = 1e-05


def dot_plain(left, right):
    return jnp.dot(left, right, preferred_element_type=F32)


def dot_over_rows(left, right):
    return lax.dot_general(left, right, (((0,), (0,)), ((), ())), preferred_element_type=F32)


def dot_over_columns(left, right):
    return lax.dot_general(left, right, (((1,), (1,)), ((), ())), preferred_element_type=F32)


def gelu_exact(inputs):
    return jax.nn.gelu(inputs, approximate=False)


def norm_parts(inputs):
    center = inputs - jnp.mean(inputs, axis=-1, keepdims=True)
    inverse = lax.rsqrt(jnp.mean(center * center, axis=-1, keepdims=True) + layer_eps)
    return center * inverse, inverse


def norm_back(unit, inverse, gain, grad):
    scaled = gain * grad
    return inverse * (
        scaled
        - jnp.mean(scaled, axis=-1, keepdims=True)
        - unit * jnp.mean(scaled * unit, axis=-1, keepdims=True)
    )


def gather_weights(weights, widths, n_dp):
    tower = lax.axis_index("dp") * 2 // n_dp
    whole = [lax.all_gather(w, "dp", axis=0, tiled=True) for w in weights]
    return [lax.dynamic_slice_in_dim(w, tower * n, n, 1) for w, n in zip(whole, widths)]


def spread_kernel(n_outer, total, whole_ref, parts_ref, all_ref, sliced_ref, local, s_one, r_one, s_two, r_two):
    dp, outer = lax.axis_index("dp"), lax.axis_index("outer")
    me = dp * n_outer + outer
    barrier = pltpu.get_barrier_semaphore()

    def greet(i, carry):
        peer = lax.rem(me + i, total)
        pl.semaphore_signal(barrier, inc=1, device_id=(peer // n_outer, lax.rem(peer, n_outer)), device_id_type=MESH)
        return carry

    lax.fori_loop(1, total, greet, 0)
    pl.semaphore_wait(barrier, total - 1)

    def copies(i):
        peer = lax.rem(me + i, total)
        there = peer // n_outer
        device = (there, lax.rem(peer, n_outer))
        one = pltpu.make_async_remote_copy(
            src_ref=whole_ref, dst_ref=all_ref.at[me], send_sem=s_one.at[i], recv_sem=r_one.at[i],
            device_id=device, device_id_type=MESH,
        )
        if parts_ref is None:
            return (one,)
        two = pltpu.make_async_remote_copy(
            src_ref=parts_ref.at[there], dst_ref=sliced_ref.at[me], send_sem=s_two.at[i], recv_sem=r_two.at[i],
            device_id=device, device_id_type=MESH,
        )
        return (one, two)

    def send(i, carry):
        for copy in copies(i):
            copy.start()
        return carry

    lax.fori_loop(1, total, send, 0)
    own = [pltpu.make_async_copy(whole_ref, all_ref.at[me], local.at[0])]
    if parts_ref is not None:
        own.append(pltpu.make_async_copy(parts_ref.at[dp], sliced_ref.at[me], local.at[1]))
    for copy in own:
        copy.start()

    def settle(i, carry):
        for copy in copies(i):
            copy.wait()
        return carry

    lax.fori_loop(1, total, settle, 0)
    for copy in own:
        copy.wait()


def spread(whole, parts, n_dp, n_outer, identity):
    total = n_dp * n_outer
    sem = pltpu.SemaphoreType.DMA
    out_shape = [jax.ShapeDtypeStruct((total,) + whole.shape, whole.dtype)]
    operands = [whole]
    if parts is not None:
        out_shape.append(jax.ShapeDtypeStruct((total,) + parts.shape[1:], parts.dtype))
        operands.append(parts)
        kernel = functools.partial(spread_kernel, n_outer, total)
        scratch = [sem((2,))] + [sem((total,))] * 4
    else:
        def kernel(w, a, local, s, r):
            spread_kernel(n_outer, total, w, None, a, None, local, s, r, None, None)
        scratch = [sem((2,))] + [sem((total,))] * 2
    return pl.pallas_call(
        kernel,
        out_shape=out_shape,
        in_specs=[pl.BlockSpec(memory_space=pltpu.VMEM)] * len(operands),
        out_specs=[pl.BlockSpec(memory_space=pltpu.VMEM)] * len(out_shape),
        scratch_shapes=scratch,
        compiler_params=pltpu.CompilerParams(
            collective_id=identity, has_side_effects=True, vmem_limit_bytes=48 << 20
        ),
        name="spread%d" % identity,
    )(*operands)


def expand_heads(rows):
    head_of = jnp.arange(D, dtype=jnp.int32) // HEAD_DIM
    keep = head_of[None, :] == jnp.arange(HEADS, dtype=jnp.int32)[:, None]
    return jnp.where(keep[:, None, :], rows[None], 0).reshape(HEADS * rows.shape[0], D)


def per_device(text_rows, text_segments, positives, w_mix, w_proj, w_up, w_down, b_up, b_rows, g_rows):
    n_dp, n_outer = lax.axis_size("dp"), lax.axis_size("outer")
    total = n_dp * n_outer
    own_index = lax.axis_index(("dp", "outer"))
    tower = own_index * 2 // total
    rows_in, segments = text_rows[0], text_segments[0]
    row_len = rows_in.shape[0]
    widths = (3 * D, D, FF, D)
    wm, wp, wu, wd = gather_weights((w_mix, w_proj, w_up, w_down), widths, n_dp)
    part_f, part_d = b_up.shape[0], b_rows.shape[0]
    small = jnp.concatenate([b_up.reshape(part_f // part_d, part_d, 2).transpose(0, 2, 1).reshape(-1, part_d), b_rows.T, g_rows.T], axis=0)
    small = lax.all_gather(small, "dp", axis=0)
    split = 2 * (part_f // part_d)
    up_b = small[:, :split].reshape(n_dp, part_f // part_d, 2, part_d).transpose(2, 0, 1, 3).reshape(2, FF)
    row_b = small[:, split : split + 12].transpose(1, 0, 2).reshape(2, 6, D)
    gain_b = small[:, split + 12 :].transpose(1, 0, 2).reshape(2, 2, D)
    pick = lambda both_towers: jnp.where(tower == 0, both_towers[0], both_towers[1]).astype(F32)
    c_up, biases, gains = pick(up_b), pick(row_b), pick(gain_b)
    bq, bv, bo, o1, bd, o2 = (biases[i] for i in range(6))
    g1, g2 = gains[0], gains[1]

    scaled = HEAD_DIM ** (-0.5)
    mixed = (dot_plain(rows_in, wm) + jnp.concatenate([bq, jnp.zeros_like(bq), bv])).astype(BF)
    q, k, v = mixed[:, :D], mixed[:, D : 2 * D], mixed[:, 2 * D :]
    allowed = segments[:, None] == segments[None, :]
    heads = lambda m: m.reshape(row_len, HEADS, HEAD_DIM)
    scores = jnp.einsum("qhe,khe->hqk", heads(q), heads(k), preferred_element_type=F32) * scaled
    scores = jnp.where(allowed[None], scores, masked_score)
    top = jnp.max(scores, axis=-1, keepdims=True)
    raised = jnp.exp(scores - top)
    chances = (raised / jnp.sum(raised, axis=-1, keepdims=True)).astype(BF)
    attended = jnp.einsum("hqk,khe->qhe", chances, heads(v), preferred_element_type=F32).reshape(row_len, D).astype(BF)
    before_one = rows_in.astype(F32) + dot_plain(attended, wp) + bo
    unit_one, inv_one = norm_parts(before_one)
    h1 = unit_one * g1 + o1
    h1_low = h1.astype(BF)
    up_pre = dot_plain(h1_low, wu) + c_up
    gelu_low = gelu_exact(up_pre).astype(BF)
    before_two = h1 + dot_plain(gelu_low, wd) + bd
    unit_two, inv_two = norm_parts(before_two)
    encoded = unit_two * g2 + o2

    levels = jnp.arange(SEGS, dtype=jnp.int32)
    starts = jnp.sum((segments[None, :] < levels[:, None]).astype(jnp.int32), axis=1)
    at = lambda m: jnp.take(m, starts, axis=0)
    vectors = at(encoded).astype(BF)
    all_cls = spread(vectors, None, n_dp, n_outer, 2)[0].reshape(total * SEGS, D)
    texts = total * SEGS // 2
    all_q, all_p = all_cls[:texts], all_cls[texts:]
    pair_scale = 2.0 * D ** (-0.5)
    logits = dot_over_columns(all_q, all_p) * pair_scale
    raised_l = jnp.exp(logits - jnp.max(logits, axis=1, keepdims=True))
    hit = (positives[:, None] == jnp.arange(texts, dtype=jnp.int32)[None, :]).astype(F32)
    d_logits = (raised_l / jnp.sum(raised_l, axis=1, keepdims=True) - hit).astype(BF)
    position = own_index * SEGS - tower * texts
    d_q = dot_plain(lax.dynamic_slice_in_dim(d_logits, position, SEGS, 0), all_p)
    d_p = dot_over_rows(lax.dynamic_slice_in_dim(d_logits, position, SEGS, 1), all_q)
    d_cls = jnp.where(tower == 0, d_q, d_p) * pair_scale

    ut, it = at(unit_two), at(inv_two)
    dg2, do2 = jnp.sum(d_cls * ut, axis=0), jnp.sum(d_cls, axis=0)
    dz2 = norm_back(ut, it, g2, d_cls)
    df = dz2.astype(BF)
    dg = dot_over_columns(df, wd)
    u_r = at(up_pre)
    _, gelu_back = jax.vjp(gelu_exact, u_r)
    du = gelu_back(dg)[0].astype(BF)
    dh1 = dz2 + dot_over_columns(du, wu)
    uo, io = at(unit_one), at(inv_one)
    dg1, do1 = jnp.sum(dh1 * uo, axis=0), jnp.sum(dh1, axis=0)
    dz1 = norm_back(uo, io, g1, dh1)
    db = dz1.astype(BF)
    da = dot_over_columns(db, wp).astype(BF)
    q_r = at(q)
    q_wide, a_wide = expand_heads(q_r), expand_heads(da)
    own_segment = jnp.tile(levels, HEADS)
    open_keys = own_segment[:, None] == segments[None, :]
    s_r = jnp.where(open_keys, dot_over_columns(q_wide, k) * scaled, masked_score)
    e_r = jnp.exp(s_r - jnp.max(s_r, axis=-1, keepdims=True))
    p_r = e_r / jnp.sum(e_r, axis=-1, keepdims=True)
    pl_r = p_r.astype(BF)
    dp_r = dot_over_columns(a_wide, v)
    ds_r = (p_r * (dp_r - jnp.sum(p_r * dp_r, axis=-1, keepdims=True))).astype(BF)
    dq_wide = dot_plain(ds_r, k).reshape(HEADS, SEGS, HEADS, HEAD_DIM)
    dq = (jnp.einsum("hshe->she", dq_wide).reshape(SEGS, D) * scaled).astype(BF)
    y_r = (dot_plain(ds_r, rows_in) * scaled).astype(BF)
    z_r = dot_plain(pl_r, rows_in).astype(BF)
    weight_sum = jnp.sum(pl_r.astype(F32), axis=1, keepdims=True)
    dbv = jnp.sum(weight_sum * a_wide.astype(F32), axis=0)
    t_k = (dot_over_columns(q_wide, wm[:, D : 2 * D]) * scaled).astype(BF)
    t_v = dot_over_columns(a_wide, wm[:, 2 * D :]).astype(BF)
    d_rows = dot_over_rows(jnp.concatenate([ds_r, pl_r], axis=0), jnp.concatenate([t_k, t_v], axis=0))
    d_rows_at = dz1 + dot_over_columns(dq, wm[:, :D])
    spot = (starts[:, None] == jnp.arange(row_len, dtype=jnp.int32)[None, :])
    for s in range(SEGS):
        d_rows = d_rows + jnp.where(spot[s][:, None], d_rows_at[s][None, :], 0.0)

    ff_rows = SEGS * FF // D
    whole = jnp.concatenate(
        [df, db, dq, q_r, da, du.reshape(ff_rows, D), jnp.stack([dbv, do1, do2, dg1, dg2]).astype(BF), jnp.zeros((3, D), BF)],
        axis=0,
    )
    g_r, h_r, at_r, x_r = at(gelu_low), at(h1_low), at(attended), at(rows_in)
    by_part = lambda m: m.reshape(m.shape[0], n_dp, m.shape[1] // n_dp).transpose(1, 0, 2)
    parts = jnp.concatenate(
        [by_part(h_r), by_part(at_r), by_part(x_r), by_part(y_r), by_part(z_r),
         by_part(g_r).reshape(n_dp, -1, part_d)],
        axis=1,
    )
    all_w, all_s = spread(whole, parts, n_dp, n_outer, 3)
    half = total // 2
    tw = all_w.reshape(2, half, -1, D)
    ts = all_s.reshape(2, half, -1, part_d)
    rank = lambda m: m.reshape(half * SEGS, -1)
    grads = []
    outs = [[], [], [], []]
    vec_b, vec_g, vec_u = [], [], []
    mine = lax.axis_index("dp")
    for t in range(2):
        w, s = tw[t], ts[t]
        df_a, db_a, dq_a, q_a, da_a = (rank(w[:, 4 * i : 4 * i + 4]) for i in range(5))
        du_a = w[:, 20 : 20 + ff_rows].reshape(half * SEGS, FF)
        vec = jnp.sum(w[:, 20 + ff_rows : 25 + ff_rows].astype(F32), axis=0)
        h_a, at_a, x_a = (rank(s[:, 4 * i : 4 * i + 4]) for i in range(3))
        y_a = s[:, 12:60].reshape(half, HEADS, SEGS, part_d)
        z_a = s[:, 60:108].reshape(half, HEADS, SEGS, part_d)
        g_a = s[:, 108:].reshape(half * SEGS, part_f)
        by_head = lambda m: m.reshape(half, SEGS, HEADS, HEAD_DIM)
        gk = jnp.einsum("rhsa,rshe->ahe", y_a, by_head(q_a), preferred_element_type=F32).reshape(part_d, D)
        gv = jnp.einsum("rhsa,rshe->ahe", z_a, by_head(da_a), preferred_element_type=F32).reshape(part_d, D)
        outs[0] += [dot_over_rows(x_a, dq_a), gk, gv]
        outs[1].append(dot_over_rows(at_a, db_a))
        outs[2].append(dot_over_rows(h_a, du_a))
        outs[3].append(dot_over_rows(g_a, df_a))
        col = lambda m, n: lax.dynamic_slice_in_dim(m, mine * n, n, 0)
        summed = lambda m: jnp.sum(m.astype(F32), axis=0)
        vec_b += [col(m, part_d) for m in (summed(dq_a), vec[0], summed(db_a), vec[1], summed(df_a), vec[2])]
        vec_g += [col(m, part_d) for m in (vec[3], vec[4])]
        vec_u.append(col(summed(du_a), part_f))
    return (
        encoded.astype(BF)[None],
        d_rows[None],
        jnp.concatenate(outs[0], axis=1),
        jnp.concatenate(outs[1], axis=1),
        jnp.concatenate(outs[2], axis=1),
        jnp.concatenate(outs[3], axis=1),
        jnp.stack(vec_u, axis=1),
        jnp.stack(vec_b, axis=1),
        jnp.stack(vec_g, axis=1),
    )


PIECES = (
    [(0, D, D), (0, 2 * D, D), (0, 0, D), (1, 0, D)]
    + [(2, D * i, D) for i in range(4)]
    + [(3, 256 * i, 256) for i in range(3)]
)
WIDTHS = (3 * D, D, FF, D)
ROW = 16
BLOCK = 256


def iota(shape, dim):
    return lax.broadcasted_iota(jnp.int32, shape, dim)


def gelu_erf(u):
    return 0.5 * u * (1.0 + lax.erf(u * 0.7071067811865476))


def gelu_slope(u):
    return 0.5 * (1.0 + lax.erf(u * 0.7071067811865476)) + u * (0.3989422804014327 * jnp.exp(-0.5 * u * u))


def main_kernel(
    x_ref, seg_ref, pos_ref, bu_ref, br_ref, gr_ref, w_mix, w_proj, w_up, w_down,
    enc_out, drow_out, fq_ref, fu_ref, fa_ref, se_ref, sg_ref, sl_ref,
    enc_ref, drow_ref, wa, wd, sv_f, sv_ref, sv_all, q_s, k_s, v_s, a_s, mask_s, b_s, h_s, hl_s, g_s, sel_s,
    cls_own, cls_all, cls_f, src_q, src_u, src_a, src_e, src_g, src_l,
    ld, far_s, near_s, z_r, rel_s, x_s, x_r, y_s, y_r, c_s, c_r, sv_sem, sv_r, cz_s, cz_r, cp_s, cp_r, done,
    fl, fz_s, fz_r, ff_s, ff_r, fg_s, fg_r, fc_s, fc_r, s1_s, s1_r, s2_s, s2_r, s3_s, s3_r,
):
    sources = (w_mix, w_proj, w_up, w_down)
    place, other = lax.axis_index("dp"), lax.axis_index("outer")
    z, x = place // 2, place % 2
    y, c = other // 2, other % 2
    tower, zi = z // 2, z % 2
    me = place * 4 + other
    inner = zi * (1 - tower) + (1 - zi) * tower
    zn = z + 1 - 2 * zi
    z_a, z_b = 2 - tower, 3 - 3 * tower
    scaled = HEAD_DIM ** (-0.5)
    row_len = x_ref.shape[0]

    def device(zz, xx, yy, cc):
        return (zz * 2 + xx, yy * 2 + cc)

    plane = x * 4 + other
    to_near, to_far = device(zn, x, y, c), device(z_a, x, y, c)
    to_x, to_y, to_core = device(z, 1 - x, y, c), device(z, x, 1 - y, c), device(z, x, y, 1 - c)

    barrier = pltpu.get_barrier_semaphore()

    def peer_at(i):
        p = lax.rem(me + i, 32)
        return (p // 4, lax.rem(p, 4))

    def greet(i, carry):
        pl.semaphore_signal(barrier, inc=1, device_id=peer_at(i), device_id_type=MESH)
        return carry

    lax.fori_loop(1, 32, greet, 0)
    pl.semaphore_wait(barrier, 31)

    def remote(src, dst, s, r, peer):
        return pltpu.make_async_remote_copy(
            src_ref=src, dst_ref=dst, send_sem=s, recv_sem=r, device_id=peer, device_id_type=MESH
        )

    def arrived(ref, s, r):
        remote(ref, ref, s, r, to_x).wait_recv()

    sent = []

    def go(copy):
        copy.start()
        sent.append(copy)

    def dims(k):
        tensor, first, cols = PIECES[k]
        return tensor, sources[tensor].shape[0], first, cols

    def own(k, which, half_row, half_col):
        tensor, r, first, n = dims(k)
        row, rows = (0, r) if half_row is None else (half_row * (r // 2), r // 2)
        col, cols = which * WIDTHS[tensor] + first, n
        if half_col is not None:
            col, cols = col + half_col * (n // 2), n // 2
        return sources[tensor].at[
            pl.ds(pl.multiple_of(row, 16), rows), pl.ds(pl.multiple_of(col, 128), cols)
        ]

    def held(k):
        return wa.at[k] if k < 8 else wd.at[k - 8]

    def full(k, zz, xx, half_row, half_col):
        tensor, r, first, n = dims(k)
        row, rows = (zz * 2 + xx) * r, r
        if half_row is not None:
            row, rows = row + half_row * (r // 2), r // 2
        col, cols = (0, n) if half_col is None else (pl.multiple_of(half_col * (n // 2), 128), n // 2)
        return held(k).at[pl.ds(pl.multiple_of(row, 16), rows), pl.ds(col, cols)]

    planes = (z, zn, z_a, z_b)
    kinds = len(PIECES)
    local = []

    def stage0(k):
        go(remote(own(k, 1 - tower, None, c), full(k, z, x, None, c), far_s.at[k], z_r.at[k, 2 - inner], to_far))
        go(remote(own(k, tower, y, c), full(k, z, x, y, c), near_s.at[k], z_r.at[k, 0], to_near))
        go(remote(own(k, tower, None, c), full(k, z, x, None, c), x_s.at[k, 0], x_r.at[k, 0], to_x))
        copy = pltpu.make_async_copy(own(k, tower, None, c), full(k, z, x, None, c), ld.at[k])
        copy.start()
        local.append(copy)

    def stage1(k):
        ref = full(k, zn, x, y, c)
        arrived(ref, near_s.at[k], z_r.at[k, 0])
        go(remote(ref, ref, x_s.at[k, 1], x_r.at[k, 1], to_x))
        go(remote(ref, ref, y_s.at[k, 0], y_r.at[k, 0], to_y))
        for j, zz in ((1, z_a), (2, z_b)):
            whole = full(k, zz, x, None, c)
            arrived(whole, near_s.at[k], z_r.at[k, j])

            @pl.when(inner == 1)
            def _():
                remote(whole, whole, rel_s.at[k, j - 1], z_r.at[k, j], to_near).start()

            ref = full(k, zz, x, y, c)
            go(remote(ref, ref, x_s.at[k, 1 + j], x_r.at[k, 1 + j], to_x))

    def stage2(k):
        arrived(full(k, z, 1 - x, None, c), x_s.at[k, 0], x_r.at[k, 0])
        for j in (1, 2, 3):
            ref = full(k, planes[j], 1 - x, y, c)
            arrived(ref, x_s.at[k, j], x_r.at[k, j])
            go(remote(ref, ref, y_s.at[k, j], y_r.at[k, j], to_y))

    def stage3(k):
        arrived(full(k, zn, x, 1 - y, c), y_s.at[k, 0], y_r.at[k, 0])
        for j in (1, 2, 3):
            arrived(full(k, planes[j], 1 - x, 1 - y, c), y_s.at[k, j], y_r.at[k, j])
        local[k].wait()
        n = dims(k)[3]
        ref = held(k).at[:, pl.ds(pl.multiple_of(c * (n // 2), 128), n // 2)]
        go(remote(ref, ref, c_s.at[k], c_r.at[k], to_core))

    def stage4(k):
        n = dims(k)[3]
        ref = held(k).at[:, pl.ds(pl.multiple_of((1 - c) * (n // 2), 128), n // 2)]
        arrived(ref, c_s.at[k], c_r.at[k])

    def sv_copy(i):
        there = lax.rem(place + i, 8)
        return remote(sv_ref.at[there // 4], sv_all.at[place], sv_sem.at[i], sv_r.at[i], (there, other))

    sv_f[...] = jnp.zeros_like(sv_f)
    for t in range(2):
        sv_f[t, 0:1, :] = bu_ref[...].astype(F32)[t : t + 1]
        sv_f[t, 1:7, 0:96] = br_ref[...].astype(F32)[6 * t : 6 * t + 6]
        sv_f[t, 7:9, 0:96] = gr_ref[...].astype(F32)[2 * t : 2 * t + 2]
    sv_ref[...] = sv_f[...].astype(BF)

    WINDOW = 2
    for k in range(WINDOW):
        stage0(k)
    for i in range(1, 8):
        sv_copy(i).start()
    sv_all[place] = sv_ref[tower]

    sel_row, sel_col = iota((D, 1024), 0), iota((D, 1024), 1)
    lane = sel_col % 128
    sel_s[...] = jnp.where((sel_row == (sel_col // 128) * 96 + lane) & (lane < 96), 1.0, 0.0).astype(BF)
    segments = seg_ref[...]
    level = iota((ROW, row_len), 0)
    begin = jnp.sum(jnp.where(segments < level, 1.0, 0.0), axis=1, keepdims=True).astype(jnp.int32)
    spot = jnp.where((iota((ROW, row_len), 1) == begin) & (level < SEGS), 1.0, 0.0).astype(BF)
    belongs = jnp.where((segments == level) & (level < SEGS), 1.0, 0.0).astype(BF)
    mask_s[...] = (dot_over_rows(belongs, belongs) - 1.0) * -masked_score
    wide_row, wide_col = iota((48, D), 0), iota((48, D), 1)
    own_head = (wide_row // SEGS) == (wide_col // HEAD_DIM)
    repeat = jnp.where(iota((48, ROW), 0) % SEGS == iota((48, ROW), 1), 1.0, 0.0).astype(BF)
    open_keys = (iota((48, row_len), 0) % SEGS) == segments
    x_r_rows = dot_plain(spot, x_ref[...])
    x_low = x_r_rows.astype(BF)

    def widen(rows):
        return jnp.where(own_head, dot_plain(repeat, rows), 0.0)

    def narrow(wide):
        return dot_over_rows(repeat, jnp.where(own_head, wide, 0.0).astype(BF))

    state = {}

    def small_vectors():
        for i in range(1, 8):
            sv_copy(i).wait_recv()
        rows = jnp.zeros((ROW, D), F32)
        for m in range(8):
            put = jnp.where((iota((128, D), 1) == iota((128, D), 0) + 96 * m) & (iota((128, D), 0) < 96), 1.0, 0.0)
            rows = rows + dot_plain(sv_all[m][:, :128], put.astype(BF))
        names = ("bq", "bv", "bo", "o1", "bd", "o2", "g1", "g2")
        for i, name in enumerate(names):
            state[name] = rows[1 + i : 2 + i, :]
        state["cu"] = [
            jnp.concatenate([sv_all[2 * j][0:1, :], sv_all[2 * j + 1][0:1, :]], axis=1).astype(F32) for j in range(4)
        ]

    def mix(k, out, bias, factor):
        for n in range(0, D, BLOCK):
            m = dot_plain(x_ref[...], wa[k, :, n : n + BLOCK])
            if bias is not None:
                m = m + state[bias][:, n : n + BLOCK]
            m = m.astype(BF)
            if factor is not None:
                m = m * jnp.asarray(factor, BF)
            out[:, n : n + BLOCK] = m

    def attend(low, high):
        rows = 256
        per = row_len // rows

        def body(i, carry):
            pair, part = i // per, lax.rem(i, per)
            cols = pl.ds(pl.multiple_of(pair * 128, 128), 128)
            at = pl.ds(pl.multiple_of(part * rows, rows), rows)
            qp, kp, vp = q_s[at, cols], k_s[:, cols], v_s[:, cols]
            left = iota((rows, 128), 1) < HEAD_DIM
            found = []
            for keep in (left, jnp.logical_not(left)):
                s = dot_over_columns(jnp.where(keep, qp, jnp.zeros((), BF)), kp) + mask_s[at, :]
                e = jnp.exp(s - jnp.max(s, axis=1, keepdims=True))
                p = (e * (1.0 / jnp.sum(e, axis=1, keepdims=True))).astype(BF)
                found.append(dot_plain(p, vp))
            a_s[at, cols] = jnp.where(left, found[0], found[1]).astype(BF)
            return carry

        lax.fori_loop(low * per, high * per, body, 0)

    def project():
        for n in range(0, D, BLOCK):
            b_s[:, n : n + BLOCK] = (
                x_ref[:, n : n + BLOCK].astype(F32)
                + dot_plain(a_s[...], wa[3, :, n : n + BLOCK])
                + state["bo"][:, n : n + BLOCK]
            )

        def body(i, carry):
            at = pl.ds(pl.multiple_of(i * 128, 128), 128)
            unit, _ = norm_parts(b_s[at, :])
            h = unit * state["g1"] + state["o1"]
            h_s[at, :] = h
            hl_s[at, :] = h.astype(BF)
            return carry

        lax.fori_loop(0, row_len // 128, body, 0)

    def up(j):
        for n in range(0, D, BLOCK):
            u = dot_plain(hl_s[...], wa[4 + j, :, n : n + BLOCK]) + state["cu"][j][:, n : n + BLOCK]
            g_s[j, :, n : n + BLOCK] = gelu_erf(u).astype(BF)

    def down(j):
        cols = slice(256 * j, 256 * j + 256)
        total = h_s[:, cols] + state["bd"][:, cols]
        for i in range(4):
            total = total + dot_plain(g_s[i], wd[j, D * i : D * i + D, :])
        b_s[:, cols] = total

    def finish():
        def body(i, carry):
            at = pl.ds(pl.multiple_of(i * 128, 128), 128)
            unit, _ = norm_parts(b_s[at, :])
            enc_ref[at, :] = (unit * state["g2"] + state["o2"]).astype(BF)
            return carry

        lax.fori_loop(0, row_len // 128, body, 0)

    def rows_attention():
        q_r = (dot_plain(x_low, wa[2]) + state["bq"]).astype(BF)
        state["q_r"] = q_r
        q_wide = (widen(q_r) * scaled).astype(BF)
        state["q_wide"] = q_wide
        s = jnp.where(open_keys, dot_over_columns(q_wide, k_s[...]), masked_score)
        e = jnp.exp(s - jnp.max(s, axis=1, keepdims=True))
        p = e * (1.0 / jnp.sum(e, axis=1, keepdims=True))
        state["p"] = p
        state["p_low"] = p.astype(BF)
        state["a_r"] = narrow(dot_plain(state["p_low"], v_s[...])).astype(BF)

    def rows_project():
        before = x_r_rows + dot_plain(state["a_r"], wa[3]) + state["bo"]
        unit, inverse = norm_parts(before)
        state["unit1"], state["inv1"] = unit, inverse
        state["h_r"] = unit * state["g1"] + state["o1"]
        state["hl_r"] = state["h_r"].astype(BF)
        state["u_r"], state["g_r"], state["f_r"] = [], [], []

    def rows_up(j):
        u = dot_plain(state["hl_r"], wa[4 + j]) + state["cu"][j]
        state["u_r"].append(u)
        state["g_r"].append(gelu_erf(u).astype(BF))

    def rows_down(j):
        f = jnp.zeros((ROW, 256), F32)
        for i in range(4):
            f = f + dot_plain(state["g_r"][i], wd[j, D * i : D * i + D, :])
        state["f_r"].append(f)

    def rows_finish():
        before = state["h_r"] + jnp.concatenate(state["f_r"], axis=1) + state["bd"]
        unit, inverse = norm_parts(before)
        state["unit2"], state["inv2"] = unit, inverse
        e = (unit * state["g2"] + state["o2"]).astype(BF)
        cls_own[...] = e[:SEGS, :]
        cls_all[z, plane] = e[:SEGS, :]

    def cls_z(r):
        peer = device(lax.rem(z + r, 4), x, y, c)
        return remote(cls_own, cls_all.at[z, plane], cz_s.at[r], cz_r.at[r], peer)

    def cls_plane(r):
        to = lax.rem(plane + r, 8)
        ref = cls_all.at[:, plane]
        return remote(ref, ref, cp_s.at[r], cp_r.at[r], (z * 2 + to // 4, lax.rem(to, 4)))

    xf, yf = x + (1 - c) * (1 - 2 * x), y + c * (1 - 2 * y)
    xg, yg = x + c * (1 - 2 * x), y + (1 - c) * (1 - 2 * y)
    to_f, to_g = device(z, xf, yf, c), device(z, xg, yg, c)
    wholes = ((src_q, fq_ref), (src_u, fu_ref), (src_a, fa_ref))
    sliced = ((src_e, se_ref), (src_g, sg_ref), (src_l, sl_ref))

    def slot(ref):
        return ref.at[tower, c, x, y, zi]

    def whole_z(i):
        src, dst = wholes[i]
        for r in (1, 2, 3):
            go(remote(src, slot(dst), fz_s.at[i, r], fz_r.at[i, r], device(lax.rem(z + r, 4), x, y, c)))
        copy = pltpu.make_async_copy(src, slot(dst), fl.at[i])
        copy.start()
        copy.wait()

    def whole_f(i):
        src, dst = wholes[i]
        for r in (1, 2, 3):
            arrived(slot(dst), fz_s.at[i, r], fz_r.at[i, r])
        ref = dst.at[:, c, x, y]
        go(remote(ref, ref, ff_s.at[i], ff_r.at[i], to_f))
        go(remote(ref, ref, fg_s.at[i, 0], fg_r.at[i, 0], to_g))

    def whole_g(i):
        dst = wholes[i][1]
        ref = dst.at[:, c, xf, yf]
        arrived(ref, ff_s.at[i], ff_r.at[i])
        go(remote(ref, ref, fg_s.at[i, 1], fg_r.at[i, 1], to_g))

    def whole_c(i):
        dst = wholes[i][1]
        for j in (0, 1):
            arrived(dst.at[:, c, xg, yg], fg_s.at[i, j], fg_r.at[i, j])
        ref = dst.at[:, c]
        go(remote(ref, ref, fc_s.at[i], fc_r.at[i], to_core))

    def whole_end(i):
        arrived(wholes[i][1].at[:, c], fc_s.at[i], fc_r.at[i])

    def slice_1(i):
        src, dst = sliced[i]
        for r in range(1, 8):
            there = lax.rem(place + r, 8)
            go(remote(src.at[there], slot(dst), s1_s.at[i, r], s1_r.at[i, r], (there, other)))
        copy = pltpu.make_async_copy(src.at[place], slot(dst), fl.at[3 + i])
        copy.start()
        copy.wait()

    def slice_2(i):
        dst = sliced[i][1]
        for r in range(1, 8):
            arrived(slot(dst), s1_s.at[i, r], s1_r.at[i, r])
        ref = dst.at[:, c, :, y]
        go(remote(ref, ref, s2_s.at[i], s2_r.at[i], to_y))

    def slice_3(i):
        dst = sliced[i][1]
        arrived(dst.at[:, c, :, y], s2_s.at[i], s2_r.at[i])
        ref = dst.at[:, c]
        go(remote(ref, ref, s3_s.at[i], s3_r.at[i], to_core))

    def slice_end(i):
        arrived(sliced[i][1].at[:, c], s3_s.at[i], s3_r.at[i])

    row16 = iota((ROW, D), 0)

    def top(rows):
        return jnp.where(row16[:, : rows.shape[1]] < SEGS, rows, 0.0)

    def pack_early():
        src_q[...] = top(state["q_r"].astype(F32)).astype(BF)
        hl_f32, a_f32, x_f32 = (top(m.astype(F32)) for m in (state["hl_r"], state["a_r"], x_low))
        three = hl_f32 + pltpu.roll(a_f32, 4, 0) + pltpu.roll(x_f32, 8, 0)
        z_rows = dot_plain(state["p_low"], x_ref[...])
        early = jnp.concatenate([three, z_rows], axis=0).astype(BF)
        early = dot_plain(early, sel_s[...]).astype(BF)
        for d in range(8):
            src_e[d] = early[:, 128 * d : 128 * d + 128]

    def pack_gelu():
        for d in range(8):
            packed = jnp.zeros((ROW, 128), F32)
            for b in range(3):
                first = 384 * d + 128 * b
                g = top(state["g_r"][first // D][:, first % D : first % D + 128].astype(F32))
                packed = packed + (pltpu.roll(g, 4 * b, 0) if b else g)
            src_g[d] = packed.astype(BF)

    after = {
        0: [lambda: small_vectors(), lambda: mix(0, k_s, None, None)],
        1: [lambda: mix(1, v_s, "bv", None)],
        2: [lambda: mix(2, q_s, "bq", scaled), rows_attention, lambda: attend(0, 2)],
        3: [rows_project, pack_early, lambda: slice_1(0), lambda: attend(2, 4)],
        4: [lambda: rows_up(0), lambda: attend(4, 6)],
        5: [lambda: rows_up(1), project, lambda: up(0)],
        6: [lambda: rows_up(2), lambda: up(1)],
        7: [lambda: rows_up(3), pack_gelu, lambda: up(2)],
        8: [lambda: rows_down(0), lambda: up(3), lambda: slice_2(0)],
        9: [lambda: rows_down(1), lambda: down(0)],
        10: [lambda: rows_down(2), rows_finish],
    }
    for i in range(kinds + 3):
        if i + WINDOW < kinds:
            stage0(i + WINDOW)
        if i < kinds:
            stage1(i)
        if 0 <= i - 1 < kinds:
            stage2(i - 1)
        if 0 <= i - 2 < kinds:
            stage3(i - 2)
        if 0 <= i - 3 < kinds:
            stage4(i - 3)
            for unit in after[i - 3]:
                unit()

    go(cls_z(1))
    go(cls_z(2))
    go(cls_z(3))
    whole_z(0)
    slice_1(1)
    down(1)
    for r in (1, 2, 3):
        cls_z(r).wait_recv()
    for r in range(1, 8):
        go(cls_plane(r))
    down(2)
    finish()

    keep_enc = pltpu.make_async_copy(enc_ref, enc_out, done.at[0])
    keep_enc.start()
    whole_f(0)
    slice_3(0)
    slice_2(1)
    for r in range(1, 8):
        cls_plane(r).wait_recv()
    for i in range(32):
        cls_f[SEGS * i : SEGS * i + SEGS, :] = cls_all[i // 8, i % 8].astype(F32)
    all_q, all_p = cls_f[:64, :].astype(BF), cls_f[64:, :].astype(BF)
    pair_scale = 2.0 * D ** (-0.5)
    logits = dot_over_columns(all_p, all_q) * pair_scale
    raised = jnp.exp(logits - jnp.max(logits, axis=0, keepdims=True))
    hit = jnp.where(iota((64, 64), 0) == pos_ref[...], 1.0, 0.0)
    d_logits = (raised / jnp.sum(raised, axis=0, keepdims=True) - hit).astype(BF)
    position = me * SEGS - tower * 64
    take = jnp.where((iota((ROW, 64), 1) == iota((ROW, 64), 0) + position) & (iota((ROW, 64), 0) < SEGS), 1.0, 0.0)
    take = take.astype(BF)
    d_q = dot_plain(dot_over_columns(take, d_logits).astype(BF), all_p)
    d_p = dot_plain(dot_plain(take, d_logits).astype(BF), all_q)
    d_cls = jnp.where(tower == 0, d_q, d_p) * pair_scale

    def total(rows):
        return jnp.sum(rows, axis=0, keepdims=True)

    vec_g2, vec_o2 = total(d_cls * state["unit2"]), total(d_cls)
    dz2 = norm_back(state["unit2"], state["inv2"], state["g2"], d_cls)
    df = dz2.astype(BF)
    dh = dz2
    du_rows = []
    for j in range(4):
        dg = jnp.zeros((ROW, D), F32)
        for i in range(3):
            dg = dg + dot_over_columns(df[:, 256 * i : 256 * i + 256], wd[i, D * j : D * j + D, :])
        du = (dg * gelu_slope(state["u_r"][j])).astype(BF)
        du_rows.append(du.astype(F32))
    packed = du_rows[0]
    for j in (1, 2, 3):
        packed = packed + pltpu.roll(du_rows[j], 4 * j, 0)
    src_u[...] = packed.astype(BF)
    whole_z(1)
    whole_g(0)
    for j in range(4):
        dh = dh + dot_over_columns(du_rows[j].astype(BF), wa[4 + j])
    vec_g1, vec_o1 = total(dh * state["unit1"]), total(dh)
    dz1 = norm_back(state["unit1"], state["inv1"], state["g1"], dh)
    db = dz1.astype(BF)
    slice_3(1)
    da = dot_over_columns(db, wa[3]).astype(BF)
    a_wide = widen(da).astype(BF)
    d_p_rows = dot_over_columns(a_wide, v_s[...])
    p = state["p"]
    ds = (p * (d_p_rows - jnp.sum(p * d_p_rows, axis=1, keepdims=True))).astype(BF)
    dq = narrow(dot_plain(ds, k_s[...]) * scaled).astype(BF)
    df_f, db_f, da_f, dq_f = (m.astype(F32) for m in (df, db, da, dq))
    src_a[...] = (df_f + pltpu.roll(db_f, 4, 0) + pltpu.roll(dq_f, 8, 0) + pltpu.roll(da_f, 12, 0)).astype(BF)
    whole_z(2)
    y_rows = dot_plain(ds, x_ref[...]) * scaled
    weight_sum = jnp.sum(state["p_low"].astype(F32), axis=1, keepdims=True)
    vec_bv = total(weight_sum * a_wide.astype(F32))
    vectors = jnp.concatenate(
        [total(dq_f), vec_bv, total(db_f), vec_o1, total(df_f), vec_o2, vec_g1, vec_g2, jnp.zeros((8, D), F32)], axis=0
    )
    late = jnp.concatenate([y_rows, vectors], axis=0).astype(BF)
    late = dot_plain(late, sel_s[...]).astype(BF)
    for d in range(8):
        src_l[d] = late[:, 128 * d : 128 * d + 128]

    slice_1(2)
    whole_f(1)
    whole_c(0)
    t_k = dot_over_columns(state["q_wide"], wa[0]).astype(BF)
    t_v = dot_over_columns(a_wide, wa[1]).astype(BF)
    at_rows = dz1 + dot_over_columns(dq, wa[2])
    high = at_rows.astype(BF)
    rest = (at_rows - high.astype(F32)).astype(BF)
    left = jnp.concatenate([ds, state["p_low"], spot, spot], axis=0)
    right = jnp.concatenate([t_k, t_v, high, rest], axis=0)
    whole_f(2)
    whole_g(1)
    for n in range(0, D, BLOCK):
        drow_ref[:, n : n + BLOCK] = dot_over_rows(left, right[:, n : n + BLOCK])
    keep_row = pltpu.make_async_copy(drow_ref, drow_out, done.at[1])
    keep_row.start()
    slice_2(2)
    whole_g(2)
    whole_c(1)
    slice_3(2)
    whole_c(2)
    for i in range(3):
        whole_end(i)
        slice_end(i)
    keep_enc.wait()
    keep_row.wait()

    for copy in sent:
        copy.wait_send()
    for k in range(kinds):

        @pl.when(inner == 1)
        def _():
            for j, zz in ((1, z_a), (2, z_b)):
                ref = full(k, zz, x, None, c)
                remote(ref, ref, rel_s.at[k, j - 1], z_r.at[k, j], to_near).wait_send()

    for i in range(1, 8):
        sv_copy(i).wait_send()


def grads_kernel(
    fq_hbm, fu_hbm, fa_hbm, se_hbm, sg_hbm, sl_hbm, enc_hbm, drow_hbm,
    enc_out, drow_out, mix_out, proj_out, up_out, down_out, upb_ref, rowb_ref, gain_ref,
    fq_ref, fu_ref, fa_ref, se_ref, sg_ref, sl_ref, mix_ref, proj_ref, up_ref, down_ref, enc_ref, drow_ref, got, put,
):
    def fetch(i, src, dst):
        copy = pltpu.make_async_copy(src, dst, got.at[i])
        copy.start()
        return copy

    order = (
        (fu_hbm, fu_ref), (se_hbm, se_ref), (fa_hbm, fa_ref), (sg_hbm, sg_ref), (fq_hbm, fq_ref), (sl_hbm, sl_ref),
        (enc_hbm, enc_ref), (drow_hbm, drow_ref),
    )
    in_u, in_e, in_a, in_g, in_q, in_l, keep_e, keep_d = (fetch(i, *pair) for i, pair in enumerate(order))
    place = lax.axis_index("dp")
    kind = iota((256, 128), 0) % ROW
    part = 96
    pick = iota((192, 64), 0)
    group, within = pick // 48, pick % SEGS
    head_row, head_col = iota((192, D), 0), iota((192, D), 1)
    own_head = (head_row % 48) // SEGS == head_col // HEAD_DIM
    take_q = jnp.where(iota((192, 64), 1) == group * ROW + within, 1.0, 0.0).astype(BF)
    take_a = jnp.where(iota((192, 64), 1) == group * ROW + within + 12, 1.0, 0.0).astype(BF)
    kind16, col16 = iota((256, ROW), 0) % ROW, iota((256, ROW), 1)
    again_row, again_col = iota((256, 256), 0), iota((256, 256), 1)
    again = jnp.where(again_col == again_row // ROW * ROW + again_row % SEGS, 1.0, 0.0).astype(BF)
    stores = []

    def store(src, dst):
        copy = pltpu.make_async_copy(src, dst, put.at[len(stores)])
        copy.start()
        stores.append(copy)

    def keep(rows, lo, hi):
        return jnp.where((kind >= lo) & (kind < hi), rows, jnp.zeros((), BF))

    in_u.wait()
    in_e.wait()
    three = [se_ref[t, :, 0:16, :].reshape(256, 128) for t in range(2)]
    for t in range(2):
        four = dot_plain(again, three[t]).astype(BF)
        for j in range(4):
            cols = slice(FF * t + D * j, FF * t + D * j + D)
            up_ref[:, cols] = dot_over_rows(keep(four, 4 * j, 4 * j + 4), fu_ref[t])[:part]
            store(up_ref.at[:, cols], up_out.at[:, cols])
    up_bias = jnp.zeros((ROW, 384), F32)
    for t in range(2):
        mine = fu_ref[t, :, pl.ds(pl.multiple_of(place % 2 * 384, 128), 384)]
        to_up = jnp.where((kind16 // 4 == place // 2) & (col16 == t), 1.0, 0.0).astype(BF)
        up_bias = up_bias + dot_over_rows(to_up, mine)
    upb_ref[...] = up_bias[:2]
    keep_e.wait()
    store(enc_ref, enc_out)
    keep_d.wait()
    store(drow_ref, drow_out)
    in_a.wait()
    in_g.wait()
    for t in range(2):
        fa = fa_ref[t]
        cols = slice(D * t, D * t + D)
        proj_ref[:, cols] = dot_over_rows(keep(three[t], 4, 8), fa)[:part]
        store(proj_ref.at[:, cols], proj_out.at[:, cols])
        first = slice(3 * D * t, 3 * D * t + D)
        mix_ref[:, first] = dot_over_rows(keep(three[t], 8, 12), fa)[:part]
        store(mix_ref.at[:, first], mix_out.at[:, first])
        df = dot_plain(again, fa).astype(BF)
        g = sg_ref[t].reshape(256, 128)
        for b in range(3):
            at = slice(128 * b, 128 * b + 128)
            down_ref[at, cols] = dot_over_rows(keep(g, 4 * b, 4 * b + 4), df)
        store(down_ref.at[:, cols], down_out.at[:, cols])
    for t in range(2):
        gv = jnp.zeros((128, D), F32)
        for s in range(4):
            a_wide = jnp.where(own_head, dot_plain(take_a, fa_ref[t, 64 * s : 64 * s + 64, :]), 0.0).astype(BF)
            gv = gv + dot_over_rows(se_ref[t, 4 * s : 4 * s + 4, 16:64, :].reshape(192, 128), a_wide)
        cols = slice(3 * D * t + 2 * D, 3 * D * t + 3 * D)
        mix_ref[:, cols] = gv[:part]
        store(mix_ref.at[:, cols], mix_out.at[:, cols])
    in_q.wait()
    in_l.wait()
    biases = jnp.zeros((ROW, 128), F32)
    gains = jnp.zeros((ROW, 128), F32)
    for t in range(2):
        gk = jnp.zeros((128, D), F32)
        for s in range(4):
            q_wide = jnp.where(own_head, dot_plain(take_q, fq_ref[t, 64 * s : 64 * s + 64, :]), 0.0).astype(BF)
            gk = gk + dot_over_rows(sl_ref[t, 4 * s : 4 * s + 4, 0:48, :].reshape(192, 128), q_wide)
        cols = slice(3 * D * t + D, 3 * D * t + 2 * D)
        mix_ref[:, cols] = gk[:part]
        store(mix_ref.at[:, cols], mix_out.at[:, cols])
        vec = sl_ref[t, :, 48:64, :].reshape(256, 128)
        to_bias = jnp.where((kind16 < 6) & (col16 == kind16 + 6 * t), 1.0, 0.0).astype(BF)
        to_gain = jnp.where((kind16 >= 6) & (kind16 < 8) & (col16 == kind16 - 6 + 2 * t), 1.0, 0.0).astype(BF)
        biases = biases + dot_over_rows(to_bias, vec)
        gains = gains + dot_over_rows(to_gain, vec)
    rowb_ref[...] = biases[:12, :part]
    gain_ref[...] = gains[:4, :part]
    for copy in stores:
        copy.wait()


def fast_device(text_rows, text_segments, positives, w_mix, w_proj, w_up, w_down, b_up, b_rows, g_rows):
    sem = pltpu.SemaphoreType.DMA
    vm = pltpu.VMEM
    part = b_rows.shape[0]
    kinds = len(PIECES)
    fulls = jax.ShapeDtypeStruct((2, 2, 2, 2, 2, ROW, D), BF)
    row_len = text_rows.shape[1]
    here, there = pl.BlockSpec(memory_space=vm), pl.BlockSpec(memory_space=pl.ANY)
    slices = lambda r: jax.ShapeDtypeStruct((2, 2, 2, 2, 2, r, 128), BF)
    encoded, d_rows, fq, fu, fa, se, sg, sl = pl.pallas_call(
        main_kernel,
        out_shape=[
            jax.ShapeDtypeStruct((row_len, D), BF),
            jax.ShapeDtypeStruct((row_len, D), F32),
            fulls, fulls, fulls, slices(64), slices(ROW), slices(64),
        ],
        in_specs=[here] * 6 + [there] * 4,
        out_specs=[there] * 2 + [here] * 6,
        scratch_shapes=[
            vm((row_len, D), BF), vm((row_len, D), F32),
            vm((8, D, D), BF), vm((3, FF, 256), BF),
            vm((2, ROW, 384), F32), vm((2, ROW, 384), BF), vm((8, ROW, 384), BF),
            vm((row_len, D), BF), vm((row_len, D), BF), vm((row_len, D), BF), vm((row_len, D), BF),
            vm((row_len, row_len), F32), vm((row_len, D), F32), vm((row_len, D), F32), vm((row_len, D), BF),
            vm((4, row_len, D), BF), vm((D, 1024), BF),
            vm((SEGS, D), BF), vm((4, 8, SEGS, D), BF), vm((128, D), F32),
            vm((ROW, D), BF), vm((ROW, D), BF), vm((ROW, D), BF),
            vm((8, 64, 128), BF), vm((8, ROW, 128), BF), vm((8, 64, 128), BF),
            sem((kinds,)), sem((kinds,)), sem((kinds,)), sem((kinds, 3)), sem((kinds, 2)),
            sem((kinds, 4)), sem((kinds, 4)), sem((kinds, 4)), sem((kinds, 4)), sem((kinds,)), sem((kinds,)),
            sem((8,)), sem((8,)), sem((4,)), sem((4,)), sem((8,)), sem((8,)), sem((2,)),
            sem((6,)), sem((3, 4)), sem((3, 4)), sem((3,)), sem((3,)), sem((3, 2)), sem((3, 2)), sem((3,)), sem((3,)),
            sem((3, 8)), sem((3, 8)), sem((3,)), sem((3,)), sem((3,)), sem((3,)),
        ],
        compiler_params=pltpu.CompilerParams(collective_id=5, has_side_effects=True, vmem_limit_bytes=60 << 20),
        name="main_step",
    )(text_rows[0], text_segments, positives[None, :], b_up.T, b_rows.T, g_rows.T, w_mix, w_proj, w_up, w_down)
    shape = lambda r, n: jax.ShapeDtypeStruct((r, n), F32)
    grads = pl.pallas_call(
        grads_kernel,
        out_shape=[
            jax.ShapeDtypeStruct((row_len, D), BF), shape(row_len, D),
            shape(part, 6 * D), shape(part, 2 * D), shape(part, 2 * FF), shape(4 * part, 2 * D),
            shape(2, 4 * part), shape(12, part), shape(4, part),
        ],
        in_specs=[there] * 8,
        out_specs=[there] * 6 + [here] * 3,
        scratch_shapes=[
            vm((2, 256, D), BF), vm((2, 256, D), BF), vm((2, 256, D), BF),
            vm((2, 16, 64, 128), BF), vm((2, 16, ROW, 128), BF), vm((2, 16, 64, 128), BF),
            vm((part, 6 * D), F32), vm((part, 2 * D), F32), vm((part, 2 * FF), F32), vm((4 * part, 2 * D), F32),
            vm((row_len, D), BF), vm((row_len, D), F32), sem((8,)), sem((20,)),
        ],
        compiler_params=pltpu.CompilerParams(vmem_limit_bytes=60 << 20),
        name="weight_grads",
    )(
        fq.reshape(2, 256, D), fu.reshape(2, 256, D), fa.reshape(2, 256, D),
        se.reshape(2, 16, 64, 128), sg.reshape(2, 16, ROW, 128), sl.reshape(2, 16, 64, 128), encoded, d_rows,
    )
    encoded, d_rows, mix, proj, up, down, up_b, row_b, gain = grads
    return encoded[None], d_rows[None], mix, proj, up, down, up_b.T, row_b.T, gain.T


def solution(mesh):
    rows, cols = P(("dp", "outer"), None, None), P("dp", None)
    sizes = (mesh.shape["dp"], mesh.shape["outer"])
    return jax.shard_map(
        fast_device if sizes == (8, 4) else per_device,
        mesh=mesh,
        in_specs=(rows, P(("dp", "outer"), None), P(), cols, cols, cols, cols, cols, cols, cols),
        out_specs=(rows, rows, cols, cols, cols, cols, cols, cols, cols),
        check_vma=False,
    )
```

```python
import functools

import jax
import jax.numpy as jnp
from jax import lax
from jax.experimental import pallas as pl
from jax.experimental.pallas import tpu as pltpu
from jax.sharding import PartitionSpec as P

D = 768
HEADS = 12
HEAD_DIM = 64
FF = 3072
SEGS = 4
BF = jnp.bfloat16
F32 = jnp.float32
MESH = pl.DeviceIdType.MESH

masked_score = -1e30
layer_eps = 1e-05


def dot_plain(left, right):
    return jnp.dot(left, right, preferred_element_type=F32)


def dot_over_rows(left, right):
    return lax.dot_general(left, right, (((0,), (0,)), ((), ())), preferred_element_type=F32)


def dot_over_columns(left, right):
    return lax.dot_general(left, right, (((1,), (1,)), ((), ())), preferred_element_type=F32)


def gelu_exact(inputs):
    return jax.nn.gelu(inputs, approximate=False)


def norm_parts(inputs):
    center = inputs - jnp.mean(inputs, axis=-1, keepdims=True)
    inverse = lax.rsqrt(jnp.mean(center * center, axis=-1, keepdims=True) + layer_eps)
    return center * inverse, inverse


def norm_back(unit, inverse, gain, grad):
    scaled = gain * grad
    return inverse * (
        scaled
        - jnp.mean(scaled, axis=-1, keepdims=True)
        - unit * jnp.mean(scaled * unit, axis=-1, keepdims=True)
    )


def gather_weights(weights, widths, n_dp):
    tower = lax.axis_index("dp") * 2 // n_dp
    whole = [lax.all_gather(w, "dp", axis=0, tiled=True) for w in weights]
    return [lax.dynamic_slice_in_dim(w, tower * n, n, 1) for w, n in zip(whole, widths)]


def spread_kernel(n_outer, total, whole_ref, parts_ref, all_ref, sliced_ref, local, s_one, r_one, s_two, r_two):
    dp, outer = lax.axis_index("dp"), lax.axis_index("outer")
    me = dp * n_outer + outer
    barrier = pltpu.get_barrier_semaphore()

    def greet(i, carry):
        peer = lax.rem(me + i, total)
        pl.semaphore_signal(barrier, inc=1, device_id=(peer // n_outer, lax.rem(peer, n_outer)), device_id_type=MESH)
        return carry

    lax.fori_loop(1, total, greet, 0)
    pl.semaphore_wait(barrier, total - 1)

    def copies(i):
        peer = lax.rem(me + i, total)
        there = peer // n_outer
        device = (there, lax.rem(peer, n_outer))
        one = pltpu.make_async_remote_copy(
            src_ref=whole_ref, dst_ref=all_ref.at[me], send_sem=s_one.at[i], recv_sem=r_one.at[i],
            device_id=device, device_id_type=MESH,
        )
        if parts_ref is None:
            return (one,)
        two = pltpu.make_async_remote_copy(
            src_ref=parts_ref.at[there], dst_ref=sliced_ref.at[me], send_sem=s_two.at[i], recv_sem=r_two.at[i],
            device_id=device, device_id_type=MESH,
        )
        return (one, two)

    def send(i, carry):
        for copy in copies(i):
            copy.start()
        return carry

    lax.fori_loop(1, total, send, 0)
    own = [pltpu.make_async_copy(whole_ref, all_ref.at[me], local.at[0])]
    if parts_ref is not None:
        own.append(pltpu.make_async_copy(parts_ref.at[dp], sliced_ref.at[me], local.at[1]))
    for copy in own:
        copy.start()

    def settle(i, carry):
        for copy in copies(i):
            copy.wait()
        return carry

    lax.fori_loop(1, total, settle, 0)
    for copy in own:
        copy.wait()


def spread(whole, parts, n_dp, n_outer, identity):
    total = n_dp * n_outer
    sem = pltpu.SemaphoreType.DMA
    out_shape = [jax.ShapeDtypeStruct((total,) + whole.shape, whole.dtype)]
    operands = [whole]
    if parts is not None:
        out_shape.append(jax.ShapeDtypeStruct((total,) + parts.shape[1:], parts.dtype))
        operands.append(parts)
        kernel = functools.partial(spread_kernel, n_outer, total)
        scratch = [sem((2,))] + [sem((total,))] * 4
    else:
        def kernel(w, a, local, s, r):
            spread_kernel(n_outer, total, w, None, a, None, local, s, r, None, None)
        scratch = [sem((2,))] + [sem((total,))] * 2
    return pl.pallas_call(
        kernel,
        out_shape=out_shape,
        in_specs=[pl.BlockSpec(memory_space=pltpu.VMEM)] * len(operands),
        out_specs=[pl.BlockSpec(memory_space=pltpu.VMEM)] * len(out_shape),
        scratch_shapes=scratch,
        compiler_params=pltpu.CompilerParams(
            collective_id=identity, has_side_effects=True, vmem_limit_bytes=48 << 20
        ),
        name="spread%d" % identity,
    )(*operands)


def expand_heads(rows):
    head_of = jnp.arange(D, dtype=jnp.int32) // HEAD_DIM
    keep = head_of[None, :] == jnp.arange(HEADS, dtype=jnp.int32)[:, None]
    return jnp.where(keep[:, None, :], rows[None], 0).reshape(HEADS * rows.shape[0], D)


def per_device(text_rows, text_segments, positives, w_mix, w_proj, w_up, w_down, b_up, b_rows, g_rows):
    n_dp, n_outer = lax.axis_size("dp"), lax.axis_size("outer")
    total = n_dp * n_outer
    own_index = lax.axis_index(("dp", "outer"))
    tower = own_index * 2 // total
    rows_in, segments = text_rows[0], text_segments[0]
    row_len = rows_in.shape[0]
    widths = (3 * D, D, FF, D)
    wm, wp, wu, wd = gather_weights((w_mix, w_proj, w_up, w_down), widths, n_dp)
    part_f, part_d = b_up.shape[0], b_rows.shape[0]
    small = jnp.concatenate([b_up.reshape(part_f // part_d, part_d, 2).transpose(0, 2, 1).reshape(-1, part_d), b_rows.T, g_rows.T], axis=0)
    small = lax.all_gather(small, "dp", axis=0)
    split = 2 * (part_f // part_d)
    up_b = small[:, :split].reshape(n_dp, part_f // part_d, 2, part_d).transpose(2, 0, 1, 3).reshape(2, FF)
    row_b = small[:, split : split + 12].transpose(1, 0, 2).reshape(2, 6, D)
    gain_b = small[:, split + 12 :].transpose(1, 0, 2).reshape(2, 2, D)
    pick = lambda both_towers: jnp.where(tower == 0, both_towers[0], both_towers[1]).astype(F32)
    c_up, biases, gains = pick(up_b), pick(row_b), pick(gain_b)
    bq, bv, bo, o1, bd, o2 = (biases[i] for i in range(6))
    g1, g2 = gains[0], gains[1]

    scaled = HEAD_DIM ** (-0.5)
    mixed = (dot_plain(rows_in, wm) + jnp.concatenate([bq, jnp.zeros_like(bq), bv])).astype(BF)
    q, k, v = mixed[:, :D], mixed[:, D : 2 * D], mixed[:, 2 * D :]
    allowed = segments[:, None] == segments[None, :]
    heads = lambda m: m.reshape(row_len, HEADS, HEAD_DIM)
    scores = jnp.einsum("qhe,khe->hqk", heads(q), heads(k), preferred_element_type=F32) * scaled
    scores = jnp.where(allowed[None], scores, masked_score)
    top = jnp.max(scores, axis=-1, keepdims=True)
    raised = jnp.exp(scores - top)
    chances = (raised / jnp.sum(raised, axis=-1, keepdims=True)).astype(BF)
    attended = jnp.einsum("hqk,khe->qhe", chances, heads(v), preferred_element_type=F32).reshape(row_len, D).astype(BF)
    before_one = rows_in.astype(F32) + dot_plain(attended, wp) + bo
    unit_one, inv_one = norm_parts(before_one)
    h1 = unit_one * g1 + o1
    h1_low = h1.astype(BF)
    up_pre = dot_plain(h1_low, wu) + c_up
    gelu_low = gelu_exact(up_pre).astype(BF)
    before_two = h1 + dot_plain(gelu_low, wd) + bd
    unit_two, inv_two = norm_parts(before_two)
    encoded = unit_two * g2 + o2

    levels = jnp.arange(SEGS, dtype=jnp.int32)
    starts = jnp.sum((segments[None, :] < levels[:, None]).astype(jnp.int32), axis=1)
    at = lambda m: jnp.take(m, starts, axis=0)
    vectors = at(encoded).astype(BF)
    all_cls = spread(vectors, None, n_dp, n_outer, 2)[0].reshape(total * SEGS, D)
    texts = total * SEGS // 2
    all_q, all_p = all_cls[:texts], all_cls[texts:]
    pair_scale = 2.0 * D ** (-0.5)
    logits = dot_over_columns(all_q, all_p) * pair_scale
    raised_l = jnp.exp(logits - jnp.max(logits, axis=1, keepdims=True))
    hit = (positives[:, None] == jnp.arange(texts, dtype=jnp.int32)[None, :]).astype(F32)
    d_logits = (raised_l / jnp.sum(raised_l, axis=1, keepdims=True) - hit).astype(BF)
    position = own_index * SEGS - tower * texts
    d_q = dot_plain(lax.dynamic_slice_in_dim(d_logits, position, SEGS, 0), all_p)
    d_p = dot_over_rows(lax.dynamic_slice_in_dim(d_logits, position, SEGS, 1), all_q)
    d_cls = jnp.where(tower == 0, d_q, d_p) * pair_scale

    ut, it = at(unit_two), at(inv_two)
    dg2, do2 = jnp.sum(d_cls * ut, axis=0), jnp.sum(d_cls, axis=0)
    dz2 = norm_back(ut, it, g2, d_cls)
    df = dz2.astype(BF)
    dg = dot_over_columns(df, wd)
    u_r = at(up_pre)
    _, gelu_back = jax.vjp(gelu_exact, u_r)
    du = gelu_back(dg)[0].astype(BF)
    dh1 = dz2 + dot_over_columns(du, wu)
    uo, io = at(unit_one), at(inv_one)
    dg1, do1 = jnp.sum(dh1 * uo, axis=0), jnp.sum(dh1, axis=0)
    dz1 = norm_back(uo, io, g1, dh1)
    db = dz1.astype(BF)
    da = dot_over_columns(db, wp).astype(BF)
    q_r = at(q)
    q_wide, a_wide = expand_heads(q_r), expand_heads(da)
    own_segment = jnp.tile(levels, HEADS)
    open_keys = own_segment[:, None] == segments[None, :]
    s_r = jnp.where(open_keys, dot_over_columns(q_wide, k) * scaled, masked_score)
    e_r = jnp.exp(s_r - jnp.max(s_r, axis=-1, keepdims=True))
    p_r = e_r / jnp.sum(e_r, axis=-1, keepdims=True)
    pl_r = p_r.astype(BF)
    dp_r = dot_over_columns(a_wide, v)
    ds_r = (p_r * (dp_r - jnp.sum(p_r * dp_r, axis=-1, keepdims=True))).astype(BF)
    dq_wide = dot_plain(ds_r, k).reshape(HEADS, SEGS, HEADS, HEAD_DIM)
    dq = (jnp.einsum("hshe->she", dq_wide).reshape(SEGS, D) * scaled).astype(BF)
    y_r = (dot_plain(ds_r, rows_in) * scaled).astype(BF)
    z_r = dot_plain(pl_r, rows_in).astype(BF)
    weight_sum = jnp.sum(pl_r.astype(F32), axis=1, keepdims=True)
    dbv = jnp.sum(weight_sum * a_wide.astype(F32), axis=0)
    t_k = (dot_over_columns(q_wide, wm[:, D : 2 * D]) * scaled).astype(BF)
    t_v = dot_over_columns(a_wide, wm[:, 2 * D :]).astype(BF)
    d_rows = dot_over_rows(jnp.concatenate([ds_r, pl_r], axis=0), jnp.concatenate([t_k, t_v], axis=0))
    d_rows_at = dz1 + dot_over_columns(dq, wm[:, :D])
    spot = (starts[:, None] == jnp.arange(row_len, dtype=jnp.int32)[None, :])
    for s in range(SEGS):
        d_rows = d_rows + jnp.where(spot[s][:, None], d_rows_at[s][None, :], 0.0)

    ff_rows = SEGS * FF // D
    whole = jnp.concatenate(
        [df, db, dq, q_r, da, du.reshape(ff_rows, D), jnp.stack([dbv, do1, do2, dg1, dg2]).astype(BF), jnp.zeros((3, D), BF)],
        axis=0,
    )
    g_r, h_r, at_r, x_r = at(gelu_low), at(h1_low), at(attended), at(rows_in)
    by_part = lambda m: m.reshape(m.shape[0], n_dp, m.shape[1] // n_dp).transpose(1, 0, 2)
    parts = jnp.concatenate(
        [by_part(h_r), by_part(at_r), by_part(x_r), by_part(y_r), by_part(z_r),
         by_part(g_r).reshape(n_dp, -1, part_d)],
        axis=1,
    )
    all_w, all_s = spread(whole, parts, n_dp, n_outer, 3)
    half = total // 2
    tw = all_w.reshape(2, half, -1, D)
    ts = all_s.reshape(2, half, -1, part_d)
    rank = lambda m: m.reshape(half * SEGS, -1)
    grads = []
    outs = [[], [], [], []]
    vec_b, vec_g, vec_u = [], [], []
    mine = lax.axis_index("dp")
    for t in range(2):
        w, s = tw[t], ts[t]
        df_a, db_a, dq_a, q_a, da_a = (rank(w[:, 4 * i : 4 * i + 4]) for i in range(5))
        du_a = w[:, 20 : 20 + ff_rows].reshape(half * SEGS, FF)
        vec = jnp.sum(w[:, 20 + ff_rows : 25 + ff_rows].astype(F32), axis=0)
        h_a, at_a, x_a = (rank(s[:, 4 * i : 4 * i + 4]) for i in range(3))
        y_a = s[:, 12:60].reshape(half, HEADS, SEGS, part_d)
        z_a = s[:, 60:108].reshape(half, HEADS, SEGS, part_d)
        g_a = s[:, 108:].reshape(half * SEGS, part_f)
        by_head = lambda m: m.reshape(half, SEGS, HEADS, HEAD_DIM)
        gk = jnp.einsum("rhsa,rshe->ahe", y_a, by_head(q_a), preferred_element_type=F32).reshape(part_d, D)
        gv = jnp.einsum("rhsa,rshe->ahe", z_a, by_head(da_a), preferred_element_type=F32).reshape(part_d, D)
        outs[0] += [dot_over_rows(x_a, dq_a), gk, gv]
        outs[1].append(dot_over_rows(at_a, db_a))
        outs[2].append(dot_over_rows(h_a, du_a))
        outs[3].append(dot_over_rows(g_a, df_a))
        col = lambda m, n: lax.dynamic_slice_in_dim(m, mine * n, n, 0)
        summed = lambda m: jnp.sum(m.astype(F32), axis=0)
        vec_b += [col(m, part_d) for m in (summed(dq_a), vec[0], summed(db_a), vec[1], summed(df_a), vec[2])]
        vec_g += [col(m, part_d) for m in (vec[3], vec[4])]
        vec_u.append(col(summed(du_a), part_f))
    return (
        encoded.astype(BF)[None],
        d_rows[None],
        jnp.concatenate(outs[0], axis=1),
        jnp.concatenate(outs[1], axis=1),
        jnp.concatenate(outs[2], axis=1),
        jnp.concatenate(outs[3], axis=1),
        jnp.stack(vec_u, axis=1),
        jnp.stack(vec_b, axis=1),
        jnp.stack(vec_g, axis=1),
    )


PIECES = (
    [(0, D, D), (0, 2 * D, D), (0, 0, D), (1, 0, D)]
    + [(2, D * i, D) for i in range(4)]
    + [(3, 256 * i, 256) for i in range(3)]
)
WIDTHS = (3 * D, D, FF, D)
ROW = 16
BLOCK = 256


def iota(shape, dim):
    return lax.broadcasted_iota(jnp.int32, shape, dim)


def gelu_erf(u):
    return 0.5 * u * (1.0 + lax.erf(u * 0.7071067811865476))


def gelu_slope(u):
    return 0.5 * (1.0 + lax.erf(u * 0.7071067811865476)) + u * (0.3989422804014327 * jnp.exp(-0.5 * u * u))


def main_kernel(
    x_in, seg_in, pos_in, bu_in, br_in, gr_in, w_mix, w_proj, w_up, w_down,
    enc_out, drow_out, fq_ref, fu_ref, fa_ref, se_ref, sg_ref, sl_ref,
    x_ref, seg_ref, pos_ref, bu_ref, br_ref, gr_ref, first, enc_ref, drow_ref, wa, wd, sv_f, sv_ref, sv_all, q_s, k_s, v_s, a_s, mask_s, b_s, h_s, hl_s, g_s, sel_s,
    cls_own, cls_all, cls_f, src_q, src_u, src_a, src_e, src_g, src_l,
    ld, far_s, near_s, z_r, rel_s, x_s, x_r, y_s, y_r, c_s, c_r, sv_sem, sv_r, cz_s, cz_r, cp_s, cp_r, done,
    fl, fz_s, fz_r, ff_s, ff_r, fg_s, fg_r, fc_s, fc_r, s1_s, s1_r, s2_s, s2_r, s3_s, s3_r,
):
    sources = (w_mix, w_proj, w_up, w_down)
    place, other = lax.axis_index("dp"), lax.axis_index("outer")
    z, x = place // 2, place % 2
    y, c = other // 2, other % 2
    tower, zi = z // 2, z % 2
    me = place * 4 + other
    inner = zi * (1 - tower) + (1 - zi) * tower
    zn = z + 1 - 2 * zi
    z_a, z_b = 2 - tower, 3 - 3 * tower
    scaled = HEAD_DIM ** (-0.5)
    row_len = x_ref.shape[0]

    def device(zz, xx, yy, cc):
        return (zz * 2 + xx, yy * 2 + cc)

    plane = x * 4 + other
    to_near, to_far = device(zn, x, y, c), device(z_a, x, y, c)
    to_x, to_y, to_core = device(z, 1 - x, y, c), device(z, x, 1 - y, c), device(z, x, y, 1 - c)

    loads = []
    pairs = ((bu_in, bu_ref), (br_in, br_ref), (gr_in, gr_ref), (seg_in, seg_ref), (pos_in, pos_ref), (x_in, x_ref))
    for i, (src, dst) in enumerate(pairs):
        loads.append(pltpu.make_async_copy(src, dst, first.at[i]))
        loads[-1].start()
    barrier = pltpu.get_barrier_semaphore()

    def peer_at(i):
        p = lax.rem(me + i, 32)
        return (p // 4, lax.rem(p, 4))

    def greet(i, carry):
        pl.semaphore_signal(barrier, inc=1, device_id=peer_at(i), device_id_type=MESH)
        return carry

    lax.fori_loop(1, 32, greet, 0)
    pl.semaphore_wait(barrier, 31)

    def remote(src, dst, s, r, peer):
        return pltpu.make_async_remote_copy(
            src_ref=src, dst_ref=dst, send_sem=s, recv_sem=r, device_id=peer, device_id_type=MESH
        )

    def arrived(ref, s, r):
        remote(ref, ref, s, r, to_x).wait_recv()

    sent = []

    def go(copy):
        copy.start()
        sent.append(copy)

    def dims(k):
        tensor, first, cols = PIECES[k]
        return tensor, sources[tensor].shape[0], first, cols

    def own(k, which, half_row, half_col):
        tensor, r, first, n = dims(k)
        row, rows = (0, r) if half_row is None else (half_row * (r // 2), r // 2)
        col, cols = which * WIDTHS[tensor] + first, n
        if half_col is not None:
            col, cols = col + half_col * (n // 2), n // 2
        return sources[tensor].at[
            pl.ds(pl.multiple_of(row, 16), rows), pl.ds(pl.multiple_of(col, 128), cols)
        ]

    def held(k):
        return wa.at[k] if k < 8 else wd.at[k - 8]

    def full(k, zz, xx, half_row, half_col):
        tensor, r, first, n = dims(k)
        row, rows = (zz * 2 + xx) * r, r
        if half_row is not None:
            row, rows = row + half_row * (r // 2), r // 2
        col, cols = (0, n) if half_col is None else (pl.multiple_of(half_col * (n // 2), 128), n // 2)
        return held(k).at[pl.ds(pl.multiple_of(row, 16), rows), pl.ds(col, cols)]

    planes = (z, zn, z_a, z_b)
    kinds = len(PIECES)
    local = []

    def stage0(k):
        go(remote(own(k, 1 - tower, None, c), full(k, z, x, None, c), far_s.at[k], z_r.at[k, 2 - inner], to_far))
        go(remote(own(k, tower, y, c), full(k, z, x, y, c), near_s.at[k], z_r.at[k, 0], to_near))
        go(remote(own(k, tower, None, c), full(k, z, x, None, c), x_s.at[k, 0], x_r.at[k, 0], to_x))
        copy = pltpu.make_async_copy(own(k, tower, None, c), full(k, z, x, None, c), ld.at[k])
        copy.start()
        local.append(copy)

    def stage1(k):
        ref = full(k, zn, x, y, c)
        arrived(ref, near_s.at[k], z_r.at[k, 0])
        go(remote(ref, ref, x_s.at[k, 1], x_r.at[k, 1], to_x))
        go(remote(ref, ref, y_s.at[k, 0], y_r.at[k, 0], to_y))
        for j, zz in ((1, z_a), (2, z_b)):
            whole = full(k, zz, x, None, c)
            arrived(whole, near_s.at[k], z_r.at[k, j])

            @pl.when(inner == 1)
            def _():
                remote(whole, whole, rel_s.at[k, j - 1], z_r.at[k, j], to_near).start()

            ref = full(k, zz, x, y, c)
            go(remote(ref, ref, x_s.at[k, 1 + j], x_r.at[k, 1 + j], to_x))

    def stage2(k):
        arrived(full(k, z, 1 - x, None, c), x_s.at[k, 0], x_r.at[k, 0])
        for j in (1, 2, 3):
            ref = full(k, planes[j], 1 - x, y, c)
            arrived(ref, x_s.at[k, j], x_r.at[k, j])
            go(remote(ref, ref, y_s.at[k, j], y_r.at[k, j], to_y))

    def stage3(k):
        arrived(full(k, zn, x, 1 - y, c), y_s.at[k, 0], y_r.at[k, 0])
        for j in (1, 2, 3):
            arrived(full(k, planes[j], 1 - x, 1 - y, c), y_s.at[k, j], y_r.at[k, j])
        local[k].wait()
        n = dims(k)[3]
        ref = held(k).at[:, pl.ds(pl.multiple_of(c * (n // 2), 128), n // 2)]
        go(remote(ref, ref, c_s.at[k], c_r.at[k], to_core))

    def stage4(k):
        n = dims(k)[3]
        ref = held(k).at[:, pl.ds(pl.multiple_of((1 - c) * (n // 2), 128), n // 2)]
        arrived(ref, c_s.at[k], c_r.at[k])

    def sv_copy(i):
        there = lax.rem(place + i, 8)
        return remote(sv_ref.at[there // 4], sv_all.at[place], sv_sem.at[i], sv_r.at[i], (there, other))

    WINDOW = 2
    for k in range(WINDOW):
        stage0(k)
    for copy in loads:
        copy.wait()
    sv_f[...] = jnp.zeros_like(sv_f)
    for t in range(2):
        sv_f[t, 0:1, :] = bu_ref[...].astype(F32)[t : t + 1]
        sv_f[t, 1:7, 0:96] = br_ref[...].astype(F32)[6 * t : 6 * t + 6]
        sv_f[t, 7:9, 0:96] = gr_ref[...].astype(F32)[2 * t : 2 * t + 2]
    sv_ref[...] = sv_f[...].astype(BF)

    for i in range(1, 8):
        sv_copy(i).start()
    sv_all[place] = sv_ref[tower]

    sel_row, sel_col = iota((D, 1024), 0), iota((D, 1024), 1)
    lane = sel_col % 128
    sel_s[...] = jnp.where((sel_row == (sel_col // 128) * 96 + lane) & (lane < 96), 1.0, 0.0).astype(BF)
    segments = seg_ref[...]
    level = iota((ROW, row_len), 0)
    begin = jnp.sum(jnp.where(segments < level, 1.0, 0.0), axis=1, keepdims=True).astype(jnp.int32)
    spot = jnp.where((iota((ROW, row_len), 1) == begin) & (level < SEGS), 1.0, 0.0).astype(BF)
    belongs = jnp.where((segments == level) & (level < SEGS), 1.0, 0.0).astype(BF)
    mask_s[...] = (dot_over_rows(belongs, belongs) - 1.0) * -masked_score
    wide_row, wide_col = iota((48, D), 0), iota((48, D), 1)
    own_head = (wide_row // SEGS) == (wide_col // HEAD_DIM)
    repeat = jnp.where(iota((48, ROW), 0) % SEGS == iota((48, ROW), 1), 1.0, 0.0).astype(BF)
    open_keys = (iota((48, row_len), 0) % SEGS) == segments
    x_r_rows = dot_plain(spot, x_ref[...])
    x_low = x_r_rows.astype(BF)

    def widen(rows):
        return jnp.where(own_head, dot_plain(repeat, rows), 0.0)

    def narrow(wide):
        return dot_over_rows(repeat, jnp.where(own_head, wide, 0.0).astype(BF))

    state = {}

    def small_vectors():
        for i in range(1, 8):
            sv_copy(i).wait_recv()
        rows = jnp.zeros((ROW, D), F32)
        for m in range(8):
            put = jnp.where((iota((128, D), 1) == iota((128, D), 0) + 96 * m) & (iota((128, D), 0) < 96), 1.0, 0.0)
            rows = rows + dot_plain(sv_all[m][:, :128], put.astype(BF))
        names = ("bq", "bv", "bo", "o1", "bd", "o2", "g1", "g2")
        for i, name in enumerate(names):
            state[name] = rows[1 + i : 2 + i, :]
        state["cu"] = [
            jnp.concatenate([sv_all[2 * j][0:1, :], sv_all[2 * j + 1][0:1, :]], axis=1).astype(F32) for j in range(4)
        ]

    def mix(k, out, bias, factor):
        for n in range(0, D, BLOCK):
            m = dot_plain(x_ref[...], wa[k, :, n : n + BLOCK])
            if bias is not None:
                m = m + state[bias][:, n : n + BLOCK]
            m = m.astype(BF)
            if factor is not None:
                m = m * jnp.asarray(factor, BF)
            out[:, n : n + BLOCK] = m

    def attend(low, high):
        left = iota((row_len, 128), 1) < HEAD_DIM
        for pair in range(low, high):
            cols = slice(128 * pair, 128 * pair + 128)
            qp, kp, vp = q_s[:, cols], k_s[:, cols], v_s[:, cols]
            found = []
            for keep in (left, jnp.logical_not(left)):
                s = dot_over_columns(jnp.where(keep, qp, jnp.zeros((), BF)), kp) + mask_s[...]
                e = jnp.exp(s - jnp.max(s, axis=1, keepdims=True))
                found.append(dot_plain(e.astype(BF), vp) * (1.0 / jnp.sum(e, axis=1, keepdims=True)))
            a_s[:, cols] = jnp.where(left, found[0], found[1]).astype(BF)

    def project():
        for n in range(0, D, BLOCK):
            b_s[:, n : n + BLOCK] = (
                x_ref[:, n : n + BLOCK].astype(F32)
                + dot_plain(a_s[...], wa[3, :, n : n + BLOCK])
                + state["bo"][:, n : n + BLOCK]
            )

        unit, _ = norm_parts(b_s[...])
        h = unit * state["g1"] + state["o1"]
        h_s[...] = h
        hl_s[...] = h.astype(BF)

    def up(j):
        for n in range(0, D, BLOCK):
            u = dot_plain(hl_s[...], wa[4 + j, :, n : n + BLOCK]) + state["cu"][j][:, n : n + BLOCK]
            g_s[j, :, n : n + BLOCK] = gelu_erf(u).astype(BF)

    def down(j):
        cols = slice(256 * j, 256 * j + 256)
        total = h_s[:, cols] + state["bd"][:, cols]
        for i in range(4):
            total = total + dot_plain(g_s[i], wd[j, D * i : D * i + D, :])
        b_s[:, cols] = total

    def finish():
        unit, _ = norm_parts(b_s[...])
        enc_ref[...] = (unit * state["g2"] + state["o2"]).astype(BF)

    def rows_attention():
        q_r = (dot_plain(x_low, wa[2]) + state["bq"]).astype(BF)
        state["q_r"] = q_r
        q_wide = (widen(q_r) * scaled).astype(BF)
        state["q_wide"] = q_wide
        s = jnp.where(open_keys, dot_over_columns(q_wide, k_s[...]), masked_score)
        e = jnp.exp(s - jnp.max(s, axis=1, keepdims=True))
        p = e * (1.0 / jnp.sum(e, axis=1, keepdims=True))
        state["p"] = p
        state["p_low"] = p.astype(BF)
        state["a_r"] = narrow(dot_plain(state["p_low"], v_s[...])).astype(BF)

    def rows_project():
        before = x_r_rows + dot_plain(state["a_r"], wa[3]) + state["bo"]
        unit, inverse = norm_parts(before)
        state["unit1"], state["inv1"] = unit, inverse
        state["h_r"] = unit * state["g1"] + state["o1"]
        state["hl_r"] = state["h_r"].astype(BF)
        state["u_r"], state["g_r"], state["f_r"] = [], [], []

    def rows_up(j):
        u = dot_plain(state["hl_r"], wa[4 + j]) + state["cu"][j]
        state["u_r"].append(u)
        state["g_r"].append(gelu_erf(u).astype(BF))

    def rows_down(j):
        f = jnp.zeros((ROW, 256), F32)
        for i in range(4):
            f = f + dot_plain(state["g_r"][i], wd[j, D * i : D * i + D, :])
        state["f_r"].append(f)

    def rows_finish():
        before = state["h_r"] + jnp.concatenate(state["f_r"], axis=1) + state["bd"]
        unit, inverse = norm_parts(before)
        state["unit2"], state["inv2"] = unit, inverse
        e = (unit * state["g2"] + state["o2"]).astype(BF)
        cls_own[...] = e[:SEGS, :]
        cls_all[z, plane] = e[:SEGS, :]

    def cls_z(r):
        peer = device(lax.rem(z + r, 4), x, y, c)
        return remote(cls_own, cls_all.at[z, plane], cz_s.at[r], cz_r.at[r], peer)

    def cls_plane(r):
        to = lax.rem(plane + r, 8)
        ref = cls_all.at[:, plane]
        return remote(ref, ref, cp_s.at[r], cp_r.at[r], (z * 2 + to // 4, lax.rem(to, 4)))

    xf, yf = x + (1 - c) * (1 - 2 * x), y + c * (1 - 2 * y)
    xg, yg = x + c * (1 - 2 * x), y + (1 - c) * (1 - 2 * y)
    to_f, to_g = device(z, xf, yf, c), device(z, xg, yg, c)
    wholes = ((src_q, fq_ref), (src_u, fu_ref), (src_a, fa_ref))
    sliced = ((src_e, se_ref), (src_g, sg_ref), (src_l, sl_ref))

    def slot(ref):
        return ref.at[tower, c, x, y, zi]

    def whole_z(i):
        src, dst = wholes[i]
        for r in (1, 2, 3):
            go(remote(src, slot(dst), fz_s.at[i, r], fz_r.at[i, r], device(lax.rem(z + r, 4), x, y, c)))
        copy = pltpu.make_async_copy(src, slot(dst), fl.at[i])
        copy.start()
        copy.wait()

    def whole_f(i):
        src, dst = wholes[i]
        for r in (1, 2, 3):
            arrived(slot(dst), fz_s.at[i, r], fz_r.at[i, r])
        ref = dst.at[:, c, x, y]
        go(remote(ref, ref, ff_s.at[i], ff_r.at[i], to_f))
        go(remote(ref, ref, fg_s.at[i, 0], fg_r.at[i, 0], to_g))

    def whole_g(i):
        dst = wholes[i][1]
        ref = dst.at[:, c, xf, yf]
        arrived(ref, ff_s.at[i], ff_r.at[i])
        go(remote(ref, ref, fg_s.at[i, 1], fg_r.at[i, 1], to_g))

    def whole_c(i):
        dst = wholes[i][1]
        for j in (0, 1):
            arrived(dst.at[:, c, xg, yg], fg_s.at[i, j], fg_r.at[i, j])
        ref = dst.at[:, c]
        go(remote(ref, ref, fc_s.at[i], fc_r.at[i], to_core))

    def whole_end(i):
        arrived(wholes[i][1].at[:, c], fc_s.at[i], fc_r.at[i])

    def slice_1(i):
        src, dst = sliced[i]
        for r in range(1, 8):
            there = lax.rem(place + r, 8)
            go(remote(src.at[there], slot(dst), s1_s.at[i, r], s1_r.at[i, r], (there, other)))
        copy = pltpu.make_async_copy(src.at[place], slot(dst), fl.at[3 + i])
        copy.start()
        copy.wait()

    def slice_2(i):
        dst = sliced[i][1]
        for r in range(1, 8):
            arrived(slot(dst), s1_s.at[i, r], s1_r.at[i, r])
        ref = dst.at[:, c, :, y]
        go(remote(ref, ref, s2_s.at[i], s2_r.at[i], to_y))

    def slice_3(i):
        dst = sliced[i][1]
        arrived(dst.at[:, c, :, y], s2_s.at[i], s2_r.at[i])
        ref = dst.at[:, c]
        go(remote(ref, ref, s3_s.at[i], s3_r.at[i], to_core))

    def slice_end(i):
        arrived(sliced[i][1].at[:, c], s3_s.at[i], s3_r.at[i])

    row16 = iota((ROW, D), 0)

    def top(rows):
        return jnp.where(row16[:, : rows.shape[1]] < SEGS, rows, 0.0)

    def pack_early():
        src_q[...] = top(state["q_r"].astype(F32)).astype(BF)
        hl_f32, a_f32, x_f32 = (top(m.astype(F32)) for m in (state["hl_r"], state["a_r"], x_low))
        three = hl_f32 + pltpu.roll(a_f32, 4, 0) + pltpu.roll(x_f32, 8, 0)
        z_rows = dot_plain(state["p_low"], x_ref[...])
        early = jnp.concatenate([three, z_rows], axis=0).astype(BF)
        early = dot_plain(early, sel_s[...]).astype(BF)
        for d in range(8):
            src_e[d] = early[:, 128 * d : 128 * d + 128]

    def pack_gelu():
        for d in range(8):
            packed = jnp.zeros((ROW, 128), F32)
            for b in range(3):
                first = 384 * d + 128 * b
                g = top(state["g_r"][first // D][:, first % D : first % D + 128].astype(F32))
                packed = packed + (pltpu.roll(g, 4 * b, 0) if b else g)
            src_g[d] = packed.astype(BF)

    after = {
        0: [lambda: small_vectors(), lambda: mix(0, k_s, None, None)],
        1: [lambda: mix(1, v_s, "bv", None)],
        2: [lambda: mix(2, q_s, "bq", scaled), rows_attention, lambda: attend(0, 2)],
        3: [rows_project, pack_early, lambda: slice_1(0), lambda: attend(2, 4)],
        4: [lambda: rows_up(0), lambda: attend(4, 6)],
        5: [lambda: rows_up(1), project, lambda: up(0)],
        6: [lambda: rows_up(2), lambda: up(1)],
        7: [lambda: rows_up(3), pack_gelu, lambda: up(2)],
        8: [lambda: rows_down(0), lambda: up(3), lambda: slice_2(0)],
        9: [lambda: rows_down(1), lambda: down(0)],
        10: [lambda: rows_down(2), rows_finish],
    }
    for i in range(kinds + 3):
        if i + WINDOW < kinds:
            stage0(i + WINDOW)
        if i < kinds:
            stage1(i)
        if 0 <= i - 1 < kinds:
            stage2(i - 1)
        if 0 <= i - 2 < kinds:
            stage3(i - 2)
        if 0 <= i - 3 < kinds:
            stage4(i - 3)
            for unit in after[i - 3]:
                unit()

    go(cls_z(1))
    go(cls_z(2))
    go(cls_z(3))
    whole_z(0)
    slice_1(1)
    down(1)
    for r in (1, 2, 3):
        cls_z(r).wait_recv()
    for r in range(1, 8):
        go(cls_plane(r))
    down(2)
    finish()

    keep_enc = pltpu.make_async_copy(enc_ref, enc_out, done.at[0])
    keep_enc.start()
    whole_f(0)
    slice_3(0)
    slice_2(1)
    for r in range(1, 8):
        cls_plane(r).wait_recv()
    for i in range(32):
        cls_f[SEGS * i : SEGS * i + SEGS, :] = cls_all[i // 8, i % 8].astype(F32)
    all_q, all_p = cls_f[:64, :].astype(BF), cls_f[64:, :].astype(BF)
    pair_scale = 2.0 * D ** (-0.5)
    logits = dot_over_columns(all_p, all_q) * pair_scale
    raised = jnp.exp(logits - jnp.max(logits, axis=0, keepdims=True))
    hit = jnp.where(iota((64, 64), 0) == pos_ref[...], 1.0, 0.0)
    d_logits = (raised / jnp.sum(raised, axis=0, keepdims=True) - hit).astype(BF)
    position = me * SEGS - tower * 64
    take = jnp.where((iota((ROW, 64), 1) == iota((ROW, 64), 0) + position) & (iota((ROW, 64), 0) < SEGS), 1.0, 0.0)
    take = take.astype(BF)
    d_q = dot_plain(dot_over_columns(take, d_logits).astype(BF), all_p)
    d_p = dot_plain(dot_plain(take, d_logits).astype(BF), all_q)
    d_cls = jnp.where(tower == 0, d_q, d_p) * pair_scale

    def total(rows):
        return jnp.sum(rows, axis=0, keepdims=True)

    vec_g2, vec_o2 = total(d_cls * state["unit2"]), total(d_cls)
    dz2 = norm_back(state["unit2"], state["inv2"], state["g2"], d_cls)
    df = dz2.astype(BF)
    dh = dz2
    du_rows = []
    for j in range(4):
        dg = jnp.zeros((ROW, D), F32)
        for i in range(3):
            dg = dg + dot_over_columns(df[:, 256 * i : 256 * i + 256], wd[i, D * j : D * j + D, :])
        du = (dg * gelu_slope(state["u_r"][j])).astype(BF)
        du_rows.append(du.astype(F32))
    packed = du_rows[0]
    for j in (1, 2, 3):
        packed = packed + pltpu.roll(du_rows[j], 4 * j, 0)
    src_u[...] = packed.astype(BF)
    whole_z(1)
    whole_g(0)
    for j in range(4):
        dh = dh + dot_over_columns(du_rows[j].astype(BF), wa[4 + j])
    vec_g1, vec_o1 = total(dh * state["unit1"]), total(dh)
    dz1 = norm_back(state["unit1"], state["inv1"], state["g1"], dh)
    db = dz1.astype(BF)
    slice_3(1)
    da = dot_over_columns(db, wa[3]).astype(BF)
    a_wide = widen(da).astype(BF)
    d_p_rows = dot_over_columns(a_wide, v_s[...])
    p = state["p"]
    ds = (p * (d_p_rows - jnp.sum(p * d_p_rows, axis=1, keepdims=True))).astype(BF)
    dq = narrow(dot_plain(ds, k_s[...]) * scaled).astype(BF)
    df_f, db_f, da_f, dq_f = (m.astype(F32) for m in (df, db, da, dq))
    src_a[...] = (df_f + pltpu.roll(db_f, 4, 0) + pltpu.roll(dq_f, 8, 0) + pltpu.roll(da_f, 12, 0)).astype(BF)
    whole_z(2)
    y_rows = dot_plain(ds, x_ref[...]) * scaled
    weight_sum = jnp.sum(state["p_low"].astype(F32), axis=1, keepdims=True)
    vec_bv = total(weight_sum * a_wide.astype(F32))
    vectors = jnp.concatenate(
        [total(dq_f), vec_bv, total(db_f), vec_o1, total(df_f), vec_o2, vec_g1, vec_g2, jnp.zeros((8, D), F32)], axis=0
    )
    late = jnp.concatenate([y_rows, vectors], axis=0).astype(BF)
    late = dot_plain(late, sel_s[...]).astype(BF)
    for d in range(8):
        src_l[d] = late[:, 128 * d : 128 * d + 128]

    slice_1(2)
    whole_f(1)
    whole_c(0)
    t_k = dot_over_columns(state["q_wide"], wa[0]).astype(BF)
    t_v = dot_over_columns(a_wide, wa[1]).astype(BF)
    at_rows = dz1 + dot_over_columns(dq, wa[2])
    high = at_rows.astype(BF)
    rest = (at_rows - high.astype(F32)).astype(BF)
    left = jnp.concatenate([ds, state["p_low"], spot, spot], axis=0)
    right = jnp.concatenate([t_k, t_v, high, rest], axis=0)
    whole_f(2)
    whole_g(1)
    for n in range(0, D, BLOCK):
        drow_ref[:, n : n + BLOCK] = dot_over_rows(left, right[:, n : n + BLOCK])
    keep_row = pltpu.make_async_copy(drow_ref, drow_out, done.at[1])
    keep_row.start()
    slice_2(2)
    whole_g(2)
    whole_c(1)
    slice_3(2)
    whole_c(2)
    for i in range(3):
        whole_end(i)
        slice_end(i)
    keep_enc.wait()
    keep_row.wait()

    for copy in sent:
        copy.wait_send()
    for k in range(kinds):

        @pl.when(inner == 1)
        def _():
            for j, zz in ((1, z_a), (2, z_b)):
                ref = full(k, zz, x, None, c)
                remote(ref, ref, rel_s.at[k, j - 1], z_r.at[k, j], to_near).wait_send()

    for i in range(1, 8):
        sv_copy(i).wait_send()


def grads_kernel(
    fq_ref, fu_ref, fa_ref, se_ref, sg_ref, sl_ref, enc_ref, drow_ref,
    enc_out, drow_out, mix_out, proj_out, up_out, down_out, upb_ref, rowb_ref, gain_ref,
    mix_ref, proj_ref, up_ref, down_ref, put,
):
    place = lax.axis_index("dp")
    kind = iota((256, 128), 0) % ROW
    part = 96
    wide_row, wide_col = iota((D, 256), 0), iota((D, 256), 1)
    first_of = wide_row // 48 * ROW + wide_row % SEGS
    take_q = jnp.where(wide_col == first_of, 1.0, 0.0).astype(BF)
    take_a = jnp.where(wide_col == first_of + 12, 1.0, 0.0).astype(BF)
    own_head = (iota((D, D), 0) % 48) // SEGS == iota((D, D), 1) // HEAD_DIM
    kind16, col16 = iota((256, ROW), 0) % ROW, iota((256, ROW), 1)
    again_row, again_col = iota((256, 256), 0), iota((256, 256), 1)
    again = jnp.where(again_col == again_row // ROW * ROW + again_row % SEGS, 1.0, 0.0).astype(BF)
    stores = []

    def store(src, dst):
        copy = pltpu.make_async_copy(src, dst, put.at[len(stores)])
        copy.start()
        stores.append(copy)

    store(enc_ref, enc_out)
    store(drow_ref, drow_out)

    def keep(rows, lo, hi):
        return jnp.where((kind >= lo) & (kind < hi), rows, jnp.zeros((), BF))

    three = [se_ref[t, :, 0:16, :].reshape(256, 128) for t in range(2)]
    for t in range(2):
        four = dot_plain(again, three[t]).astype(BF)
        for j in range(4):
            cols = slice(FF * t + D * j, FF * t + D * j + D)
            up_ref[:, cols] = dot_over_rows(keep(four, 4 * j, 4 * j + 4), fu_ref[t])[:part]
            store(up_ref.at[:, cols], up_out.at[:, cols])
    up_bias = jnp.zeros((ROW, 384), F32)
    for t in range(2):
        mine = fu_ref[t, :, pl.ds(pl.multiple_of(place % 2 * 384, 128), 384)]
        to_up = jnp.where((kind16 // 4 == place // 2) & (col16 == t), 1.0, 0.0).astype(BF)
        up_bias = up_bias + dot_over_rows(to_up, mine)
    upb_ref[...] = up_bias[:2]
    for t in range(2):
        fa = fa_ref[t]
        cols = slice(D * t, D * t + D)
        proj_ref[:, cols] = dot_over_rows(keep(three[t], 4, 8), fa)[:part]
        store(proj_ref.at[:, cols], proj_out.at[:, cols])
        first = slice(3 * D * t, 3 * D * t + D)
        mix_ref[:, first] = dot_over_rows(keep(three[t], 8, 12), fa)[:part]
        store(mix_ref.at[:, first], mix_out.at[:, first])
        df = dot_plain(again, fa).astype(BF)
        g = sg_ref[t].reshape(256, 128)
        for b in range(3):
            at = slice(128 * b, 128 * b + 128)
            down_ref[at, cols] = dot_over_rows(keep(g, 4 * b, 4 * b + 4), df)
        store(down_ref.at[:, cols], down_out.at[:, cols])
    for t in range(2):
        a_wide = jnp.where(own_head, dot_plain(take_a, fa_ref[t]), 0.0).astype(BF)
        gv = dot_over_rows(se_ref[t, :, 16:64, :].reshape(D, 128), a_wide)
        cols = slice(3 * D * t + 2 * D, 3 * D * t + 3 * D)
        mix_ref[:, cols] = gv[:part]
        store(mix_ref.at[:, cols], mix_out.at[:, cols])
    biases = jnp.zeros((ROW, 128), F32)
    gains = jnp.zeros((ROW, 128), F32)
    for t in range(2):
        q_wide = jnp.where(own_head, dot_plain(take_q, fq_ref[t]), 0.0).astype(BF)
        gk = dot_over_rows(sl_ref[t, :, 0:48, :].reshape(D, 128), q_wide)
        cols = slice(3 * D * t + D, 3 * D * t + 2 * D)
        mix_ref[:, cols] = gk[:part]
        store(mix_ref.at[:, cols], mix_out.at[:, cols])
        vec = sl_ref[t, :, 48:64, :].reshape(256, 128)
        to_bias = jnp.where((kind16 < 6) & (col16 == kind16 + 6 * t), 1.0, 0.0).astype(BF)
        to_gain = jnp.where((kind16 >= 6) & (kind16 < 8) & (col16 == kind16 - 6 + 2 * t), 1.0, 0.0).astype(BF)
        biases = biases + dot_over_rows(to_bias, vec)
        gains = gains + dot_over_rows(to_gain, vec)
    rowb_ref[...] = biases[:12, :part]
    gain_ref[...] = gains[:4, :part]
    for copy in stores:
        copy.wait()


def fast_device(text_rows, text_segments, positives, w_mix, w_proj, w_up, w_down, b_up, b_rows, g_rows):
    sem = pltpu.SemaphoreType.DMA
    vm = pltpu.VMEM
    part = b_rows.shape[0]
    kinds = len(PIECES)
    fulls = jax.ShapeDtypeStruct((2, 2, 2, 2, 2, ROW, D), BF)
    row_len = text_rows.shape[1]
    here, there = pl.BlockSpec(memory_space=vm), pl.BlockSpec(memory_space=pl.ANY)
    slices = lambda r: jax.ShapeDtypeStruct((2, 2, 2, 2, 2, r, 128), BF)
    encoded, d_rows, fq, fu, fa, se, sg, sl = pl.pallas_call(
        main_kernel,
        out_shape=[
            jax.ShapeDtypeStruct((row_len, D), BF),
            jax.ShapeDtypeStruct((row_len, D), F32),
            fulls, fulls, fulls, slices(64), slices(ROW), slices(64),
        ],
        in_specs=[pl.BlockSpec(memory_space=pltpu.HBM)] * 10,
        out_specs=[there] * 2 + [here] * 6,
        scratch_shapes=[
            vm((row_len, D), BF), vm((1, row_len), jnp.int32), vm((1, 64), jnp.int32),
            vm((2, 384), BF), vm((12, 96), BF), vm((4, 96), BF), sem((6,)),
            vm((row_len, D), BF), vm((row_len, D), F32),
            vm((8, D, D), BF), vm((3, FF, 256), BF),
            vm((2, ROW, 384), F32), vm((2, ROW, 384), BF), vm((8, ROW, 384), BF),
            vm((row_len, D), BF), vm((row_len, D), BF), vm((row_len, D), BF), vm((row_len, D), BF),
            vm((row_len, row_len), F32), vm((row_len, D), F32), vm((row_len, D), F32), vm((row_len, D), BF),
            vm((4, row_len, D), BF), vm((D, 1024), BF),
            vm((SEGS, D), BF), vm((4, 8, SEGS, D), BF), vm((128, D), F32),
            vm((ROW, D), BF), vm((ROW, D), BF), vm((ROW, D), BF),
            vm((8, 64, 128), BF), vm((8, ROW, 128), BF), vm((8, 64, 128), BF),
            sem((kinds,)), sem((kinds,)), sem((kinds,)), sem((kinds, 3)), sem((kinds, 2)),
            sem((kinds, 4)), sem((kinds, 4)), sem((kinds, 4)), sem((kinds, 4)), sem((kinds,)), sem((kinds,)),
            sem((8,)), sem((8,)), sem((4,)), sem((4,)), sem((8,)), sem((8,)), sem((2,)),
            sem((6,)), sem((3, 4)), sem((3, 4)), sem((3,)), sem((3,)), sem((3, 2)), sem((3, 2)), sem((3,)), sem((3,)),
            sem((3, 8)), sem((3, 8)), sem((3,)), sem((3,)), sem((3,)), sem((3,)),
        ],
        compiler_params=pltpu.CompilerParams(collective_id=5, has_side_effects=True, vmem_limit_bytes=44 << 20),
        name="main_step",
    )(*(pltpu.with_memory_space_constraint(m, pltpu.HBM) for m in (text_rows[0], text_segments, positives[None, :], b_up.T, b_rows.T, g_rows.T, w_mix, w_proj, w_up, w_down)))
    shape = lambda r, n: jax.ShapeDtypeStruct((r, n), F32)
    grads = pl.pallas_call(
        grads_kernel,
        out_shape=[
            jax.ShapeDtypeStruct((row_len, D), BF), shape(row_len, D),
            shape(part, 6 * D), shape(part, 2 * D), shape(part, 2 * FF), shape(4 * part, 2 * D),
            shape(2, 4 * part), shape(12, part), shape(4, part),
        ],
        in_specs=[here] * 8,
        out_specs=[there] * 6 + [here] * 3,
        scratch_shapes=[
            vm((part, 6 * D), F32), vm((part, 2 * D), F32), vm((part, 2 * FF), F32), vm((4 * part, 2 * D), F32),
            sem((20,)),
        ],
        compiler_params=pltpu.CompilerParams(vmem_limit_bytes=24 << 20),
        name="weight_grads",
    )(
        fq.reshape(2, 256, D), fu.reshape(2, 256, D), fa.reshape(2, 256, D),
        se.reshape(2, 16, 64, 128), sg.reshape(2, 16, ROW, 128), sl.reshape(2, 16, 64, 128), encoded, d_rows,
    )
    encoded, d_rows, mix, proj, up, down, up_b, row_b, gain = grads
    return encoded[None], d_rows[None], mix, proj, up, down, up_b.T, row_b.T, gain.T


def solution(mesh):
    rows, cols = P(("dp", "outer"), None, None), P("dp", None)
    sizes = (mesh.shape["dp"], mesh.shape["outer"])
    return jax.shard_map(
        fast_device if sizes == (8, 4) else per_device,
        mesh=mesh,
        in_specs=(rows, P(("dp", "outer"), None), P(), cols, cols, cols, cols, cols, cols, cols),
        out_specs=(rows, rows, cols, cols, cols, cols, cols, cols, cols),
        check_vma=False,
    )
```

```python
import functools

import jax
import jax.numpy as jnp
from jax import lax
from jax.experimental import pallas as pl
from jax.experimental.pallas import tpu as pltpu
from jax.sharding import PartitionSpec as P

D = 768
HEADS = 12
HEAD_DIM = 64
FF = 3072
SEGS = 4
BF = jnp.bfloat16
F32 = jnp.float32
MESH = pl.DeviceIdType.MESH

masked_score = -1e30
layer_eps = 1e-05


def dot_plain(left, right):
    return jnp.dot(left, right, preferred_element_type=F32)


def dot_over_rows(left, right):
    return lax.dot_general(left, right, (((0,), (0,)), ((), ())), preferred_element_type=F32)


def dot_over_columns(left, right):
    return lax.dot_general(left, right, (((1,), (1,)), ((), ())), preferred_element_type=F32)


def gelu_exact(inputs):
    return jax.nn.gelu(inputs, approximate=False)


def norm_parts(inputs):
    center = inputs - jnp.mean(inputs, axis=-1, keepdims=True)
    inverse = lax.rsqrt(jnp.mean(center * center, axis=-1, keepdims=True) + layer_eps)
    return center * inverse, inverse


def norm_back(unit, inverse, gain, grad):
    scaled = gain * grad
    return inverse * (
        scaled
        - jnp.mean(scaled, axis=-1, keepdims=True)
        - unit * jnp.mean(scaled * unit, axis=-1, keepdims=True)
    )


def gather_weights(weights, widths, n_dp):
    tower = lax.axis_index("dp") * 2 // n_dp
    whole = [lax.all_gather(w, "dp", axis=0, tiled=True) for w in weights]
    return [lax.dynamic_slice_in_dim(w, tower * n, n, 1) for w, n in zip(whole, widths)]


def spread_kernel(n_outer, total, whole_ref, parts_ref, all_ref, sliced_ref, local, s_one, r_one, s_two, r_two):
    dp, outer = lax.axis_index("dp"), lax.axis_index("outer")
    me = dp * n_outer + outer
    barrier = pltpu.get_barrier_semaphore()

    def greet(i, carry):
        peer = lax.rem(me + i, total)
        pl.semaphore_signal(barrier, inc=1, device_id=(peer // n_outer, lax.rem(peer, n_outer)), device_id_type=MESH)
        return carry

    lax.fori_loop(1, total, greet, 0)
    pl.semaphore_wait(barrier, total - 1)

    def copies(i):
        peer = lax.rem(me + i, total)
        there = peer // n_outer
        device = (there, lax.rem(peer, n_outer))
        one = pltpu.make_async_remote_copy(
            src_ref=whole_ref, dst_ref=all_ref.at[me], send_sem=s_one.at[i], recv_sem=r_one.at[i],
            device_id=device, device_id_type=MESH,
        )
        if parts_ref is None:
            return (one,)
        two = pltpu.make_async_remote_copy(
            src_ref=parts_ref.at[there], dst_ref=sliced_ref.at[me], send_sem=s_two.at[i], recv_sem=r_two.at[i],
            device_id=device, device_id_type=MESH,
        )
        return (one, two)

    def send(i, carry):
        for copy in copies(i):
            copy.start()
        return carry

    lax.fori_loop(1, total, send, 0)
    own = [pltpu.make_async_copy(whole_ref, all_ref.at[me], local.at[0])]
    if parts_ref is not None:
        own.append(pltpu.make_async_copy(parts_ref.at[dp], sliced_ref.at[me], local.at[1]))
    for copy in own:
        copy.start()

    def settle(i, carry):
        for copy in copies(i):
            copy.wait()
        return carry

    lax.fori_loop(1, total, settle, 0)
    for copy in own:
        copy.wait()


def spread(whole, parts, n_dp, n_outer, identity):
    total = n_dp * n_outer
    sem = pltpu.SemaphoreType.DMA
    out_shape = [jax.ShapeDtypeStruct((total,) + whole.shape, whole.dtype)]
    operands = [whole]
    if parts is not None:
        out_shape.append(jax.ShapeDtypeStruct((total,) + parts.shape[1:], parts.dtype))
        operands.append(parts)
        kernel = functools.partial(spread_kernel, n_outer, total)
        scratch = [sem((2,))] + [sem((total,))] * 4
    else:
        def kernel(w, a, local, s, r):
            spread_kernel(n_outer, total, w, None, a, None, local, s, r, None, None)
        scratch = [sem((2,))] + [sem((total,))] * 2
    return pl.pallas_call(
        kernel,
        out_shape=out_shape,
        in_specs=[pl.BlockSpec(memory_space=pltpu.VMEM)] * len(operands),
        out_specs=[pl.BlockSpec(memory_space=pltpu.VMEM)] * len(out_shape),
        scratch_shapes=scratch,
        compiler_params=pltpu.CompilerParams(
            collective_id=identity, has_side_effects=True, vmem_limit_bytes=48 << 20
        ),
        name="spread%d" % identity,
    )(*operands)


def expand_heads(rows):
    head_of = jnp.arange(D, dtype=jnp.int32) // HEAD_DIM
    keep = head_of[None, :] == jnp.arange(HEADS, dtype=jnp.int32)[:, None]
    return jnp.where(keep[:, None, :], rows[None], 0).reshape(HEADS * rows.shape[0], D)


def per_device(text_rows, text_segments, positives, w_mix, w_proj, w_up, w_down, b_up, b_rows, g_rows):
    n_dp, n_outer = lax.axis_size("dp"), lax.axis_size("outer")
    total = n_dp * n_outer
    own_index = lax.axis_index(("dp", "outer"))
    tower = own_index * 2 // total
    rows_in, segments = text_rows[0], text_segments[0]
    row_len = rows_in.shape[0]
    widths = (3 * D, D, FF, D)
    wm, wp, wu, wd = gather_weights((w_mix, w_proj, w_up, w_down), widths, n_dp)
    part_f, part_d = b_up.shape[0], b_rows.shape[0]
    small = jnp.concatenate([b_up.reshape(part_f // part_d, part_d, 2).transpose(0, 2, 1).reshape(-1, part_d), b_rows.T, g_rows.T], axis=0)
    small = lax.all_gather(small, "dp", axis=0)
    split = 2 * (part_f // part_d)
    up_b = small[:, :split].reshape(n_dp, part_f // part_d, 2, part_d).transpose(2, 0, 1, 3).reshape(2, FF)
    row_b = small[:, split : split + 12].transpose(1, 0, 2).reshape(2, 6, D)
    gain_b = small[:, split + 12 :].transpose(1, 0, 2).reshape(2, 2, D)
    pick = lambda both_towers: jnp.where(tower == 0, both_towers[0], both_towers[1]).astype(F32)
    c_up, biases, gains = pick(up_b), pick(row_b), pick(gain_b)
    bq, bv, bo, o1, bd, o2 = (biases[i] for i in range(6))
    g1, g2 = gains[0], gains[1]

    scaled = HEAD_DIM ** (-0.5)
    mixed = (dot_plain(rows_in, wm) + jnp.concatenate([bq, jnp.zeros_like(bq), bv])).astype(BF)
    q, k, v = mixed[:, :D], mixed[:, D : 2 * D], mixed[:, 2 * D :]
    allowed = segments[:, None] == segments[None, :]
    heads = lambda m: m.reshape(row_len, HEADS, HEAD_DIM)
    scores = jnp.einsum("qhe,khe->hqk", heads(q), heads(k), preferred_element_type=F32) * scaled
    scores = jnp.where(allowed[None], scores, masked_score)
    top = jnp.max(scores, axis=-1, keepdims=True)
    raised = jnp.exp(scores - top)
    chances = (raised / jnp.sum(raised, axis=-1, keepdims=True)).astype(BF)
    attended = jnp.einsum("hqk,khe->qhe", chances, heads(v), preferred_element_type=F32).reshape(row_len, D).astype(BF)
    before_one = rows_in.astype(F32) + dot_plain(attended, wp) + bo
    unit_one, inv_one = norm_parts(before_one)
    h1 = unit_one * g1 + o1
    h1_low = h1.astype(BF)
    up_pre = dot_plain(h1_low, wu) + c_up
    gelu_low = gelu_exact(up_pre).astype(BF)
    before_two = h1 + dot_plain(gelu_low, wd) + bd
    unit_two, inv_two = norm_parts(before_two)
    encoded = unit_two * g2 + o2

    levels = jnp.arange(SEGS, dtype=jnp.int32)
    starts = jnp.sum((segments[None, :] < levels[:, None]).astype(jnp.int32), axis=1)
    at = lambda m: jnp.take(m, starts, axis=0)
    vectors = at(encoded).astype(BF)
    all_cls = spread(vectors, None, n_dp, n_outer, 2)[0].reshape(total * SEGS, D)
    texts = total * SEGS // 2
    all_q, all_p = all_cls[:texts], all_cls[texts:]
    pair_scale = 2.0 * D ** (-0.5)
    logits = dot_over_columns(all_q, all_p) * pair_scale
    raised_l = jnp.exp(logits - jnp.max(logits, axis=1, keepdims=True))
    hit = (positives[:, None] == jnp.arange(texts, dtype=jnp.int32)[None, :]).astype(F32)
    d_logits = (raised_l / jnp.sum(raised_l, axis=1, keepdims=True) - hit).astype(BF)
    position = own_index * SEGS - tower * texts
    d_q = dot_plain(lax.dynamic_slice_in_dim(d_logits, position, SEGS, 0), all_p)
    d_p = dot_over_rows(lax.dynamic_slice_in_dim(d_logits, position, SEGS, 1), all_q)
    d_cls = jnp.where(tower == 0, d_q, d_p) * pair_scale

    ut, it = at(unit_two), at(inv_two)
    dg2, do2 = jnp.sum(d_cls * ut, axis=0), jnp.sum(d_cls, axis=0)
    dz2 = norm_back(ut, it, g2, d_cls)
    df = dz2.astype(BF)
    dg = dot_over_columns(df, wd)
    u_r = at(up_pre)
    _, gelu_back = jax.vjp(gelu_exact, u_r)
    du = gelu_back(dg)[0].astype(BF)
    dh1 = dz2 + dot_over_columns(du, wu)
    uo, io = at(unit_one), at(inv_one)
    dg1, do1 = jnp.sum(dh1 * uo, axis=0), jnp.sum(dh1, axis=0)
    dz1 = norm_back(uo, io, g1, dh1)
    db = dz1.astype(BF)
    da = dot_over_columns(db, wp).astype(BF)
    q_r = at(q)
    q_wide, a_wide = expand_heads(q_r), expand_heads(da)
    own_segment = jnp.tile(levels, HEADS)
    open_keys = own_segment[:, None] == segments[None, :]
    s_r = jnp.where(open_keys, dot_over_columns(q_wide, k) * scaled, masked_score)
    e_r = jnp.exp(s_r - jnp.max(s_r, axis=-1, keepdims=True))
    p_r = e_r / jnp.sum(e_r, axis=-1, keepdims=True)
    pl_r = p_r.astype(BF)
    dp_r = dot_over_columns(a_wide, v)
    ds_r = (p_r * (dp_r - jnp.sum(p_r * dp_r, axis=-1, keepdims=True))).astype(BF)
    dq_wide = dot_plain(ds_r, k).reshape(HEADS, SEGS, HEADS, HEAD_DIM)
    dq = (jnp.einsum("hshe->she", dq_wide).reshape(SEGS, D) * scaled).astype(BF)
    y_r = (dot_plain(ds_r, rows_in) * scaled).astype(BF)
    z_r = dot_plain(pl_r, rows_in).astype(BF)
    weight_sum = jnp.sum(pl_r.astype(F32), axis=1, keepdims=True)
    dbv = jnp.sum(weight_sum * a_wide.astype(F32), axis=0)
    t_k = (dot_over_columns(q_wide, wm[:, D : 2 * D]) * scaled).astype(BF)
    t_v = dot_over_columns(a_wide, wm[:, 2 * D :]).astype(BF)
    d_rows = dot_over_rows(jnp.concatenate([ds_r, pl_r], axis=0), jnp.concatenate([t_k, t_v], axis=0))
    d_rows_at = dz1 + dot_over_columns(dq, wm[:, :D])
    spot = (starts[:, None] == jnp.arange(row_len, dtype=jnp.int32)[None, :])
    for s in range(SEGS):
        d_rows = d_rows + jnp.where(spot[s][:, None], d_rows_at[s][None, :], 0.0)

    ff_rows = SEGS * FF // D
    whole = jnp.concatenate(
        [df, db, dq, q_r, da, du.reshape(ff_rows, D), jnp.stack([dbv, do1, do2, dg1, dg2]).astype(BF), jnp.zeros((3, D), BF)],
        axis=0,
    )
    g_r, h_r, at_r, x_r = at(gelu_low), at(h1_low), at(attended), at(rows_in)
    by_part = lambda m: m.reshape(m.shape[0], n_dp, m.shape[1] // n_dp).transpose(1, 0, 2)
    parts = jnp.concatenate(
        [by_part(h_r), by_part(at_r), by_part(x_r), by_part(y_r), by_part(z_r),
         by_part(g_r).reshape(n_dp, -1, part_d)],
        axis=1,
    )
    all_w, all_s = spread(whole, parts, n_dp, n_outer, 3)
    half = total // 2
    tw = all_w.reshape(2, half, -1, D)
    ts = all_s.reshape(2, half, -1, part_d)
    rank = lambda m: m.reshape(half * SEGS, -1)
    grads = []
    outs = [[], [], [], []]
    vec_b, vec_g, vec_u = [], [], []
    mine = lax.axis_index("dp")
    for t in range(2):
        w, s = tw[t], ts[t]
        df_a, db_a, dq_a, q_a, da_a = (rank(w[:, 4 * i : 4 * i + 4]) for i in range(5))
        du_a = w[:, 20 : 20 + ff_rows].reshape(half * SEGS, FF)
        vec = jnp.sum(w[:, 20 + ff_rows : 25 + ff_rows].astype(F32), axis=0)
        h_a, at_a, x_a = (rank(s[:, 4 * i : 4 * i + 4]) for i in range(3))
        y_a = s[:, 12:60].reshape(half, HEADS, SEGS, part_d)
        z_a = s[:, 60:108].reshape(half, HEADS, SEGS, part_d)
        g_a = s[:, 108:].reshape(half * SEGS, part_f)
        by_head = lambda m: m.reshape(half, SEGS, HEADS, HEAD_DIM)
        gk = jnp.einsum("rhsa,rshe->ahe", y_a, by_head(q_a), preferred_element_type=F32).reshape(part_d, D)
        gv = jnp.einsum("rhsa,rshe->ahe", z_a, by_head(da_a), preferred_element_type=F32).reshape(part_d, D)
        outs[0] += [dot_over_rows(x_a, dq_a), gk, gv]
        outs[1].append(dot_over_rows(at_a, db_a))
        outs[2].append(dot_over_rows(h_a, du_a))
        outs[3].append(dot_over_rows(g_a, df_a))
        col = lambda m, n: lax.dynamic_slice_in_dim(m, mine * n, n, 0)
        summed = lambda m: jnp.sum(m.astype(F32), axis=0)
        vec_b += [col(m, part_d) for m in (summed(dq_a), vec[0], summed(db_a), vec[1], summed(df_a), vec[2])]
        vec_g += [col(m, part_d) for m in (vec[3], vec[4])]
        vec_u.append(col(summed(du_a), part_f))
    return (
        encoded.astype(BF)[None],
        d_rows[None],
        jnp.concatenate(outs[0], axis=1),
        jnp.concatenate(outs[1], axis=1),
        jnp.concatenate(outs[2], axis=1),
        jnp.concatenate(outs[3], axis=1),
        jnp.stack(vec_u, axis=1),
        jnp.stack(vec_b, axis=1),
        jnp.stack(vec_g, axis=1),
    )


PIECES = (
    [(0, D, D), (0, 2 * D, D), (0, 0, D), (1, 0, D)]
    + [(2, D * i, D) for i in range(4)]
    + [(3, 256 * i, 256) for i in range(3)]
)
WIDTHS = (3 * D, D, FF, D)
THIN = (2, 5, 8)
ROW = 16
BLOCK = 256


def iota(shape, dim):
    return lax.broadcasted_iota(jnp.int32, shape, dim)


def gelu_erf(u):
    return 0.5 * u * (1.0 + lax.erf(u * 0.7071067811865476))


def gelu_slope(u):
    return 0.5 * (1.0 + lax.erf(u * 0.7071067811865476)) + u * (0.3989422804014327 * jnp.exp(-0.5 * u * u))


def main_kernel(
    x_in, seg_in, pos_in, bu_in, br_in, gr_in, w_mix, w_proj, w_up, w_down,
    enc_out, drow_out, fq_ref, fu_ref, fa_ref, fb_ref, se_ref, sg_ref, sl_ref,
    x_ref, seg_ref, pos_ref, bu_ref, br_ref, gr_ref, first, enc_ref, drow_ref, wa, wd, sv_f, sv_ref, sv_all, q_s, k_s, v_s, a_s, mask_s, b_s, h_s, hl_s, g_s, sel_s,
    cls_own, cls_all, cls_f, src_q, src_u, src_a, src_b, src_e, src_g, src_l,
    ld, far_s, near_s, z_r, rel_s, x_s, x_r, y_s, y_r, c_s, c_r, o_s, o_r, sv_sem, sv_r, cz_s, cz_r, cp_s, cp_r, done,
    fl, fz_s, fz_r, ff_s, ff_r, fg_s, fg_r, fc_s, fc_r, s1_s, s1_r, s2_s, s2_r, s3_s, s3_r,
):
    sources = (w_mix, w_proj, w_up, w_down)
    place, other = lax.axis_index("dp"), lax.axis_index("outer")
    z, x = place // 2, place % 2
    y, c = other // 2, other % 2
    tower, zi = z // 2, z % 2
    me = place * 4 + other
    inner = zi * (1 - tower) + (1 - zi) * tower
    zn = z + 1 - 2 * zi
    z_a, z_b = 2 - tower, 3 - 3 * tower
    scaled = HEAD_DIM ** (-0.5)
    row_len = x_ref.shape[0]

    def device(zz, xx, yy, cc):
        return (zz * 2 + xx, yy * 2 + cc)

    plane = x * 4 + other
    to_near, to_far = device(zn, x, y, c), device(z_a, x, y, c)
    to_x, to_y, to_core = device(z, 1 - x, y, c), device(z, x, 1 - y, c), device(z, x, y, 1 - c)

    loads = []
    pairs = ((bu_in, bu_ref), (br_in, br_ref), (gr_in, gr_ref), (seg_in, seg_ref), (pos_in, pos_ref), (x_in, x_ref))
    for i, (src, dst) in enumerate(pairs):
        loads.append(pltpu.make_async_copy(src, dst, first.at[i]))
        loads[-1].start()
    barrier = pltpu.get_barrier_semaphore()

    greeted = [device(lax.rem(z + r, 4), x, y, c) for r in (1, 2, 3)]
    greeted += [device(lax.rem(z + r, 4), 1 - x, y, c) for r in (1, 2, 3)]
    for r in range(1, 8):
        to = lax.rem(plane + r, 8)
        greeted.append((z * 2 + to // 4, lax.rem(to, 4)))
    for peer in greeted:
        pl.semaphore_signal(barrier, inc=1, device_id=peer, device_id_type=MESH)
    pl.semaphore_wait(barrier, len(greeted))

    def remote(src, dst, s, r, peer):
        return pltpu.make_async_remote_copy(
            src_ref=src, dst_ref=dst, send_sem=s, recv_sem=r, device_id=peer, device_id_type=MESH
        )

    def arrived(ref, s, r):
        remote(ref, ref, s, r, to_x).wait_recv()

    state_sent = []

    def go(copy):
        copy.start()
        state_sent.append(copy)

    def dims(k):
        tensor, first, cols = PIECES[k]
        return tensor, sources[tensor].shape[0], first, cols

    def own(k, which, half_row, half_col):
        tensor, r, first, n = dims(k)
        row, rows = (0, r) if half_row is None else (half_row * (r // 2), r // 2)
        col, cols = which * WIDTHS[tensor] + first, n
        if half_col is not None:
            col, cols = col + half_col * (n // 2), n // 2
        return sources[tensor].at[
            pl.ds(pl.multiple_of(row, 16), rows), pl.ds(pl.multiple_of(col, 128), cols)
        ]

    def held(k):
        return wa.at[k] if k < 8 else wd.at[k - 8]

    def full(k, zz, xx, half_row, half_col):
        tensor, r, first, n = dims(k)
        row, rows = (zz * 2 + xx) * r, r
        if half_row is not None:
            row, rows = row + half_row * (r // 2), r // 2
        col, cols = (0, n) if half_col is None else (pl.multiple_of(half_col * (n // 2), 128), n // 2)
        return held(k).at[pl.ds(pl.multiple_of(row, 16), rows), pl.ds(col, cols)]

    planes = (z, zn, z_a, z_b)
    kinds = len(PIECES)
    local = []

    def stage0(k):
        go(remote(own(k, 1 - tower, None, c), full(k, z, x, None, c), far_s.at[k], z_r.at[k, 2 - inner], to_far))
        go(remote(own(k, tower, y, c), full(k, z, x, y, c), near_s.at[k], z_r.at[k, 0], to_near))
        go(remote(own(k, tower, None, c), full(k, z, x, None, c), x_s.at[k, 0], x_r.at[k, 0], to_x))
        copy = pltpu.make_async_copy(own(k, tower, None, c), full(k, z, x, None, c), ld.at[k])
        copy.start()
        local.append(copy)

    def stage1(k):
        ref = full(k, zn, x, y, c)
        arrived(ref, near_s.at[k], z_r.at[k, 0])
        go(remote(ref, ref, x_s.at[k, 1], x_r.at[k, 1], to_x))
        go(remote(ref, ref, y_s.at[k, 0], y_r.at[k, 0], to_y))
        for j, zz in ((1, z_a), (2, z_b)):
            whole, part = full(k, zz, x, None, c), full(k, zz, x, y, c)
            passed = part if k in THIN else whole

            @pl.when(inner == 1)
            def _():
                arrived(whole, near_s.at[k], z_r.at[k, j])
                remote(passed, passed, rel_s.at[k, j - 1], z_r.at[k, j], to_near).start()

            @pl.when(inner == 0)
            def _():
                arrived(passed, near_s.at[k], z_r.at[k, j])
                if k in THIN:
                    remote(part, part, o_s.at[k, j - 1], o_r.at[k, j - 1], to_y).start()

            go(remote(part, part, x_s.at[k, 1 + j], x_r.at[k, 1 + j], to_x))

    def stage2(k):
        arrived(full(k, z, 1 - x, None, c), x_s.at[k, 0], x_r.at[k, 0])
        for j in (1, 2, 3):
            ref = full(k, planes[j], 1 - x, y, c)
            arrived(ref, x_s.at[k, j], x_r.at[k, j])
            go(remote(ref, ref, y_s.at[k, j], y_r.at[k, j], to_y))

    def stage3(k):
        arrived(full(k, zn, x, 1 - y, c), y_s.at[k, 0], y_r.at[k, 0])
        for j in (1, 2, 3):
            arrived(full(k, planes[j], 1 - x, 1 - y, c), y_s.at[k, j], y_r.at[k, j])
        if k in THIN:

            @pl.when(inner == 0)
            def _():
                for j, zz in ((1, z_a), (2, z_b)):
                    arrived(full(k, zz, x, 1 - y, c), o_s.at[k, j - 1], o_r.at[k, j - 1])

        local[k].wait()
        n = dims(k)[3]
        ref = held(k).at[:, pl.ds(pl.multiple_of(c * (n // 2), 128), n // 2)]
        go(remote(ref, ref, c_s.at[k], c_r.at[k], to_core))

    def stage4(k):
        n = dims(k)[3]
        ref = held(k).at[:, pl.ds(pl.multiple_of((1 - c) * (n // 2), 128), n // 2)]
        arrived(ref, c_s.at[k], c_r.at[k])

    def sv_copy(i):
        there = lax.rem(place + i, 8)
        return remote(sv_ref.at[there // 4], sv_all.at[place], sv_sem.at[i], sv_r.at[i], (there, other))

    WINDOW = 2
    for k in range(WINDOW):
        stage0(k)
    for copy in loads:
        copy.wait()
    sv_f[...] = jnp.zeros_like(sv_f)
    for t in range(2):
        sv_f[t, 0:1, :] = bu_ref[...].astype(F32)[t : t + 1]
        sv_f[t, 1:7, 0:96] = br_ref[...].astype(F32)[6 * t : 6 * t + 6]
        sv_f[t, 7:9, 0:96] = gr_ref[...].astype(F32)[2 * t : 2 * t + 2]
    sv_ref[...] = sv_f[...].astype(BF)

    for i in range(1, 8):
        sv_copy(i).start()
    sv_all[place] = sv_ref[tower]

    sel_row, sel_col = iota((D, 1024), 0), iota((D, 1024), 1)
    lane = sel_col % 128
    sel_s[...] = jnp.where((sel_row == (sel_col // 128) * 96 + lane) & (lane < 96), 1.0, 0.0).astype(BF)
    segments = seg_ref[...]
    level = iota((ROW, row_len), 0)
    begin = jnp.sum(jnp.where(segments < level, 1.0, 0.0), axis=1, keepdims=True).astype(jnp.int32)
    spot = jnp.where((iota((ROW, row_len), 1) == begin) & (level < SEGS), 1.0, 0.0).astype(BF)
    belongs = jnp.where((segments == level) & (level < SEGS), 1.0, 0.0).astype(BF)
    mask_s[...] = (dot_over_rows(belongs, belongs) - 1.0) * -masked_score
    wide_row, wide_col = iota((48, D), 0), iota((48, D), 1)
    own_head = (wide_row // SEGS) == (wide_col // HEAD_DIM)
    repeat = jnp.where(iota((48, ROW), 0) % SEGS == iota((48, ROW), 1), 1.0, 0.0).astype(BF)
    open_keys = (iota((48, row_len), 0) % SEGS) == segments
    x_r_rows = dot_plain(spot, x_ref[...])
    x_low = x_r_rows.astype(BF)

    def widen(rows):
        return jnp.where(own_head, dot_plain(repeat, rows), 0.0)

    def narrow(wide):
        return dot_over_rows(repeat, jnp.where(own_head, wide, 0.0).astype(BF))

    state = {}

    def small_vectors():
        for i in range(1, 8):
            sv_copy(i).wait_recv()
        rows = jnp.zeros((ROW, D), F32)
        for m in range(8):
            put = jnp.where((iota((128, D), 1) == iota((128, D), 0) + 96 * m) & (iota((128, D), 0) < 96), 1.0, 0.0)
            rows = rows + dot_plain(sv_all[m][:, :128], put.astype(BF))
        names = ("bq", "bv", "bo", "o1", "bd", "o2", "g1", "g2")
        for i, name in enumerate(names):
            state[name] = rows[1 + i : 2 + i, :]
        state["cu"] = [
            jnp.concatenate([sv_all[2 * j][0:1, :], sv_all[2 * j + 1][0:1, :]], axis=1).astype(F32) for j in range(4)
        ]

    def mix(k, out, bias, factor):
        for n in range(0, D, BLOCK):
            m = dot_plain(x_ref[...], wa[k, :, n : n + BLOCK])
            if bias is not None:
                m = m + state[bias][:, n : n + BLOCK]
            m = m.astype(BF)
            if factor is not None:
                m = m * jnp.asarray(factor, BF)
            out[:, n : n + BLOCK] = m

    def attend(low, high):
        left = iota((row_len, 128), 1) < HEAD_DIM
        for pair in range(low, high):
            cols = slice(128 * pair, 128 * pair + 128)
            qp, kp, vp = q_s[:, cols], k_s[:, cols], v_s[:, cols]
            found = []
            for keep in (left, jnp.logical_not(left)):
                s = dot_over_columns(jnp.where(keep, qp, jnp.zeros((), BF)), kp) + mask_s[...]
                e = jnp.exp(s - jnp.max(s, axis=1, keepdims=True))
                found.append(dot_plain(e.astype(BF), vp) * (1.0 / jnp.sum(e, axis=1, keepdims=True)))
            a_s[:, cols] = jnp.where(left, found[0], found[1]).astype(BF)

    def project():
        for n in range(0, D, BLOCK):
            b_s[:, n : n + BLOCK] = (
                x_ref[:, n : n + BLOCK].astype(F32)
                + dot_plain(a_s[...], wa[3, :, n : n + BLOCK])
                + state["bo"][:, n : n + BLOCK]
            )

        unit, _ = norm_parts(b_s[...])
        h = unit * state["g1"] + state["o1"]
        h_s[...] = h
        hl_s[...] = h.astype(BF)

    def up(j):
        for n in range(0, D, BLOCK):
            u = dot_plain(hl_s[...], wa[4 + j, :, n : n + BLOCK]) + state["cu"][j][:, n : n + BLOCK]
            g_s[j, :, n : n + BLOCK] = gelu_erf(u).astype(BF)

    def down(j):
        cols = slice(256 * j, 256 * j + 256)
        total = h_s[:, cols] + state["bd"][:, cols]
        for i in range(4):
            total = total + dot_plain(g_s[i], wd[j, D * i : D * i + D, :])
        b_s[:, cols] = total

    def finish():
        unit, _ = norm_parts(b_s[...])
        enc_ref[...] = (unit * state["g2"] + state["o2"]).astype(BF)

    def rows_attention():
        q_r = (dot_plain(x_low, wa[2]) + state["bq"]).astype(BF)
        state["q_r"] = q_r
        q_wide = (widen(q_r) * scaled).astype(BF)
        state["q_wide"] = q_wide
        s = jnp.where(open_keys, dot_over_columns(q_wide, k_s[...]), masked_score)
        e = jnp.exp(s - jnp.max(s, axis=1, keepdims=True))
        p = e * (1.0 / jnp.sum(e, axis=1, keepdims=True))
        state["p"] = p
        state["p_low"] = p.astype(BF)
        state["a_r"] = narrow(dot_plain(state["p_low"], v_s[...])).astype(BF)

    def rows_project():
        before = x_r_rows + dot_plain(state["a_r"], wa[3]) + state["bo"]
        unit, inverse = norm_parts(before)
        state["unit1"], state["inv1"] = unit, inverse
        state["h_r"] = unit * state["g1"] + state["o1"]
        state["hl_r"] = state["h_r"].astype(BF)
        state["u_r"], state["g_r"], state["f_r"] = [], [], []

    def rows_up(j):
        u = dot_plain(state["hl_r"], wa[4 + j]) + state["cu"][j]
        state["u_r"].append(u)
        state["g_r"].append(gelu_erf(u).astype(BF))

    def rows_down(j):
        f = jnp.zeros((ROW, 256), F32)
        for i in range(4):
            f = f + dot_plain(state["g_r"][i], wd[j, D * i : D * i + D, :])
        state["f_r"].append(f)

    def rows_finish():
        before = state["h_r"] + jnp.concatenate(state["f_r"], axis=1) + state["bd"]
        unit, inverse = norm_parts(before)
        state["unit2"], state["inv2"] = unit, inverse
        e = (unit * state["g2"] + state["o2"]).astype(BF)
        cls_own[...] = e[:SEGS, :]
        cls_all[z, plane] = e[:SEGS, :]

    def cls_z(r):
        peer = device(lax.rem(z + r, 4), x, y, c)
        return remote(cls_own, cls_all.at[z, plane], cz_s.at[r], cz_r.at[r], peer)

    def cls_plane(r):
        to = lax.rem(plane + r, 8)
        ref = cls_all.at[:, plane]
        return remote(ref, ref, cp_s.at[r], cp_r.at[r], (z * 2 + to // 4, lax.rem(to, 4)))

    xf, yf = x + (1 - c) * (1 - 2 * x), y + c * (1 - 2 * y)
    xg, yg = x + c * (1 - 2 * x), y + (1 - c) * (1 - 2 * y)
    to_f, to_g = device(z, xf, yf, c), device(z, xg, yg, c)
    wholes = ((src_q, fq_ref), (src_u, fu_ref), (src_a, fa_ref), (src_b, fb_ref))
    sliced = ((src_e, se_ref), (src_g, sg_ref), (src_l, sl_ref))

    def slot(ref):
        return ref.at[tower, c, x, y, zi]

    def whole_z(i):
        src, dst = wholes[i]
        for r in (1, 2, 3):
            go(remote(src, slot(dst), fz_s.at[i, r], fz_r.at[i, r], device(lax.rem(z + r, 4), x, y, c)))
        copy = pltpu.make_async_copy(src, slot(dst), fl.at[i])
        copy.start()
        copy.wait()

    def whole_f(i):
        src, dst = wholes[i]
        for r in (1, 2, 3):
            arrived(slot(dst), fz_s.at[i, r], fz_r.at[i, r])
        ref = dst.at[:, c, x, y]
        go(remote(ref, ref, ff_s.at[i], ff_r.at[i], to_f))
        go(remote(ref, ref, fg_s.at[i, 0], fg_r.at[i, 0], to_g))

    def whole_g(i):
        dst = wholes[i][1]
        ref = dst.at[:, c, xf, yf]
        arrived(ref, ff_s.at[i], ff_r.at[i])
        go(remote(ref, ref, fg_s.at[i, 1], fg_r.at[i, 1], to_g))

    def whole_c(i):
        dst = wholes[i][1]
        for j in (0, 1):
            arrived(dst.at[:, c, xg, yg], fg_s.at[i, j], fg_r.at[i, j])
        ref = dst.at[:, c]
        go(remote(ref, ref, fc_s.at[i], fc_r.at[i], to_core))

    def whole_end(i):
        arrived(wholes[i][1].at[:, c], fc_s.at[i], fc_r.at[i])

    def slice_1(i):
        src, dst = sliced[i]
        for r in range(1, 8):
            there = lax.rem(place + r, 8)
            go(remote(src.at[there], slot(dst), s1_s.at[i, r], s1_r.at[i, r], (there, other)))
        copy = pltpu.make_async_copy(src.at[place], slot(dst), fl.at[4 + i])
        copy.start()
        copy.wait()

    def slice_2(i):
        dst = sliced[i][1]
        for r in range(1, 8):
            arrived(slot(dst), s1_s.at[i, r], s1_r.at[i, r])
        ref = dst.at[:, c, :, y]
        go(remote(ref, ref, s2_s.at[i], s2_r.at[i], to_y))

    def slice_3(i):
        dst = sliced[i][1]
        arrived(dst.at[:, c, :, y], s2_s.at[i], s2_r.at[i])
        ref = dst.at[:, c]
        go(remote(ref, ref, s3_s.at[i], s3_r.at[i], to_core))

    def slice_end(i):
        arrived(sliced[i][1].at[:, c], s3_s.at[i], s3_r.at[i])

    row16 = iota((ROW, D), 0)

    def top(rows):
        return jnp.where(row16[:, : rows.shape[1]] < SEGS, rows, 0.0)

    def pack_early():
        src_q[...] = top(state["q_r"].astype(F32))[:8].astype(BF)
        hl_f32, a_f32, x_f32 = (top(m.astype(F32)) for m in (state["hl_r"], state["a_r"], x_low))
        three = hl_f32 + pltpu.roll(a_f32, 4, 0) + pltpu.roll(x_f32, 8, 0)
        z_rows = dot_plain(state["p_low"], x_ref[...])
        early = jnp.concatenate([three, z_rows], axis=0).astype(BF)
        early = dot_plain(early, sel_s[...]).astype(BF)
        for d in range(8):
            src_e[d] = early[:, 128 * d : 128 * d + 128]

    def pack_gelu():
        for d in range(8):
            packed = jnp.zeros((ROW, 128), F32)
            for b in range(3):
                first = 384 * d + 128 * b
                g = top(state["g_r"][first // D][:, first % D : first % D + 128].astype(F32))
                packed = packed + (pltpu.roll(g, 4 * b, 0) if b else g)
            src_g[d] = packed.astype(BF)

    after = {
        0: [lambda: small_vectors(), lambda: mix(0, k_s, None, None)],
        1: [lambda: mix(1, v_s, "bv", None)],
        2: [lambda: mix(2, q_s, "bq", scaled), rows_attention, lambda: attend(0, 2)],
        3: [rows_project, pack_early, lambda: slice_1(0), lambda: attend(2, 4)],
        4: [lambda: rows_up(0), lambda: attend(4, 6)],
        5: [lambda: rows_up(1), project, lambda: up(0)],
        6: [lambda: rows_up(2), lambda: up(1)],
        7: [lambda: rows_up(3), pack_gelu, lambda: up(2)],
        8: [lambda: rows_down(0), lambda: up(3), lambda: slice_2(0)],
        9: [lambda: rows_down(1), lambda: down(0)],
        10: [lambda: rows_down(2), rows_finish],
    }
    for i in range(kinds + 3):
        if i + WINDOW < kinds:
            stage0(i + WINDOW)
        if i < kinds:
            stage1(i)
        if 0 <= i - 1 < kinds:
            stage2(i - 1)
        if 0 <= i - 2 < kinds:
            stage3(i - 2)
        if 0 <= i - 3 < kinds:
            stage4(i - 3)
            for unit in after[i - 3]:
                unit()

    def drain():
        for copy in gone:
            copy.wait_send()

        @pl.when(inner == 1)
        def _():
            for k in range(kinds):
                for j, zz in ((1, z_a), (2, z_b)):
                    ref = full(k, zz, x, y if k in THIN else None, c)
                    remote(ref, ref, rel_s.at[k, j - 1], z_r.at[k, j], to_near).wait_send()

        @pl.when(inner == 0)
        def _():
            for k in THIN:
                for j, zz in ((1, z_a), (2, z_b)):
                    ref = full(k, zz, x, y, c)
                    remote(ref, ref, o_s.at[k, j - 1], o_r.at[k, j - 1], to_y).wait_send()

        for i in range(1, 8):
            sv_copy(i).wait_send()

    gone = list(state_sent)
    state_sent.clear()
    go(cls_z(1))
    go(cls_z(2))
    go(cls_z(3))
    whole_z(0)
    slice_1(1)
    down(1)
    for r in (1, 2, 3):
        cls_z(r).wait_recv()
    for r in range(1, 8):
        go(cls_plane(r))
    down(2)
    finish()

    keep_enc = pltpu.make_async_copy(enc_ref, enc_out, done.at[0])
    keep_enc.start()
    whole_f(0)
    slice_3(0)
    slice_2(1)
    for r in range(1, 8):
        cls_plane(r).wait_recv()
    for i in range(32):
        cls_f[SEGS * i : SEGS * i + SEGS, :] = cls_all[i // 8, i % 8].astype(F32)
    all_q, all_p = cls_f[:64, :].astype(BF), cls_f[64:, :].astype(BF)
    pair_scale = 2.0 * D ** (-0.5)
    logits = dot_over_columns(all_p, all_q) * pair_scale
    raised = jnp.exp(logits - jnp.max(logits, axis=0, keepdims=True))
    hit = jnp.where(iota((64, 64), 0) == pos_ref[...], 1.0, 0.0)
    d_logits = (raised / jnp.sum(raised, axis=0, keepdims=True) - hit).astype(BF)
    position = me * SEGS - tower * 64
    take = jnp.where((iota((ROW, 64), 1) == iota((ROW, 64), 0) + position) & (iota((ROW, 64), 0) < SEGS), 1.0, 0.0)
    take = take.astype(BF)
    d_q = dot_plain(dot_over_columns(take, d_logits).astype(BF), all_p)
    d_p = dot_plain(dot_plain(take, d_logits).astype(BF), all_q)
    d_cls = jnp.where(tower == 0, d_q, d_p) * pair_scale

    def total(rows):
        return jnp.sum(rows, axis=0, keepdims=True)

    vec_g2, vec_o2 = total(d_cls * state["unit2"]), total(d_cls)
    dz2 = norm_back(state["unit2"], state["inv2"], state["g2"], d_cls)
    df = dz2.astype(BF)
    dh = dz2
    du_rows = []
    for j in range(4):
        dg = jnp.zeros((ROW, D), F32)
        for i in range(3):
            dg = dg + dot_over_columns(df[:, 256 * i : 256 * i + 256], wd[i, D * j : D * j + D, :])
        du = (dg * gelu_slope(state["u_r"][j])).astype(BF)
        du_rows.append(du.astype(F32))
    packed = du_rows[0]
    for j in (1, 2, 3):
        packed = packed + pltpu.roll(du_rows[j], 4 * j, 0)
    src_u[...] = packed.astype(BF)
    whole_z(1)
    whole_g(0)
    for j in range(4):
        dh = dh + dot_over_columns(du_rows[j].astype(BF), wa[4 + j])
    vec_g1, vec_o1 = total(dh * state["unit1"]), total(dh)
    dz1 = norm_back(state["unit1"], state["inv1"], state["g1"], dh)
    db = dz1.astype(BF)
    slice_3(1)
    src_a[...] = (df.astype(F32) + pltpu.roll(db.astype(F32), 4, 0))[:8].astype(BF)
    whole_z(2)
    da = dot_over_columns(db, wa[3]).astype(BF)
    a_wide = widen(da).astype(BF)
    d_p_rows = dot_over_columns(a_wide, v_s[...])
    p = state["p"]
    ds = (p * (d_p_rows - jnp.sum(p * d_p_rows, axis=1, keepdims=True))).astype(BF)
    dq = narrow(dot_plain(ds, k_s[...]) * scaled).astype(BF)
    df_f, db_f, da_f, dq_f = (m.astype(F32) for m in (df, db, da, dq))
    src_b[...] = (dq_f + pltpu.roll(da_f, 4, 0))[:8].astype(BF)
    whole_z(3)
    y_rows = dot_plain(ds, x_ref[...]) * scaled
    weight_sum = jnp.sum(state["p_low"].astype(F32), axis=1, keepdims=True)
    vec_bv = total(weight_sum * a_wide.astype(F32))
    vectors = jnp.concatenate(
        [total(dq_f), vec_bv, total(db_f), vec_o1, total(df_f), vec_o2, vec_g1, vec_g2, jnp.zeros((8, D), F32)], axis=0
    )
    late = jnp.concatenate([y_rows, vectors], axis=0).astype(BF)
    late = dot_plain(late, sel_s[...]).astype(BF)
    for d in range(8):
        src_l[d] = late[:, 128 * d : 128 * d + 128]

    slice_1(2)
    whole_f(1)
    whole_c(0)
    t_k = dot_over_columns(state["q_wide"], wa[0]).astype(BF)
    t_v = dot_over_columns(a_wide, wa[1]).astype(BF)
    at_rows = dz1 + dot_over_columns(dq, wa[2])
    high = at_rows.astype(BF)
    rest = (at_rows - high.astype(F32)).astype(BF)
    left = jnp.concatenate([ds, state["p_low"], spot, spot], axis=0)
    right = jnp.concatenate([t_k, t_v, high, rest], axis=0)
    whole_f(2)
    drain()
    whole_f(3)
    whole_g(1)
    whole_g(2)
    for n in range(0, D, BLOCK):
        drow_ref[:, n : n + BLOCK] = dot_over_rows(left, right[:, n : n + BLOCK])
    keep_row = pltpu.make_async_copy(drow_ref, drow_out, done.at[1])
    keep_row.start()
    slice_2(2)
    whole_g(3)
    whole_c(1)
    whole_c(2)
    slice_3(2)
    whole_c(3)
    for i in range(4):
        whole_end(i)
    for i in range(3):
        slice_end(i)
    keep_enc.wait()
    keep_row.wait()

    for copy in state_sent:
        copy.wait_send()


def grads_kernel(
    fq_ref, fu_ref, fa_ref, fb_ref, se_ref, sg_ref, sl_ref, enc_ref, drow_ref,
    enc_out, drow_out, mix_out, proj_out, up_out, down_out, upb_ref, rowb_ref, gain_ref,
    mix_ref, proj_ref, up_ref, down_ref, put,
):
    place = lax.axis_index("dp")
    kind = iota((256, 128), 0) % ROW
    part = 96
    wide_row, wide_col = iota((D, 128), 0), iota((D, 128), 1)
    first_of = wide_row // 48 * 8 + wide_row % SEGS
    take_q = jnp.where(wide_col == first_of, 1.0, 0.0).astype(BF)
    take_a = jnp.where(wide_col == first_of + SEGS, 1.0, 0.0).astype(BF)
    kind8 = iota((128, 128), 0) % 8
    own_head = (iota((D, D), 0) % 48) // SEGS == iota((D, D), 1) // HEAD_DIM
    kind16, col16 = iota((256, ROW), 0) % ROW, iota((256, ROW), 1)
    again_row, again_col = iota((256, 128), 0), iota((256, 128), 1)
    again = jnp.where(again_col == again_row // ROW * 8 + again_row % SEGS, 1.0, 0.0).astype(BF)
    stores = []

    def store(src, dst):
        copy = pltpu.make_async_copy(src, dst, put.at[len(stores)])
        copy.start()
        stores.append(copy)

    store(enc_ref, enc_out)
    store(drow_ref, drow_out)

    def keep(rows, lo, hi):
        return jnp.where((kind >= lo) & (kind < hi), rows, jnp.zeros((), BF))

    pair = [se_ref[t, :, 0:8, :].reshape(128, 128) for t in range(2)]
    last = [se_ref[t, :, 8:16, :].reshape(128, 128) for t in range(2)]
    none = jnp.zeros((), BF)
    for t in range(2):
        four = dot_plain(again, pair[t]).astype(BF)
        for j in range(4):
            cols = slice(FF * t + D * j, FF * t + D * j + D)
            up_ref[:, cols] = dot_over_rows(keep(four, 4 * j, 4 * j + 4), fu_ref[t])[:part]
            store(up_ref.at[:, cols], up_out.at[:, cols])
    up_bias = jnp.zeros((ROW, 384), F32)
    for t in range(2):
        mine = fu_ref[t, :, pl.ds(pl.multiple_of(place % 2 * 384, 128), 384)]
        to_up = jnp.where((kind16 // 4 == place // 2) & (col16 == t), 1.0, 0.0).astype(BF)
        up_bias = up_bias + dot_over_rows(to_up, mine)
    upb_ref[...] = up_bias[:2]
    for t in range(2):
        fa = fa_ref[t]
        cols = slice(D * t, D * t + D)
        proj_ref[:, cols] = dot_over_rows(jnp.where(kind8 >= SEGS, pair[t], none), fa)[:part]
        store(proj_ref.at[:, cols], proj_out.at[:, cols])
        first = slice(3 * D * t, 3 * D * t + D)
        mix_ref[:, first] = dot_over_rows(jnp.where(kind8 < SEGS, last[t], none), fb_ref[t])[:part]
        store(mix_ref.at[:, first], mix_out.at[:, first])
        df = dot_plain(again, fa).astype(BF)
        g = sg_ref[t].reshape(256, 128)
        for b in range(3):
            at = slice(128 * b, 128 * b + 128)
            down_ref[at, cols] = dot_over_rows(keep(g, 4 * b, 4 * b + 4), df)
        store(down_ref.at[:, cols], down_out.at[:, cols])
    for t in range(2):
        a_wide = jnp.where(own_head, dot_plain(take_a, fb_ref[t]), 0.0).astype(BF)
        gv = dot_over_rows(se_ref[t, :, 16:64, :].reshape(D, 128), a_wide)
        cols = slice(3 * D * t + 2 * D, 3 * D * t + 3 * D)
        mix_ref[:, cols] = gv[:part]
        store(mix_ref.at[:, cols], mix_out.at[:, cols])
    biases = jnp.zeros((ROW, 128), F32)
    gains = jnp.zeros((ROW, 128), F32)
    for t in range(2):
        q_wide = jnp.where(own_head, dot_plain(take_q, fq_ref[t]), 0.0).astype(BF)
        gk = dot_over_rows(sl_ref[t, :, 0:48, :].reshape(D, 128), q_wide)
        cols = slice(3 * D * t + D, 3 * D * t + 2 * D)
        mix_ref[:, cols] = gk[:part]
        store(mix_ref.at[:, cols], mix_out.at[:, cols])
        vec = sl_ref[t, :, 48:64, :].reshape(256, 128)
        to_bias = jnp.where((kind16 < 6) & (col16 == kind16 + 6 * t), 1.0, 0.0).astype(BF)
        to_gain = jnp.where((kind16 >= 6) & (kind16 < 8) & (col16 == kind16 - 6 + 2 * t), 1.0, 0.0).astype(BF)
        biases = biases + dot_over_rows(to_bias, vec)
        gains = gains + dot_over_rows(to_gain, vec)
    rowb_ref[...] = biases[:12, :part]
    gain_ref[...] = gains[:4, :part]
    for copy in stores:
        copy.wait()


def fast_device(text_rows, text_segments, positives, w_mix, w_proj, w_up, w_down, b_up, b_rows, g_rows):
    sem = pltpu.SemaphoreType.DMA
    vm = pltpu.VMEM
    part = b_rows.shape[0]
    kinds = len(PIECES)
    fulls = lambda r: jax.ShapeDtypeStruct((2, 2, 2, 2, 2, r, D), BF)
    row_len = text_rows.shape[1]
    here, there = pl.BlockSpec(memory_space=vm), pl.BlockSpec(memory_space=pl.ANY)
    slices = lambda r: jax.ShapeDtypeStruct((2, 2, 2, 2, 2, r, 128), BF)
    encoded, d_rows, fq, fu, fa, fb, se, sg, sl = pl.pallas_call(
        main_kernel,
        out_shape=[
            jax.ShapeDtypeStruct((row_len, D), BF),
            jax.ShapeDtypeStruct((row_len, D), F32),
            fulls(8), fulls(ROW), fulls(8), fulls(8), slices(64), slices(ROW), slices(64),
        ],
        in_specs=[pl.BlockSpec(memory_space=pltpu.HBM)] * 10,
        out_specs=[there] * 2 + [here] * 7,
        scratch_shapes=[
            vm((row_len, D), BF), vm((1, row_len), jnp.int32), vm((1, 64), jnp.int32),
            vm((2, 384), BF), vm((12, 96), BF), vm((4, 96), BF), sem((6,)),
            vm((row_len, D), BF), vm((row_len, D), F32),
            vm((8, D, D), BF), vm((3, FF, 256), BF),
            vm((2, ROW, 384), F32), vm((2, ROW, 384), BF), vm((8, ROW, 384), BF),
            vm((row_len, D), BF), vm((row_len, D), BF), vm((row_len, D), BF), vm((row_len, D), BF),
            vm((row_len, row_len), F32), vm((row_len, D), F32), vm((row_len, D), F32), vm((row_len, D), BF),
            vm((4, row_len, D), BF), vm((D, 1024), BF),
            vm((SEGS, D), BF), vm((4, 8, SEGS, D), BF), vm((128, D), F32),
            vm((8, D), BF), vm((ROW, D), BF), vm((8, D), BF), vm((8, D), BF),
            vm((8, 64, 128), BF), vm((8, ROW, 128), BF), vm((8, 64, 128), BF),
            sem((kinds,)), sem((kinds,)), sem((kinds,)), sem((kinds, 3)), sem((kinds, 2)),
            sem((kinds, 4)), sem((kinds, 4)), sem((kinds, 4)), sem((kinds, 4)), sem((kinds,)), sem((kinds,)),
            sem((kinds, 2)), sem((kinds, 2)), sem((8,)), sem((8,)), sem((4,)), sem((4,)), sem((8,)), sem((8,)), sem((2,)),
            sem((7,)), sem((4, 4)), sem((4, 4)), sem((4,)), sem((4,)), sem((4, 2)), sem((4, 2)), sem((4,)), sem((4,)),
            sem((3, 8)), sem((3, 8)), sem((3,)), sem((3,)), sem((3,)), sem((3,)),
        ],
        compiler_params=pltpu.CompilerParams(collective_id=5, has_side_effects=True, vmem_limit_bytes=44 << 20),
        name="main_step",
    )(*(pltpu.with_memory_space_constraint(m, pltpu.HBM) for m in (text_rows[0], text_segments, positives[None, :], b_up.T, b_rows.T, g_rows.T, w_mix, w_proj, w_up, w_down)))
    shape = lambda r, n: jax.ShapeDtypeStruct((r, n), F32)
    grads = pl.pallas_call(
        grads_kernel,
        out_shape=[
            jax.ShapeDtypeStruct((row_len, D), BF), shape(row_len, D),
            shape(part, 6 * D), shape(part, 2 * D), shape(part, 2 * FF), shape(4 * part, 2 * D),
            shape(2, 4 * part), shape(12, part), shape(4, part),
        ],
        in_specs=[here] * 9,
        out_specs=[there] * 6 + [here] * 3,
        scratch_shapes=[
            vm((part, 6 * D), F32), vm((part, 2 * D), F32), vm((part, 2 * FF), F32), vm((4 * part, 2 * D), F32),
            sem((20,)),
        ],
        compiler_params=pltpu.CompilerParams(vmem_limit_bytes=24 << 20),
        name="weight_grads",
    )(
        fq.reshape(2, 128, D), fu.reshape(2, 256, D), fa.reshape(2, 128, D), fb.reshape(2, 128, D),
        se.reshape(2, 16, 64, 128), sg.reshape(2, 16, ROW, 128), sl.reshape(2, 16, 64, 128), encoded, d_rows,
    )
    encoded, d_rows, mix, proj, up, down, up_b, row_b, gain = grads
    return encoded[None], d_rows[None], mix, proj, up, down, up_b.T, row_b.T, gain.T


def solution(mesh):
    rows, cols = P(("dp", "outer"), None, None), P("dp", None)
    sizes = (mesh.shape["dp"], mesh.shape["outer"])
    return jax.shard_map(
        fast_device if sizes == (8, 4) else per_device,
        mesh=mesh,
        in_specs=(rows, P(("dp", "outer"), None), P(), cols, cols, cols, cols, cols, cols, cols),
        out_specs=(rows, rows, cols, cols, cols, cols, cols, cols, cols),
        check_vma=False,
    )
```

```python
import functools

import jax
import jax.numpy as jnp
from jax import lax
from jax.experimental import pallas as pl
from jax.experimental.pallas import tpu as pltpu
from jax.sharding import PartitionSpec as P

D = 768
HEADS = 12
HEAD_DIM = 64
FF = 3072
SEGS = 4
BF = jnp.bfloat16
F32 = jnp.float32
MESH = pl.DeviceIdType.MESH

masked_score = -1e30
layer_eps = 1e-05


def dot_plain(left, right):
    return jnp.dot(left, right, preferred_element_type=F32)


def dot_over_rows(left, right):
    return lax.dot_general(left, right, (((0,), (0,)), ((), ())), preferred_element_type=F32)


def dot_over_columns(left, right):
    return lax.dot_general(left, right, (((1,), (1,)), ((), ())), preferred_element_type=F32)


def gelu_exact(inputs):
    return jax.nn.gelu(inputs, approximate=False)


def norm_parts(inputs):
    center = inputs - jnp.mean(inputs, axis=-1, keepdims=True)
    inverse = lax.rsqrt(jnp.mean(center * center, axis=-1, keepdims=True) + layer_eps)
    return center * inverse, inverse


def norm_back(unit, inverse, gain, grad):
    scaled = gain * grad
    return inverse * (
        scaled
        - jnp.mean(scaled, axis=-1, keepdims=True)
        - unit * jnp.mean(scaled * unit, axis=-1, keepdims=True)
    )


def gather_weights(weights, widths, n_dp):
    tower = lax.axis_index("dp") * 2 // n_dp
    whole = [lax.all_gather(w, "dp", axis=0, tiled=True) for w in weights]
    return [lax.dynamic_slice_in_dim(w, tower * n, n, 1) for w, n in zip(whole, widths)]


def spread_kernel(n_outer, total, whole_ref, parts_ref, all_ref, sliced_ref, local, s_one, r_one, s_two, r_two):
    dp, outer = lax.axis_index("dp"), lax.axis_index("outer")
    me = dp * n_outer + outer
    barrier = pltpu.get_barrier_semaphore()

    def greet(i, carry):
        peer = lax.rem(me + i, total)
        pl.semaphore_signal(barrier, inc=1, device_id=(peer // n_outer, lax.rem(peer, n_outer)), device_id_type=MESH)
        return carry

    lax.fori_loop(1, total, greet, 0)
    pl.semaphore_wait(barrier, total - 1)

    def copies(i):
        peer = lax.rem(me + i, total)
        there = peer // n_outer
        device = (there, lax.rem(peer, n_outer))
        one = pltpu.make_async_remote_copy(
            src_ref=whole_ref, dst_ref=all_ref.at[me], send_sem=s_one.at[i], recv_sem=r_one.at[i],
            device_id=device, device_id_type=MESH,
        )
        if parts_ref is None:
            return (one,)
        two = pltpu.make_async_remote_copy(
            src_ref=parts_ref.at[there], dst_ref=sliced_ref.at[me], send_sem=s_two.at[i], recv_sem=r_two.at[i],
            device_id=device, device_id_type=MESH,
        )
        return (one, two)

    def send(i, carry):
        for copy in copies(i):
            copy.start()
        return carry

    lax.fori_loop(1, total, send, 0)
    own = [pltpu.make_async_copy(whole_ref, all_ref.at[me], local.at[0])]
    if parts_ref is not None:
        own.append(pltpu.make_async_copy(parts_ref.at[dp], sliced_ref.at[me], local.at[1]))
    for copy in own:
        copy.start()

    def settle(i, carry):
        for copy in copies(i):
            copy.wait()
        return carry

    lax.fori_loop(1, total, settle, 0)
    for copy in own:
        copy.wait()


def spread(whole, parts, n_dp, n_outer, identity):
    total = n_dp * n_outer
    sem = pltpu.SemaphoreType.DMA
    out_shape = [jax.ShapeDtypeStruct((total,) + whole.shape, whole.dtype)]
    operands = [whole]
    if parts is not None:
        out_shape.append(jax.ShapeDtypeStruct((total,) + parts.shape[1:], parts.dtype))
        operands.append(parts)
        kernel = functools.partial(spread_kernel, n_outer, total)
        scratch = [sem((2,))] + [sem((total,))] * 4
    else:
        def kernel(w, a, local, s, r):
            spread_kernel(n_outer, total, w, None, a, None, local, s, r, None, None)
        scratch = [sem((2,))] + [sem((total,))] * 2
    return pl.pallas_call(
        kernel,
        out_shape=out_shape,
        in_specs=[pl.BlockSpec(memory_space=pltpu.VMEM)] * len(operands),
        out_specs=[pl.BlockSpec(memory_space=pltpu.VMEM)] * len(out_shape),
        scratch_shapes=scratch,
        compiler_params=pltpu.CompilerParams(
            collective_id=identity, has_side_effects=True, vmem_limit_bytes=48 << 20
        ),
        name="spread%d" % identity,
    )(*operands)


def expand_heads(rows):
    head_of = jnp.arange(D, dtype=jnp.int32) // HEAD_DIM
    keep = head_of[None, :] == jnp.arange(HEADS, dtype=jnp.int32)[:, None]
    return jnp.where(keep[:, None, :], rows[None], 0).reshape(HEADS * rows.shape[0], D)


def per_device(text_rows, text_segments, positives, w_mix, w_proj, w_up, w_down, b_up, b_rows, g_rows):
    n_dp, n_outer = lax.axis_size("dp"), lax.axis_size("outer")
    total = n_dp * n_outer
    own_index = lax.axis_index(("dp", "outer"))
    tower = own_index * 2 // total
    rows_in, segments = text_rows[0], text_segments[0]
    row_len = rows_in.shape[0]
    widths = (3 * D, D, FF, D)
    wm, wp, wu, wd = gather_weights((w_mix, w_proj, w_up, w_down), widths, n_dp)
    part_f, part_d = b_up.shape[0], b_rows.shape[0]
    small = jnp.concatenate([b_up.reshape(part_f // part_d, part_d, 2).transpose(0, 2, 1).reshape(-1, part_d), b_rows.T, g_rows.T], axis=0)
    small = lax.all_gather(small, "dp", axis=0)
    split = 2 * (part_f // part_d)
    up_b = small[:, :split].reshape(n_dp, part_f // part_d, 2, part_d).transpose(2, 0, 1, 3).reshape(2, FF)
    row_b = small[:, split : split + 12].transpose(1, 0, 2).reshape(2, 6, D)
    gain_b = small[:, split + 12 :].transpose(1, 0, 2).reshape(2, 2, D)
    pick = lambda both_towers: jnp.where(tower == 0, both_towers[0], both_towers[1]).astype(F32)
    c_up, biases, gains = pick(up_b), pick(row_b), pick(gain_b)
    bq, bv, bo, o1, bd, o2 = (biases[i] for i in range(6))
    g1, g2 = gains[0], gains[1]

    scaled = HEAD_DIM ** (-0.5)
    mixed = (dot_plain(rows_in, wm) + jnp.concatenate([bq, jnp.zeros_like(bq), bv])).astype(BF)
    q, k, v = mixed[:, :D], mixed[:, D : 2 * D], mixed[:, 2 * D :]
    allowed = segments[:, None] == segments[None, :]
    heads = lambda m: m.reshape(row_len, HEADS, HEAD_DIM)
    scores = jnp.einsum("qhe,khe->hqk", heads(q), heads(k), preferred_element_type=F32) * scaled
    scores = jnp.where(allowed[None], scores, masked_score)
    top = jnp.max(scores, axis=-1, keepdims=True)
    raised = jnp.exp(scores - top)
    chances = (raised / jnp.sum(raised, axis=-1, keepdims=True)).astype(BF)
    attended = jnp.einsum("hqk,khe->qhe", chances, heads(v), preferred_element_type=F32).reshape(row_len, D).astype(BF)
    before_one = rows_in.astype(F32) + dot_plain(attended, wp) + bo
    unit_one, inv_one = norm_parts(before_one)
    h1 = unit_one * g1 + o1
    h1_low = h1.astype(BF)
    up_pre = dot_plain(h1_low, wu) + c_up
    gelu_low = gelu_exact(up_pre).astype(BF)
    before_two = h1 + dot_plain(gelu_low, wd) + bd
    unit_two, inv_two = norm_parts(before_two)
    encoded = unit_two * g2 + o2

    levels = jnp.arange(SEGS, dtype=jnp.int32)
    starts = jnp.sum((segments[None, :] < levels[:, None]).astype(jnp.int32), axis=1)
    at = lambda m: jnp.take(m, starts, axis=0)
    vectors = at(encoded).astype(BF)
    all_cls = spread(vectors, None, n_dp, n_outer, 2)[0].reshape(total * SEGS, D)
    texts = total * SEGS // 2
    all_q, all_p = all_cls[:texts], all_cls[texts:]
    pair_scale = 2.0 * D ** (-0.5)
    logits = dot_over_columns(all_q, all_p) * pair_scale
    raised_l = jnp.exp(logits - jnp.max(logits, axis=1, keepdims=True))
    hit = (positives[:, None] == jnp.arange(texts, dtype=jnp.int32)[None, :]).astype(F32)
    d_logits = (raised_l / jnp.sum(raised_l, axis=1, keepdims=True) - hit).astype(BF)
    position = own_index * SEGS - tower * texts
    d_q = dot_plain(lax.dynamic_slice_in_dim(d_logits, position, SEGS, 0), all_p)
    d_p = dot_over_rows(lax.dynamic_slice_in_dim(d_logits, position, SEGS, 1), all_q)
    d_cls = jnp.where(tower == 0, d_q, d_p) * pair_scale

    ut, it = at(unit_two), at(inv_two)
    dg2, do2 = jnp.sum(d_cls * ut, axis=0), jnp.sum(d_cls, axis=0)
    dz2 = norm_back(ut, it, g2, d_cls)
    df = dz2.astype(BF)
    dg = dot_over_columns(df, wd)
    u_r = at(up_pre)
    _, gelu_back = jax.vjp(gelu_exact, u_r)
    du = gelu_back(dg)[0].astype(BF)
    dh1 = dz2 + dot_over_columns(du, wu)
    uo, io = at(unit_one), at(inv_one)
    dg1, do1 = jnp.sum(dh1 * uo, axis=0), jnp.sum(dh1, axis=0)
    dz1 = norm_back(uo, io, g1, dh1)
    db = dz1.astype(BF)
    da = dot_over_columns(db, wp).astype(BF)
    q_r = at(q)
    q_wide, a_wide = expand_heads(q_r), expand_heads(da)
    own_segment = jnp.tile(levels, HEADS)
    open_keys = own_segment[:, None] == segments[None, :]
    s_r = jnp.where(open_keys, dot_over_columns(q_wide, k) * scaled, masked_score)
    e_r = jnp.exp(s_r - jnp.max(s_r, axis=-1, keepdims=True))
    p_r = e_r / jnp.sum(e_r, axis=-1, keepdims=True)
    pl_r = p_r.astype(BF)
    dp_r = dot_over_columns(a_wide, v)
    ds_r = (p_r * (dp_r - jnp.sum(p_r * dp_r, axis=-1, keepdims=True))).astype(BF)
    dq_wide = dot_plain(ds_r, k).reshape(HEADS, SEGS, HEADS, HEAD_DIM)
    dq = (jnp.einsum("hshe->she", dq_wide).reshape(SEGS, D) * scaled).astype(BF)
    y_r = (dot_plain(ds_r, rows_in) * scaled).astype(BF)
    z_r = dot_plain(pl_r, rows_in).astype(BF)
    weight_sum = jnp.sum(pl_r.astype(F32), axis=1, keepdims=True)
    dbv = jnp.sum(weight_sum * a_wide.astype(F32), axis=0)
    t_k = (dot_over_columns(q_wide, wm[:, D : 2 * D]) * scaled).astype(BF)
    t_v = dot_over_columns(a_wide, wm[:, 2 * D :]).astype(BF)
    d_rows = dot_over_rows(jnp.concatenate([ds_r, pl_r], axis=0), jnp.concatenate([t_k, t_v], axis=0))
    d_rows_at = dz1 + dot_over_columns(dq, wm[:, :D])
    spot = (starts[:, None] == jnp.arange(row_len, dtype=jnp.int32)[None, :])
    for s in range(SEGS):
        d_rows = d_rows + jnp.where(spot[s][:, None], d_rows_at[s][None, :], 0.0)

    ff_rows = SEGS * FF // D
    whole = jnp.concatenate(
        [df, db, dq, q_r, da, du.reshape(ff_rows, D), jnp.stack([dbv, do1, do2, dg1, dg2]).astype(BF), jnp.zeros((3, D), BF)],
        axis=0,
    )
    g_r, h_r, at_r, x_r = at(gelu_low), at(h1_low), at(attended), at(rows_in)
    by_part = lambda m: m.reshape(m.shape[0], n_dp, m.shape[1] // n_dp).transpose(1, 0, 2)
    parts = jnp.concatenate(
        [by_part(h_r), by_part(at_r), by_part(x_r), by_part(y_r), by_part(z_r),
         by_part(g_r).reshape(n_dp, -1, part_d)],
        axis=1,
    )
    all_w, all_s = spread(whole, parts, n_dp, n_outer, 3)
    half = total // 2
    tw = all_w.reshape(2, half, -1, D)
    ts = all_s.reshape(2, half, -1, part_d)
    rank = lambda m: m.reshape(half * SEGS, -1)
    grads = []
    outs = [[], [], [], []]
    vec_b, vec_g, vec_u = [], [], []
    mine = lax.axis_index("dp")
    for t in range(2):
        w, s = tw[t], ts[t]
        df_a, db_a, dq_a, q_a, da_a = (rank(w[:, 4 * i : 4 * i + 4]) for i in range(5))
        du_a = w[:, 20 : 20 + ff_rows].reshape(half * SEGS, FF)
        vec = jnp.sum(w[:, 20 + ff_rows : 25 + ff_rows].astype(F32), axis=0)
        h_a, at_a, x_a = (rank(s[:, 4 * i : 4 * i + 4]) for i in range(3))
        y_a = s[:, 12:60].reshape(half, HEADS, SEGS, part_d)
        z_a = s[:, 60:108].reshape(half, HEADS, SEGS, part_d)
        g_a = s[:, 108:].reshape(half * SEGS, part_f)
        by_head = lambda m: m.reshape(half, SEGS, HEADS, HEAD_DIM)
        gk = jnp.einsum("rhsa,rshe->ahe", y_a, by_head(q_a), preferred_element_type=F32).reshape(part_d, D)
        gv = jnp.einsum("rhsa,rshe->ahe", z_a, by_head(da_a), preferred_element_type=F32).reshape(part_d, D)
        outs[0] += [dot_over_rows(x_a, dq_a), gk, gv]
        outs[1].append(dot_over_rows(at_a, db_a))
        outs[2].append(dot_over_rows(h_a, du_a))
        outs[3].append(dot_over_rows(g_a, df_a))
        col = lambda m, n: lax.dynamic_slice_in_dim(m, mine * n, n, 0)
        summed = lambda m: jnp.sum(m.astype(F32), axis=0)
        vec_b += [col(m, part_d) for m in (summed(dq_a), vec[0], summed(db_a), vec[1], summed(df_a), vec[2])]
        vec_g += [col(m, part_d) for m in (vec[3], vec[4])]
        vec_u.append(col(summed(du_a), part_f))
    return (
        encoded.astype(BF)[None],
        d_rows[None],
        jnp.concatenate(outs[0], axis=1),
        jnp.concatenate(outs[1], axis=1),
        jnp.concatenate(outs[2], axis=1),
        jnp.concatenate(outs[3], axis=1),
        jnp.stack(vec_u, axis=1),
        jnp.stack(vec_b, axis=1),
        jnp.stack(vec_g, axis=1),
    )


PIECES = (
    [(0, D, D), (0, 2 * D, D), (0, 0, D), (1, 0, D)]
    + [(2, D * i, D) for i in range(4)]
    + [(3, 256 * i, 256) for i in range(3)]
)
WIDTHS = (3 * D, D, FF, D)
THIN = (2, 5, 8)
ROW = 16
BLOCK = 256


def iota(shape, dim):
    return lax.broadcasted_iota(jnp.int32, shape, dim)


def gelu_erf(u):
    return 0.5 * u * (1.0 + lax.erf(u * 0.7071067811865476))


def gelu_slope(u):
    return 0.5 * (1.0 + lax.erf(u * 0.7071067811865476)) + u * (0.3989422804014327 * jnp.exp(-0.5 * u * u))


def main_kernel(
    x_in, seg_in, pos_in, bu_in, br_in, gr_in, w_mix, w_proj, w_up, w_down,
    enc_out, drow_out, fq_ref, fu_ref, fa_ref, fb_ref, se_ref, sg_ref, sl_ref,
    x_ref, seg_ref, pos_ref, bu_ref, br_ref, gr_ref, first, enc_ref, drow_ref, wa, wd, sv_f, sv_ref, sv_all, q_s, k_s, v_s, a_s, mask_s, b_s, h_s, hl_s, g_s, sel_s,
    cls_own, cls_all, cls_f, src_q, src_u, src_a, src_b, src_e, src_g, src_l,
    ld, far_s, near_s, z_r, rel_s, x_s, x_r, y_s, y_r, c_s, c_r, o_s, o_r, sv_sem, sv_r, cz_s, cz_r, cp_s, cp_r, done,
    fl, fz_s, fz_r, ff_s, ff_r, fg_s, fg_r, fc_s, fc_r, s1_s, s1_r, s2_s, s2_r, s3_s, s3_r,
):
    sources = (w_mix, w_proj, w_up, w_down)
    place, other = lax.axis_index("dp"), lax.axis_index("outer")
    z, x = place // 2, place % 2
    y, c = other // 2, other % 2
    tower, zi = z // 2, z % 2
    me = place * 4 + other
    inner = zi * (1 - tower) + (1 - zi) * tower
    zn = z + 1 - 2 * zi
    z_a, z_b = 2 - tower, 3 - 3 * tower
    scaled = HEAD_DIM ** (-0.5)
    row_len = x_ref.shape[0]

    def device(zz, xx, yy, cc):
        return (zz * 2 + xx, yy * 2 + cc)

    plane = x * 4 + other
    to_near, to_far = device(zn, x, y, c), device(z_a, x, y, c)
    to_x, to_y, to_core = device(z, 1 - x, y, c), device(z, x, 1 - y, c), device(z, x, y, 1 - c)

    loads = []
    pairs = ((bu_in, bu_ref), (br_in, br_ref), (gr_in, gr_ref), (seg_in, seg_ref), (pos_in, pos_ref), (x_in, x_ref))
    for i, (src, dst) in enumerate(pairs):
        loads.append(pltpu.make_async_copy(src, dst, first.at[i]))
        loads[-1].start()
    barrier = pltpu.get_barrier_semaphore()

    greeted = [device(lax.rem(z + r, 4), x, y, c) for r in (1, 2, 3)]
    greeted += [device(lax.rem(z + r, 4), 1 - x, y, c) for r in (1, 2, 3)]
    for r in range(1, 8):
        to = lax.rem(plane + r, 8)
        greeted.append((z * 2 + to // 4, lax.rem(to, 4)))
    for peer in greeted:
        pl.semaphore_signal(barrier, inc=1, device_id=peer, device_id_type=MESH)
    pl.semaphore_wait(barrier, len(greeted))

    def remote(src, dst, s, r, peer):
        return pltpu.make_async_remote_copy(
            src_ref=src, dst_ref=dst, send_sem=s, recv_sem=r, device_id=peer, device_id_type=MESH
        )

    def arrived(ref, s, r):
        remote(ref, ref, s, r, to_x).wait_recv()

    state_sent = []

    def go(copy):
        copy.start()
        state_sent.append(copy)

    def dims(k):
        tensor, first, cols = PIECES[k]
        return tensor, sources[tensor].shape[0], first, cols

    def own(k, which, half_row, half_col):
        tensor, r, first, n = dims(k)
        row, rows = (0, r) if half_row is None else (half_row * (r // 2), r // 2)
        col, cols = which * WIDTHS[tensor] + first, n
        if half_col is not None:
            col, cols = col + half_col * (n // 2), n // 2
        return sources[tensor].at[
            pl.ds(pl.multiple_of(row, 16), rows), pl.ds(pl.multiple_of(col, 128), cols)
        ]

    def held(k):
        return wa.at[k] if k < 8 else wd.at[k - 8]

    def full(k, zz, xx, half_row, half_col):
        tensor, r, first, n = dims(k)
        row, rows = (zz * 2 + xx) * r, r
        if half_row is not None:
            row, rows = row + half_row * (r // 2), r // 2
        col, cols = (0, n) if half_col is None else (pl.multiple_of(half_col * (n // 2), 128), n // 2)
        return held(k).at[pl.ds(pl.multiple_of(row, 16), rows), pl.ds(col, cols)]

    planes = (z, zn, z_a, z_b)
    kinds = len(PIECES)
    local = []

    def stage0(k):
        go(remote(own(k, tower, y, c), full(k, z, x, y, c), near_s.at[k], z_r.at[k, 0], to_near))
        go(remote(own(k, 1 - tower, None, c), full(k, z, x, None, c), far_s.at[k], z_r.at[k, 2 - inner], to_far))
        go(remote(own(k, tower, None, c), full(k, z, x, None, c), x_s.at[k, 0], x_r.at[k, 0], to_x))
        copy = pltpu.make_async_copy(own(k, tower, None, c), full(k, z, x, None, c), ld.at[k])
        copy.start()
        local.append(copy)

    def stage1(k):
        ref = full(k, zn, x, y, c)
        arrived(ref, near_s.at[k], z_r.at[k, 0])
        go(remote(ref, ref, x_s.at[k, 1], x_r.at[k, 1], to_x))
        go(remote(ref, ref, y_s.at[k, 0], y_r.at[k, 0], to_y))
        for j, zz in ((1, z_a), (2, z_b)):
            whole, part = full(k, zz, x, None, c), full(k, zz, x, y, c)
            passed = part if k in THIN else whole

            @pl.when(inner == 1)
            def _():
                arrived(whole, near_s.at[k], z_r.at[k, j])
                remote(passed, passed, rel_s.at[k, j - 1], z_r.at[k, j], to_near).start()

            @pl.when(inner == 0)
            def _():
                arrived(passed, near_s.at[k], z_r.at[k, j])
                if k in THIN:
                    remote(part, part, o_s.at[k, j - 1], o_r.at[k, j - 1], to_y).start()

            go(remote(part, part, x_s.at[k, 1 + j], x_r.at[k, 1 + j], to_x))

    def stage2(k):
        arrived(full(k, z, 1 - x, None, c), x_s.at[k, 0], x_r.at[k, 0])
        for j in (1, 2, 3):
            ref = full(k, planes[j], 1 - x, y, c)
            arrived(ref, x_s.at[k, j], x_r.at[k, j])
            go(remote(ref, ref, y_s.at[k, j], y_r.at[k, j], to_y))

    def stage3(k):
        arrived(full(k, zn, x, 1 - y, c), y_s.at[k, 0], y_r.at[k, 0])
        for j in (1, 2, 3):
            arrived(full(k, planes[j], 1 - x, 1 - y, c), y_s.at[k, j], y_r.at[k, j])
        if k in THIN:

            @pl.when(inner == 0)
            def _():
                for j, zz in ((1, z_a), (2, z_b)):
                    arrived(full(k, zz, x, 1 - y, c), o_s.at[k, j - 1], o_r.at[k, j - 1])

        local[k].wait()
        n = dims(k)[3]
        ref = held(k).at[:, pl.ds(pl.multiple_of(c * (n // 2), 128), n // 2)]
        go(remote(ref, ref, c_s.at[k], c_r.at[k], to_core))

    def stage4(k):
        n = dims(k)[3]
        ref = held(k).at[:, pl.ds(pl.multiple_of((1 - c) * (n // 2), 128), n // 2)]
        arrived(ref, c_s.at[k], c_r.at[k])

    def sv_copy(i):
        there = lax.rem(place + i, 8)
        return remote(sv_ref.at[there // 4], sv_all.at[place], sv_sem.at[i], sv_r.at[i], (there, other))

    WINDOW = 2
    for k in range(WINDOW):
        stage0(k)
    for copy in loads:
        copy.wait()
    sv_f[...] = jnp.zeros_like(sv_f)
    for t in range(2):
        sv_f[t, 0:1, :] = bu_ref[...].astype(F32)[t : t + 1]
        sv_f[t, 1:7, 0:96] = br_ref[...].astype(F32)[6 * t : 6 * t + 6]
        sv_f[t, 7:9, 0:96] = gr_ref[...].astype(F32)[2 * t : 2 * t + 2]
    sv_ref[...] = sv_f[...].astype(BF)

    for i in range(1, 8):
        sv_copy(i).start()
    sv_all[place] = sv_ref[tower]

    sel_row, sel_col = iota((D, 1024), 0), iota((D, 1024), 1)
    lane = sel_col % 128
    sel_s[...] = jnp.where((sel_row == (sel_col // 128) * 96 + lane) & (lane < 96), 1.0, 0.0).astype(BF)
    segments = seg_ref[...]
    level = iota((ROW, row_len), 0)
    begin = jnp.sum(jnp.where(segments < level, 1.0, 0.0), axis=1, keepdims=True).astype(jnp.int32)
    spot = jnp.where((iota((ROW, row_len), 1) == begin) & (level < SEGS), 1.0, 0.0).astype(BF)
    belongs = jnp.where((segments == level) & (level < SEGS), 1.0, 0.0).astype(BF)
    mask_s[...] = (dot_over_rows(belongs, belongs) - 1.0) * -masked_score
    wide_row, wide_col = iota((48, D), 0), iota((48, D), 1)
    own_head = (wide_row // SEGS) == (wide_col // HEAD_DIM)
    repeat = jnp.where(iota((48, ROW), 0) % SEGS == iota((48, ROW), 1), 1.0, 0.0).astype(BF)
    open_keys = (iota((48, row_len), 0) % SEGS) == segments
    x_r_rows = dot_plain(spot, x_ref[...])
    x_low = x_r_rows.astype(BF)

    def widen(rows):
        return jnp.where(own_head, dot_plain(repeat, rows), 0.0)

    def narrow(wide):
        return dot_over_rows(repeat, jnp.where(own_head, wide, 0.0).astype(BF))

    state = {}

    def small_vectors():
        for i in range(1, 8):
            sv_copy(i).wait_recv()
        rows = jnp.zeros((ROW, D), F32)
        for m in range(8):
            put = jnp.where((iota((128, D), 1) == iota((128, D), 0) + 96 * m) & (iota((128, D), 0) < 96), 1.0, 0.0)
            rows = rows + dot_plain(sv_all[m][:, :128], put.astype(BF))
        names = ("bq", "bv", "bo", "o1", "bd", "o2", "g1", "g2")
        for i, name in enumerate(names):
            state[name] = rows[1 + i : 2 + i, :]
        state["cu"] = [
            jnp.concatenate([sv_all[2 * j][0:1, :], sv_all[2 * j + 1][0:1, :]], axis=1).astype(F32) for j in range(4)
        ]

    def mix(k, out, bias, factor):
        for n in range(0, D, BLOCK):
            m = dot_plain(x_ref[...], wa[k, :, n : n + BLOCK])
            if bias is not None:
                m = m + state[bias][:, n : n + BLOCK]
            m = m.astype(BF)
            if factor is not None:
                m = m * jnp.asarray(factor, BF)
            out[:, n : n + BLOCK] = m

    def attend(low, high):
        left = iota((row_len, 128), 1) < HEAD_DIM
        for pair in range(low, high):
            cols = slice(128 * pair, 128 * pair + 128)
            qp, kp, vp = q_s[:, cols], k_s[:, cols], v_s[:, cols]
            found = []
            for keep in (left, jnp.logical_not(left)):
                s = dot_over_columns(jnp.where(keep, qp, jnp.zeros((), BF)), kp) + mask_s[...]
                e = jnp.exp(s - jnp.max(s, axis=1, keepdims=True))
                found.append(dot_plain(e.astype(BF), vp) * (1.0 / jnp.sum(e, axis=1, keepdims=True)))
            a_s[:, cols] = jnp.where(left, found[0], found[1]).astype(BF)

    def project():
        for n in range(0, D, BLOCK):
            b_s[:, n : n + BLOCK] = (
                x_ref[:, n : n + BLOCK].astype(F32)
                + dot_plain(a_s[...], wa[3, :, n : n + BLOCK])
                + state["bo"][:, n : n + BLOCK]
            )

        unit, _ = norm_parts(b_s[...])
        h = unit * state["g1"] + state["o1"]
        h_s[...] = h
        hl_s[...] = h.astype(BF)

    def up(j):
        for n in range(0, D, BLOCK):
            u = dot_plain(hl_s[...], wa[4 + j, :, n : n + BLOCK]) + state["cu"][j][:, n : n + BLOCK]
            g_s[j, :, n : n + BLOCK] = gelu_erf(u).astype(BF)

    def down(j):
        cols = slice(256 * j, 256 * j + 256)
        total = h_s[:, cols] + state["bd"][:, cols]
        for i in range(4):
            total = total + dot_plain(g_s[i], wd[j, D * i : D * i + D, :])
        b_s[:, cols] = total

    def finish():
        unit, _ = norm_parts(b_s[...])
        enc_ref[...] = (unit * state["g2"] + state["o2"]).astype(BF)

    def rows_attention():
        q_r = (dot_plain(x_low, wa[2]) + state["bq"]).astype(BF)
        state["q_r"] = q_r
        q_wide = (widen(q_r) * scaled).astype(BF)
        state["q_wide"] = q_wide
        s = jnp.where(open_keys, dot_over_columns(q_wide, k_s[...]), masked_score)
        e = jnp.exp(s - jnp.max(s, axis=1, keepdims=True))
        p = e * (1.0 / jnp.sum(e, axis=1, keepdims=True))
        state["p"] = p
        state["p_low"] = p.astype(BF)
        state["a_r"] = narrow(dot_plain(state["p_low"], v_s[...])).astype(BF)

    def rows_project():
        before = x_r_rows + dot_plain(state["a_r"], wa[3]) + state["bo"]
        unit, inverse = norm_parts(before)
        state["unit1"], state["inv1"] = unit, inverse
        state["h_r"] = unit * state["g1"] + state["o1"]
        state["hl_r"] = state["h_r"].astype(BF)
        state["u_r"], state["g_r"], state["f_r"] = [], [], []

    def rows_up(j):
        u = dot_plain(state["hl_r"], wa[4 + j]) + state["cu"][j]
        state["u_r"].append(u)
        state["g_r"].append(gelu_erf(u).astype(BF))

    def rows_down(j):
        f = jnp.zeros((ROW, 256), F32)
        for i in range(4):
            f = f + dot_plain(state["g_r"][i], wd[j, D * i : D * i + D, :])
        state["f_r"].append(f)

    def rows_finish():
        before = state["h_r"] + jnp.concatenate(state["f_r"], axis=1) + state["bd"]
        unit, inverse = norm_parts(before)
        state["unit2"], state["inv2"] = unit, inverse
        e = (unit * state["g2"] + state["o2"]).astype(BF)
        cls_own[...] = e[:SEGS, :]
        cls_all[z, plane] = e[:SEGS, :]

    def cls_z(r):
        peer = device(lax.rem(z + r, 4), x, y, c)
        return remote(cls_own, cls_all.at[z, plane], cz_s.at[r], cz_r.at[r], peer)

    def cls_plane(r):
        to = lax.rem(plane + r, 8)
        ref = cls_all.at[:, plane]
        return remote(ref, ref, cp_s.at[r], cp_r.at[r], (z * 2 + to // 4, lax.rem(to, 4)))

    xf, yf = x + (1 - c) * (1 - 2 * x), y + c * (1 - 2 * y)
    xg, yg = x + c * (1 - 2 * x), y + (1 - c) * (1 - 2 * y)
    to_f, to_g = device(z, xf, yf, c), device(z, xg, yg, c)
    wholes = ((src_q, fq_ref), (src_u, fu_ref), (src_a, fa_ref), (src_b, fb_ref))
    sliced = ((src_e, se_ref), (src_g, sg_ref), (src_l, sl_ref))

    def slot(ref):
        return ref.at[tower, c, x, y, zi]

    def whole_z(i):
        src, dst = wholes[i]
        for r in (1, 2, 3):
            go(remote(src, slot(dst), fz_s.at[i, r], fz_r.at[i, r], device(lax.rem(z + r, 4), x, y, c)))
        copy = pltpu.make_async_copy(src, slot(dst), fl.at[i])
        copy.start()
        copy.wait()

    def whole_f(i):
        src, dst = wholes[i]
        for r in (1, 2, 3):
            arrived(slot(dst), fz_s.at[i, r], fz_r.at[i, r])
        ref = dst.at[:, c, x, y]
        go(remote(ref, ref, ff_s.at[i], ff_r.at[i], to_f))
        go(remote(ref, ref, fg_s.at[i, 0], fg_r.at[i, 0], to_g))

    def whole_g(i):
        dst = wholes[i][1]
        ref = dst.at[:, c, xf, yf]
        arrived(ref, ff_s.at[i], ff_r.at[i])
        go(remote(ref, ref, fg_s.at[i, 1], fg_r.at[i, 1], to_g))

    def whole_c(i):
        dst = wholes[i][1]
        for j in (0, 1):
            arrived(dst.at[:, c, xg, yg], fg_s.at[i, j], fg_r.at[i, j])
        ref = dst.at[:, c]
        go(remote(ref, ref, fc_s.at[i], fc_r.at[i], to_core))

    def whole_end(i):
        arrived(wholes[i][1].at[:, c], fc_s.at[i], fc_r.at[i])

    def slice_1(i):
        src, dst = sliced[i]
        for r in range(1, 8):
            there = lax.rem(place + r, 8)
            go(remote(src.at[there], slot(dst), s1_s.at[i, r], s1_r.at[i, r], (there, other)))
        copy = pltpu.make_async_copy(src.at[place], slot(dst), fl.at[4 + i])
        copy.start()
        copy.wait()

    def slice_2(i):
        dst = sliced[i][1]
        for r in range(1, 8):
            arrived(slot(dst), s1_s.at[i, r], s1_r.at[i, r])
        ref = dst.at[:, c, :, y]
        go(remote(ref, ref, s2_s.at[i], s2_r.at[i], to_y))

    def slice_3(i):
        dst = sliced[i][1]
        arrived(dst.at[:, c, :, y], s2_s.at[i], s2_r.at[i])
        ref = dst.at[:, c]
        go(remote(ref, ref, s3_s.at[i], s3_r.at[i], to_core))

    def slice_end(i):
        arrived(sliced[i][1].at[:, c], s3_s.at[i], s3_r.at[i])

    row16 = iota((ROW, D), 0)

    def top(rows):
        return jnp.where(row16[:, : rows.shape[1]] < SEGS, rows, 0.0)

    def pack_early():
        src_q[...] = top(state["q_r"].astype(F32))[:8].astype(BF)
        hl_f32, a_f32, x_f32 = (top(m.astype(F32)) for m in (state["hl_r"], state["a_r"], x_low))
        three = hl_f32 + pltpu.roll(a_f32, 4, 0) + pltpu.roll(x_f32, 8, 0)
        z_rows = dot_plain(state["p_low"], x_ref[...])
        early = jnp.concatenate([three, z_rows], axis=0).astype(BF)
        early = dot_plain(early, sel_s[...]).astype(BF)
        for d in range(8):
            src_e[d] = early[:, 128 * d : 128 * d + 128]

    def pack_gelu():
        for d in range(8):
            packed = jnp.zeros((ROW, 128), F32)
            for b in range(3):
                first = 384 * d + 128 * b
                g = top(state["g_r"][first // D][:, first % D : first % D + 128].astype(F32))
                packed = packed + (pltpu.roll(g, 4 * b, 0) if b else g)
            src_g[d] = packed.astype(BF)

    after = {
        0: [lambda: small_vectors(), lambda: mix(0, k_s, None, None)],
        1: [lambda: mix(1, v_s, "bv", None)],
        2: [lambda: mix(2, q_s, "bq", scaled), rows_attention, lambda: attend(0, 2)],
        3: [rows_project, pack_early, lambda: slice_1(0), lambda: attend(2, 4)],
        4: [lambda: rows_up(0), lambda: attend(4, 6)],
        5: [lambda: rows_up(1), project, lambda: up(0)],
        6: [lambda: rows_up(2), lambda: up(1)],
        7: [lambda: rows_up(3), pack_gelu, lambda: up(2)],
        8: [lambda: rows_down(0), lambda: up(3), lambda: slice_2(0)],
        9: [lambda: rows_down(1), lambda: down(0)],
        10: [lambda: rows_down(2), rows_finish],
    }
    for i in range(kinds + 3):
        if i + WINDOW < kinds:
            stage0(i + WINDOW)
        if i < kinds:
            stage1(i)
        if 0 <= i - 1 < kinds:
            stage2(i - 1)
        if 0 <= i - 2 < kinds:
            stage3(i - 2)
        if 0 <= i - 3 < kinds:
            stage4(i - 3)
            for unit in after[i - 3]:
                unit()

    def drain():
        for copy in gone:
            copy.wait_send()

        @pl.when(inner == 1)
        def _():
            for k in range(kinds):
                for j, zz in ((1, z_a), (2, z_b)):
                    ref = full(k, zz, x, y if k in THIN else None, c)
                    remote(ref, ref, rel_s.at[k, j - 1], z_r.at[k, j], to_near).wait_send()

        @pl.when(inner == 0)
        def _():
            for k in THIN:
                for j, zz in ((1, z_a), (2, z_b)):
                    ref = full(k, zz, x, y, c)
                    remote(ref, ref, o_s.at[k, j - 1], o_r.at[k, j - 1], to_y).wait_send()

        for i in range(1, 8):
            sv_copy(i).wait_send()

    gone = list(state_sent)
    state_sent.clear()
    go(cls_z(1))
    go(cls_z(2))
    go(cls_z(3))
    whole_z(0)
    slice_1(1)
    down(1)
    for r in (1, 2, 3):
        cls_z(r).wait_recv()
    for r in range(1, 8):
        go(cls_plane(r))
    down(2)
    finish()

    keep_enc = pltpu.make_async_copy(enc_ref, enc_out, done.at[0])
    keep_enc.start()
    whole_f(0)
    slice_3(0)
    slice_2(1)
    for r in range(1, 8):
        cls_plane(r).wait_recv()
    for i in range(32):
        cls_f[SEGS * i : SEGS * i + SEGS, :] = cls_all[i // 8, i % 8].astype(F32)
    all_q, all_p = cls_f[:64, :].astype(BF), cls_f[64:, :].astype(BF)
    pair_scale = 2.0 * D ** (-0.5)
    logits = dot_over_columns(all_p, all_q) * pair_scale
    raised = jnp.exp(logits - jnp.max(logits, axis=0, keepdims=True))
    hit = jnp.where(iota((64, 64), 0) == pos_ref[...], 1.0, 0.0)
    d_logits = (raised / jnp.sum(raised, axis=0, keepdims=True) - hit).astype(BF)
    position = me * SEGS - tower * 64
    take = jnp.where((iota((ROW, 64), 1) == iota((ROW, 64), 0) + position) & (iota((ROW, 64), 0) < SEGS), 1.0, 0.0)
    take = take.astype(BF)
    d_q = dot_plain(dot_over_columns(take, d_logits).astype(BF), all_p)
    d_p = dot_plain(dot_plain(take, d_logits).astype(BF), all_q)
    d_cls = jnp.where(tower == 0, d_q, d_p) * pair_scale

    def total(rows):
        return jnp.sum(rows, axis=0, keepdims=True)

    vec_g2, vec_o2 = total(d_cls * state["unit2"]), total(d_cls)
    dz2 = norm_back(state["unit2"], state["inv2"], state["g2"], d_cls)
    df = dz2.astype(BF)
    dh = dz2
    du_rows = []
    for j in range(4):
        dg = jnp.zeros((ROW, D), F32)
        for i in range(3):
            dg = dg + dot_over_columns(df[:, 256 * i : 256 * i + 256], wd[i, D * j : D * j + D, :])
        du = (dg * gelu_slope(state["u_r"][j])).astype(BF)
        du_rows.append(du.astype(F32))
    packed = du_rows[0]
    for j in (1, 2, 3):
        packed = packed + pltpu.roll(du_rows[j], 4 * j, 0)
    src_u[...] = packed.astype(BF)
    whole_z(1)
    whole_g(0)
    for j in range(4):
        dh = dh + dot_over_columns(du_rows[j].astype(BF), wa[4 + j])
    vec_g1, vec_o1 = total(dh * state["unit1"]), total(dh)
    dz1 = norm_back(state["unit1"], state["inv1"], state["g1"], dh)
    db = dz1.astype(BF)
    slice_3(1)
    src_a[...] = (df.astype(F32) + pltpu.roll(db.astype(F32), 4, 0))[:8].astype(BF)
    whole_z(2)
    da = dot_over_columns(db, wa[3]).astype(BF)
    a_wide = widen(da).astype(BF)
    d_p_rows = dot_over_columns(a_wide, v_s[...])
    p = state["p"]
    ds = (p * (d_p_rows - jnp.sum(p * d_p_rows, axis=1, keepdims=True))).astype(BF)
    dq = narrow(dot_plain(ds, k_s[...]) * scaled).astype(BF)
    df_f, db_f, da_f, dq_f = (m.astype(F32) for m in (df, db, da, dq))
    src_b[...] = (dq_f + pltpu.roll(da_f, 4, 0))[:8].astype(BF)
    whole_z(3)
    y_rows = dot_plain(ds, x_ref[...]) * scaled
    weight_sum = jnp.sum(state["p_low"].astype(F32), axis=1, keepdims=True)
    vec_bv = total(weight_sum * a_wide.astype(F32))
    vectors = jnp.concatenate(
        [total(dq_f), vec_bv, total(db_f), vec_o1, total(df_f), vec_o2, vec_g1, vec_g2, jnp.zeros((8, D), F32)], axis=0
    )
    late = jnp.concatenate([y_rows, vectors], axis=0).astype(BF)
    late = dot_plain(late, sel_s[...]).astype(BF)
    for d in range(8):
        src_l[d] = late[:, 128 * d : 128 * d + 128]

    slice_1(2)
    whole_f(1)
    whole_c(0)
    t_k = dot_over_columns(state["q_wide"], wa[0]).astype(BF)
    t_v = dot_over_columns(a_wide, wa[1]).astype(BF)
    at_rows = dz1 + dot_over_columns(dq, wa[2])
    high = at_rows.astype(BF)
    rest = (at_rows - high.astype(F32)).astype(BF)
    left = jnp.concatenate([ds, state["p_low"], spot, spot], axis=0)
    right = jnp.concatenate([t_k, t_v, high, rest], axis=0)
    whole_f(2)
    drain()
    whole_f(3)
    whole_g(1)
    whole_g(2)
    for n in range(0, D, BLOCK):
        drow_ref[:, n : n + BLOCK] = dot_over_rows(left, right[:, n : n + BLOCK])
    keep_row = pltpu.make_async_copy(drow_ref, drow_out, done.at[1])
    keep_row.start()
    slice_2(2)
    whole_g(3)
    whole_c(1)
    whole_c(2)
    slice_3(2)
    whole_c(3)
    for i in range(4):
        whole_end(i)
    for i in range(3):
        slice_end(i)
    keep_enc.wait()
    keep_row.wait()

    for copy in state_sent:
        copy.wait_send()


def grads_kernel(
    fq_ref, fu_ref, fa_ref, fb_ref, se_ref, sg_ref, sl_ref, enc_ref, drow_ref,
    enc_out, drow_out, mix_out, proj_out, up_out, down_out, upb_ref, rowb_ref, gain_ref,
    mix_ref, proj_ref, up_ref, down_ref, put,
):
    place = lax.axis_index("dp")
    kind = iota((256, 128), 0) % ROW
    part = 96
    wide_row, wide_col = iota((D, 128), 0), iota((D, 128), 1)
    first_of = wide_row // 48 * 8 + wide_row % SEGS
    take_q = jnp.where(wide_col == first_of, 1.0, 0.0).astype(BF)
    take_a = jnp.where(wide_col == first_of + SEGS, 1.0, 0.0).astype(BF)
    kind8 = iota((128, 128), 0) % 8
    own_head = (iota((D, D), 0) % 48) // SEGS == iota((D, D), 1) // HEAD_DIM
    kind16, col16 = iota((256, ROW), 0) % ROW, iota((256, ROW), 1)
    again_row, again_col = iota((256, 128), 0), iota((256, 128), 1)
    again = jnp.where(again_col == again_row // ROW * 8 + again_row % SEGS, 1.0, 0.0).astype(BF)
    stores = []

    def store(src, dst):
        copy = pltpu.make_async_copy(src, dst, put.at[len(stores)])
        copy.start()
        stores.append(copy)

    store(enc_ref, enc_out)
    store(drow_ref, drow_out)

    def keep(rows, lo, hi):
        return jnp.where((kind >= lo) & (kind < hi), rows, jnp.zeros((), BF))

    pair = [se_ref[t, :, 0:8, :].reshape(128, 128) for t in range(2)]
    last = [se_ref[t, :, 8:16, :].reshape(128, 128) for t in range(2)]
    none = jnp.zeros((), BF)
    for t in range(2):
        four = dot_plain(again, pair[t]).astype(BF)
        for j in range(4):
            cols = slice(FF * t + D * j, FF * t + D * j + D)
            up_ref[:, cols] = dot_over_rows(keep(four, 4 * j, 4 * j + 4), fu_ref[t])[:part]
            store(up_ref.at[:, cols], up_out.at[:, cols])
    up_bias = jnp.zeros((ROW, 384), F32)
    for t in range(2):
        mine = fu_ref[t, :, pl.ds(pl.multiple_of(place % 2 * 384, 128), 384)]
        to_up = jnp.where((kind16 // 4 == place // 2) & (col16 == t), 1.0, 0.0).astype(BF)
        up_bias = up_bias + dot_over_rows(to_up, mine)
    upb_ref[...] = up_bias[:2]
    for t in range(2):
        fa = fa_ref[t]
        cols = slice(D * t, D * t + D)
        proj_ref[:, cols] = dot_over_rows(jnp.where(kind8 >= SEGS, pair[t], none), fa)[:part]
        store(proj_ref.at[:, cols], proj_out.at[:, cols])
        first = slice(3 * D * t, 3 * D * t + D)
        mix_ref[:, first] = dot_over_rows(jnp.where(kind8 < SEGS, last[t], none), fb_ref[t])[:part]
        store(mix_ref.at[:, first], mix_out.at[:, first])
        df = dot_plain(again, fa).astype(BF)
        g = sg_ref[t].reshape(256, 128)
        for b in range(3):
            at = slice(128 * b, 128 * b + 128)
            down_ref[at, cols] = dot_over_rows(keep(g, 4 * b, 4 * b + 4), df)
        store(down_ref.at[:, cols], down_out.at[:, cols])
    for t in range(2):
        a_wide = jnp.where(own_head, dot_plain(take_a, fb_ref[t]), 0.0).astype(BF)
        gv = dot_over_rows(se_ref[t, :, 16:64, :].reshape(D, 128), a_wide)
        cols = slice(3 * D * t + 2 * D, 3 * D * t + 3 * D)
        mix_ref[:, cols] = gv[:part]
        store(mix_ref.at[:, cols], mix_out.at[:, cols])
    biases = jnp.zeros((ROW, 128), F32)
    gains = jnp.zeros((ROW, 128), F32)
    for t in range(2):
        q_wide = jnp.where(own_head, dot_plain(take_q, fq_ref[t]), 0.0).astype(BF)
        gk = dot_over_rows(sl_ref[t, :, 0:48, :].reshape(D, 128), q_wide)
        cols = slice(3 * D * t + D, 3 * D * t + 2 * D)
        mix_ref[:, cols] = gk[:part]
        store(mix_ref.at[:, cols], mix_out.at[:, cols])
        vec = sl_ref[t, :, 48:64, :].reshape(256, 128)
        to_bias = jnp.where((kind16 < 6) & (col16 == kind16 + 6 * t), 1.0, 0.0).astype(BF)
        to_gain = jnp.where((kind16 >= 6) & (kind16 < 8) & (col16 == kind16 - 6 + 2 * t), 1.0, 0.0).astype(BF)
        biases = biases + dot_over_rows(to_bias, vec)
        gains = gains + dot_over_rows(to_gain, vec)
    rowb_ref[...] = biases[:12, :part]
    gain_ref[...] = gains[:4, :part]
    for copy in stores:
        copy.wait()


def fast_device(text_rows, text_segments, positives, w_mix, w_proj, w_up, w_down, b_up, b_rows, g_rows):
    sem = pltpu.SemaphoreType.DMA
    vm = pltpu.VMEM
    part = b_rows.shape[0]
    kinds = len(PIECES)
    fulls = lambda r: jax.ShapeDtypeStruct((2, 2, 2, 2, 2, r, D), BF)
    row_len = text_rows.shape[1]
    here, there = pl.BlockSpec(memory_space=vm), pl.BlockSpec(memory_space=pl.ANY)
    slices = lambda r: jax.ShapeDtypeStruct((2, 2, 2, 2, 2, r, 128), BF)
    encoded, d_rows, fq, fu, fa, fb, se, sg, sl = pl.pallas_call(
        main_kernel,
        out_shape=[
            jax.ShapeDtypeStruct((row_len, D), BF),
            jax.ShapeDtypeStruct((row_len, D), F32),
            fulls(8), fulls(ROW), fulls(8), fulls(8), slices(64), slices(ROW), slices(64),
        ],
        in_specs=[pl.BlockSpec(memory_space=pltpu.HBM)] * 10,
        out_specs=[there] * 2 + [here] * 7,
        scratch_shapes=[
            vm((row_len, D), BF), vm((1, row_len), jnp.int32), vm((1, 64), jnp.int32),
            vm((2, 384), BF), vm((12, 96), BF), vm((4, 96), BF), sem((6,)),
            vm((row_len, D), BF), vm((row_len, D), F32),
            vm((8, D, D), BF), vm((3, FF, 256), BF),
            vm((2, ROW, 384), F32), vm((2, ROW, 384), BF), vm((8, ROW, 384), BF),
            vm((row_len, D), BF), vm((row_len, D), BF), vm((row_len, D), BF), vm((row_len, D), BF),
            vm((row_len, row_len), F32), vm((row_len, D), F32), vm((row_len, D), F32), vm((row_len, D), BF),
            vm((4, row_len, D), BF), vm((D, 1024), BF),
            vm((SEGS, D), BF), vm((4, 8, SEGS, D), BF), vm((128, D), F32),
            vm((8, D), BF), vm((ROW, D), BF), vm((8, D), BF), vm((8, D), BF),
            vm((8, 64, 128), BF), vm((8, ROW, 128), BF), vm((8, 64, 128), BF),
            sem((kinds,)), sem((kinds,)), sem((kinds,)), sem((kinds, 3)), sem((kinds, 2)),
            sem((kinds, 4)), sem((kinds, 4)), sem((kinds, 4)), sem((kinds, 4)), sem((kinds,)), sem((kinds,)),
            sem((kinds, 2)), sem((kinds, 2)), sem((8,)), sem((8,)), sem((4,)), sem((4,)), sem((8,)), sem((8,)), sem((2,)),
            sem((7,)), sem((4, 4)), sem((4, 4)), sem((4,)), sem((4,)), sem((4, 2)), sem((4, 2)), sem((4,)), sem((4,)),
            sem((3, 8)), sem((3, 8)), sem((3,)), sem((3,)), sem((3,)), sem((3,)),
        ],
        compiler_params=pltpu.CompilerParams(collective_id=5, has_side_effects=True, vmem_limit_bytes=44 << 20),
        name="main_step",
    )(*(pltpu.with_memory_space_constraint(m, pltpu.HBM) for m in (text_rows[0], text_segments, positives[None, :], b_up.T, b_rows.T, g_rows.T, w_mix, w_proj, w_up, w_down)))
    shape = lambda r, n: jax.ShapeDtypeStruct((r, n), F32)
    grads = pl.pallas_call(
        grads_kernel,
        out_shape=[
            jax.ShapeDtypeStruct((row_len, D), BF), shape(row_len, D),
            shape(part, 6 * D), shape(part, 2 * D), shape(part, 2 * FF), shape(4 * part, 2 * D),
            shape(2, 4 * part), shape(12, part), shape(4, part),
        ],
        in_specs=[here] * 9,
        out_specs=[there] * 6 + [here] * 3,
        scratch_shapes=[
            vm((part, 6 * D), F32), vm((part, 2 * D), F32), vm((part, 2 * FF), F32), vm((4 * part, 2 * D), F32),
            sem((20,)),
        ],
        compiler_params=pltpu.CompilerParams(vmem_limit_bytes=24 << 20),
        name="weight_grads",
    )(
        fq.reshape(2, 128, D), fu.reshape(2, 256, D), fa.reshape(2, 128, D), fb.reshape(2, 128, D),
        se.reshape(2, 16, 64, 128), sg.reshape(2, 16, ROW, 128), sl.reshape(2, 16, 64, 128), encoded, d_rows,
    )
    encoded, d_rows, mix, proj, up, down, up_b, row_b, gain = grads
    return encoded[None], d_rows[None], mix, proj, up, down, up_b.T, row_b.T, gain.T


def solution(mesh):
    rows, cols = P(("dp", "outer"), None, None), P("dp", None)
    sizes = (mesh.shape["dp"], mesh.shape["outer"])
    return jax.shard_map(
        fast_device if sizes == (8, 4) else per_device,
        mesh=mesh,
        in_specs=(rows, P(("dp", "outer"), None), P(), cols, cols, cols, cols, cols, cols, cols),
        out_specs=(rows, rows, cols, cols, cols, cols, cols, cols, cols),
        check_vma=False,
    )
```
